32 devices in a mesh: groups: 2 (over y), ctx: 4 (over z), heads: 2 (over x), dp: 2 (over core).
Axes of the slice: x: 2, y: 2, z: 4, core: 2. Of those that a mesh axis runs over, the one named last changes fastest.
Arguments:
- tokens: bfloat16 [4, 2048, 1024], P(('groups', 'dp'), 'ctx', 'heads'), parts along dimension 0, may hold values from -12 to 12
- w_qkv: bfloat16 [3, 1024, 1024], P(None, None, 'heads'), may hold values from -0.375 to 0.375
- w_out: bfloat16 [1024, 1024], P('heads'), may hold values from -0.1875 to 0.1875
- ln_gain: float32 [1024], P('heads'), may hold values from 0.5 to 1.5
- ln_bias: float32 [1024], P('heads'), may hold values from -3 to 3
- random_blocks: int32 [4, 16, 3], P(('groups', 'dp'), 'ctx'), parts along dimension 0, may hold values from 0 to 15, as said below
- summary_pos: int32 [4, 16], P(('groups', 'dp')), parts along dimension 0, may hold values from 0 to 2047, as said below
- summary_blocks: int32 [4, 16, 8], P(('groups', 'dp')), parts along dimension 0, may hold values from 0 to 15, as said below
- pair_lengths: int32 [4, 4], P(('groups', 'dp')), parts along dimension 0, may hold values from 1 to 1536, 2048 in all within a row
Outputs:
- normed: bfloat16 [4, 2048, 1024], P(('groups', 'dp'), 'ctx', 'heads'), parts along dimension 0
The draws below stay inside these ranges and needn't reach their ends.
There are 2 independent parts, one for each index of `groups`. The reference program is written for one: setup_inputs(seed, part) draws one part's arguments, and reference() takes and returns one part's arrays. A program takes and returns all parts, laid end to end along the dimension named above; an argument that names none is the same for every part. Nothing has to cross between parts.
Inputs may be any that keep to these rules, and one draw needn't show every extreme that they name: `random_blocks`: the 4 x 3 entries of one device's range name at most 3 blocks of any one device's range of 4 blocks, repeats counted; in every draw some range is named exactly 3 times from every device's range. `summary_pos`: each range of 512 positions of a sequence holds exactly 4 of them; they are distinct and increasing. `summary_blocks`: the first entry of each list is the block holding that row's summary position; entries may repeat.
All inputs are finite; a program needn't handle non-finite values.
Results may differ from the reference program's by a relative error of at most 0.012.
The reference program's roundings to bfloat16 on the way count: a program that leaves them out, or rounds other values in their place, can miss the bound.
Values may be sent and summed in bfloat16 or wider, within the bound.
A program may use at most 64 MiB of HBM per device.

```python
import math
import jax
import jax.numpy as jnp
import numpy as np
from jax import lax

D = 1024
HEADS = 16
HEAD = 64
BLOCK = 128
RAND = 3
LISTED = 8
PAIRS = 4
TOK_DEV = 512
SUMM_DEV = 4
BLOCKS_DEV = 4
SEQ_LEN = 2048
NBLOCKS = 16
SEQS = 2
CAP = 3
SUMMARIES = 16
N_CTX = 4
N_HEADS = 2


def summary_positions(key):
    base = jax.random.fold_in(key, 7001)

    def pick_one(flat_index):
        chosen = jax.random.permutation(jax.random.fold_in(base, flat_index), TOK_DEV)[:SUMM_DEV]
        return jnp.sort(chosen.astype(jnp.int32))
    picked = jax.vmap(pick_one)(jnp.arange(SEQS * N_CTX)).reshape(SEQS, N_CTX, SUMM_DEV)
    offsets = (jnp.arange(N_CTX, dtype=jnp.int32) * TOK_DEV)[None, :, None]
    return (picked + offsets).reshape(SEQS, SUMMARIES).astype(jnp.int32)


def draw_summary_pos(key, part):
    return summary_positions(key)


def draw_summary_blocks(key, part):
    positions = summary_positions(key)
    own_block = positions // BLOCK
    others = jax.random.randint(jax.random.fold_in(key, 7002), (SEQS, SUMMARIES, LISTED - 1), 0, NBLOCKS)
    return jnp.concatenate([own_block[:, :, None], others.astype(jnp.int32)], axis=2).astype(jnp.int32)


def draw_random_blocks(key, part):
    pick_count = BLOCKS_DEV * RAND
    base = jax.random.fold_in(key, 7003)
    hottest = jax.random.randint(jax.random.fold_in(base, 1), (SEQS,), 0, N_CTX).astype(jnp.int32)

    def one_range(seq_index, ctx_index):
        range_key = jax.random.fold_in(jax.random.fold_in(base, seq_index + 2), ctx_index)
        others = jax.random.permutation(jax.random.fold_in(range_key, 1), CAP * (N_CTX - 1))[:pick_count - CAP] // CAP
        others = others.astype(jnp.int32)
        others = others + (others >= hottest[seq_index]).astype(jnp.int32)
        owners = jnp.concatenate([jnp.zeros((CAP,), jnp.int32) + hottest[seq_index], others])
        owners = jax.random.permutation(jax.random.fold_in(range_key, 2), owners)
        within = jax.random.randint(jax.random.fold_in(range_key, 3), (pick_count,), 0, BLOCKS_DEV).astype(jnp.int32)
        return (owners * BLOCKS_DEV + within).reshape(BLOCKS_DEV, RAND)
    grid = jax.vmap(lambda seq_index: jax.vmap(lambda ctx_index: one_range(seq_index, ctx_index))(jnp.arange(N_CTX)))(jnp.arange(SEQS))
    return grid.reshape(SEQS, NBLOCKS, RAND).astype(jnp.int32)


def draw_tokens(key, part):
    base = jax.random.fold_in(key, 7004)
    values = jnp.clip(jax.random.normal(jax.random.fold_in(base, 7), (SEQS, SEQ_LEN, D), jnp.float32), -6.0, 6.0)
    return values.astype(jnp.bfloat16)


def block_scale(stream_key, shape, shards, smallest, largest):
    loudness = 1.0
    for dim, shards_of in shards:
        draws = jax.random.uniform(jax.random.fold_in(jax.random.fold_in(stream_key, 6), dim), (shards_of,), jnp.float32, smallest / len(shards), largest / len(shards))
        loudness = loudness * jnp.repeat(jnp.exp(draws), shape[dim] // shards_of).reshape((-1,) + (1,) * (len(shape) - 1 - dim))
    return loudness


def split_up(amount, total, bound, slope):
    portions = [(1 << 20) // math.isqrt(standing ** slope) + 1 for standing in range(2, amount + 1)]
    rest, counts = total - bound - (amount - 1), [1] * (amount - 1)
    while rest > 0:
        free = [i for i in range(amount - 1) if counts[i] < bound]
        mass, budget = sum([portions[i] for i in free]), rest
        for i in free:
            addition = min(bound - counts[i], max(1, budget * portions[i] // mass), rest)
            counts[i] = counts[i] + addition
            rest = rest - addition
    return np.array([bound] + counts)


def ragged(own_key, count, total, limit, lean):
    if count == 2:
        one = jax.random.randint(own_key, (), max(1, total - limit), min(limit, total - 1) + 1)
        return jnp.stack([one, total - one])
    tallies = jnp.asarray(split_up(count, total, limit, lean), jnp.int32)
    couples = (count - 1) // 2
    donor, sink = tallies[1:1 + 2 * couples:2], tallies[2:2 + 2 * couples:2]
    margin = jnp.minimum(donor - 1, limit - sink)
    passed = jax.random.randint(jax.random.fold_in(own_key, 1), (couples,), 0, 1 << 20) % (margin + 1)
    tallies = tallies.at[1:1 + 2 * couples:2].set(donor - passed).at[2:2 + 2 * couples:2].set(sink + passed)
    return tallies[jax.random.permutation(jax.random.fold_in(own_key, 2), count)]


def normal_values(stream_key, dims, spread, limit, cuts=(), held_as=jnp.bfloat16):
    level = block_scale(stream_key, dims, cuts, -0.22, 0.18) if cuts else 1.0
    entries = jax.random.normal(stream_key, dims, jnp.float32) * spread * level
    return jnp.minimum(jnp.maximum(entries, -limit), limit).astype(held_as)


def setup_inputs(seed: int = 0, part: int = 0) -> dict:
    seeds = jax.random.split(jax.random.key(seed), 10)
    own_keys = jax.random.split(jax.random.fold_in(seeds[9], part), 10)
    tokens = draw_tokens(jax.random.fold_in(jax.random.fold_in(seeds[9], part), 71), part)
    w_qkv = normal_values(seeds[1], (3, D, D), (D // 4) ** -0.5, 0.375, ((2, 2),))
    w_out = normal_values(seeds[2], (D, D), D ** -0.5, 0.1875, ((0, 2),))
    ln_gain = jnp.clip(1.0 + 0.1 * jax.random.normal(seeds[3], (D,), jnp.float32), 0.5, 1.5)
    ln_bias = normal_values(seeds[4], (D,), 0.5, 3.0, ((0, 2),), jnp.float32)
    random_blocks = draw_random_blocks(jax.random.fold_in(jax.random.fold_in(seeds[9], part), 71), part)
    summary_pos = draw_summary_pos(jax.random.fold_in(jax.random.fold_in(seeds[9], part), 71), part)
    summary_blocks = draw_summary_blocks(jax.random.fold_in(jax.random.fold_in(seeds[9], part), 71), part)
    pair_lengths = jax.vmap(lambda own: ragged(own, PAIRS, SEQ_LEN, 3 * SEQ_LEN // 4, 0))(jax.random.split(own_keys[8], SEQS)).reshape((SEQS, PAIRS)).astype(jnp.int32)
    return {"tokens": tokens, "w_qkv": w_qkv, "w_out": w_out, "ln_gain": ln_gain, "ln_bias": ln_bias, "random_blocks": random_blocks, "summary_pos": summary_pos, "summary_blocks": summary_blocks, "pair_lengths": pair_lengths}


MASKED = -1e+30

def segment_ids(positions, bounds):
    return lax.optimization_barrier(jnp.sum((positions[..., None] >= bounds).astype(jnp.int32), axis=-1))

def attend(queries, keys, values, allowed, head_count):
    group_count, query_len, all_width = queries.shape
    key_len = keys.shape[1]
    query_heads = queries.astype(jnp.float32).reshape(group_count, query_len, head_count, HEAD)
    key_heads = keys.astype(jnp.float32).reshape(group_count, key_len, head_count, HEAD)
    value_heads = values.astype(jnp.float32).reshape(group_count, key_len, head_count, HEAD)
    scores = jnp.einsum('gqhe,gkhe->ghqk', query_heads, key_heads) * HEAD ** (-0.5)
    scores = jnp.where(allowed[:, None], scores, MASKED)
    maxima = lax.optimization_barrier(jnp.max(scores, axis=-1, keepdims=True))
    weights = jnp.where(allowed[:, None], jnp.exp(scores - maxima), 0.0)
    totals = lax.optimization_barrier(jnp.sum(weights, axis=-1))
    rounded = lax.optimization_barrier(weights.astype(jnp.bfloat16)).astype(jnp.float32)
    mixture = jnp.einsum('ghqk,gkhe->gqhe', rounded, value_heads)
    mixture = mixture / jnp.transpose(totals, (0, 2, 1))[..., None]
    return mixture.reshape(group_count, query_len, all_width).astype(jnp.bfloat16)

def one_sequence(seq_tokens, w_qkv, w_out, ln_gain, ln_bias, random_rows, summary_rows, summary_lists, pair_row):
    seq_len = seq_tokens.shape[0]
    block_count = seq_len // BLOCK
    queries = jnp.dot(seq_tokens, w_qkv[0], preferred_element_type=jnp.float32).astype(jnp.bfloat16)
    keys = jnp.dot(seq_tokens, w_qkv[1], preferred_element_type=jnp.float32).astype(jnp.bfloat16)
    values = jnp.dot(seq_tokens, w_qkv[2], preferred_element_type=jnp.float32).astype(jnp.bfloat16)
    bounds = jnp.cumsum(pair_row)
    positions = jnp.arange(seq_len, dtype=jnp.int32)
    segments = segment_ids(positions, bounds)
    padding = jnp.zeros((BLOCK, keys.shape[1]), jnp.bfloat16)
    keys_pad = jnp.concatenate([padding, keys, padding], axis=0)
    values_pad = jnp.concatenate([padding, values, padding], axis=0)
    rim_pos = jnp.arange(seq_len + 2 * BLOCK, dtype=jnp.int32) - BLOCK
    rim_ok = (rim_pos >= 0) & (rim_pos < seq_len)
    rim_seg = segment_ids(rim_pos, bounds)
    offsets = jnp.arange(BLOCK, dtype=jnp.int32)

    def per_block(block_index):
        first_row = (block_index * BLOCK).astype(jnp.int32)
        query_block = lax.dynamic_slice_in_dim(queries, first_row, BLOCK, 0)
        near_keys = lax.dynamic_slice_in_dim(keys_pad, first_row, 3 * BLOCK, 0)
        near_values = lax.dynamic_slice_in_dim(values_pad, first_row, 3 * BLOCK, 0)
        far_pos = (random_rows[block_index][:, None] * BLOCK + offsets[None, :]).reshape(-1).astype(jnp.int32)
        all_keys = jnp.concatenate([near_keys, jnp.take(keys, far_pos, axis=0)], axis=0)
        all_values = jnp.concatenate([near_values, jnp.take(values, far_pos, axis=0)], axis=0)
        key_seg = jnp.concatenate([lax.dynamic_slice_in_dim(rim_seg, first_row, 3 * BLOCK, 0), jnp.take(segments, far_pos)])
        key_ok = jnp.concatenate([lax.dynamic_slice_in_dim(rim_ok, first_row, 3 * BLOCK, 0), jnp.ones((far_pos.shape[0],), jnp.bool_)])
        query_seg = lax.dynamic_slice_in_dim(segments, first_row, BLOCK, 0)
        allowed = key_ok[None, :] & (key_seg[None, :] == query_seg[:, None])
        return attend(query_block[None], all_keys[None], all_values[None], allowed[None], HEADS)[0]
    blocks_out = lax.map(per_block, jnp.arange(block_count, dtype=jnp.int32)).reshape(seq_len, -1)
    list_len = summary_lists.shape[1]
    slot_order = jnp.arange(list_len, dtype=jnp.int32)

    def per_summary(summary_index):
        position = summary_rows[summary_index].astype(jnp.int32)
        listing = summary_lists[summary_index]
        repeated = jnp.any((listing[:, None] == listing[None, :]) & (slot_order[None, :] < slot_order[:, None]), axis=1)
        key_pos = (listing[:, None] * BLOCK + offsets[None, :]).reshape(-1).astype(jnp.int32)
        fresh = jnp.repeat(jnp.logical_not(repeated), BLOCK)
        allowed = fresh & (jnp.take(segments, key_pos) == segments[position])
        query_row = lax.dynamic_slice_in_dim(queries, position, 1, 0)
        listed_keys = jnp.take(keys, key_pos, axis=0)
        listed_values = jnp.take(values, key_pos, axis=0)
        return attend(query_row[None], listed_keys[None], listed_values[None], allowed[None, None], HEADS)[0, 0]
    summary_out = lax.map(per_summary, jnp.arange(summary_rows.shape[0], dtype=jnp.int32))
    attention = blocks_out.at[summary_rows].set(summary_out)
    part_cols = attention.shape[1] // N_HEADS
    summed = jnp.zeros((seq_len, w_out.shape[1]), jnp.float32)
    for group_index in range(N_HEADS):
        low_col = group_index * part_cols
        term = jnp.dot(attention[:, low_col:low_col + part_cols], w_out[low_col:low_col + part_cols], preferred_element_type=jnp.float32)
        summed = summed + lax.optimization_barrier(term.astype(jnp.bfloat16)).astype(jnp.float32)
    hidden = seq_tokens.astype(jnp.float32) + summed
    row_mean = lax.optimization_barrier(jnp.mean(hidden, axis=1, keepdims=True))
    row_var = lax.optimization_barrier(jnp.mean(hidden * hidden, axis=1, keepdims=True)) - row_mean * row_mean
    normed = (hidden - row_mean) * lax.rsqrt(row_var + 1e-05) * ln_gain + ln_bias
    return normed.astype(jnp.bfloat16)

def reference(tokens, w_qkv, w_out, ln_gain, ln_bias, random_blocks, summary_pos, summary_blocks, pair_lengths):
    results = []
    for seq_index in range(tokens.shape[0]):
        results.append(one_sequence(tokens[seq_index], w_qkv, w_out, ln_gain, ln_bias, random_blocks[seq_index], summary_pos[seq_index], summary_blocks[seq_index], pair_lengths[seq_index]))
    return jnp.stack(results)
```

```python
import functools

import jax
import jax.numpy as jnp
from jax import lax
from jax.experimental import pallas as pl
from jax.experimental.pallas import tpu as pltpu
from jax.sharding import PartitionSpec as P

HEAD = 64
BLOCK = 128


MASKED = -1e30
LOG2E = 1.4426950408889634


def extended(x, sides, width):
    for axis, dim in sides:
        size, length = (lax.axis_size(axis), x.shape[dim])
        up = [(i, (i + 1) % size) for i in range(size - 1)]
        down = [(j, i) for i, j in up]
        last = lax.slice_in_dim(x, length - width, length, axis=dim)
        first = lax.slice_in_dim(x, 0, width, axis=dim)
        before = lax.ppermute(last, axis, up)
        after = lax.ppermute(first, axis, down)
        x = jnp.concatenate([before, x, after], axis=dim)
    return x


def segment_ids(positions, bounds):
    return jnp.sum((positions[..., None] >= bounds).astype(jnp.int32), axis=-1)


def attend(queries, keys, values, allowed, head_count):
    group_count, query_len, all_width = queries.shape
    key_len = keys.shape[1]
    query_heads = queries.reshape(group_count, query_len, head_count, HEAD)
    key_heads = keys.reshape(group_count, key_len, head_count, HEAD)
    value_heads = values.reshape(group_count, key_len, head_count, HEAD)
    scores = jnp.einsum(
        "gqhe,gkhe->ghqk", query_heads, key_heads, preferred_element_type=jnp.float32
    ) * HEAD ** (-0.5)
    scores = jnp.where(allowed[:, None], scores, MASKED)
    maxima = jnp.max(scores, axis=-1, keepdims=True)
    weights = jnp.where(allowed[:, None], jnp.exp(scores - maxima), 0.0)
    totals = jnp.sum(weights, axis=-1)
    mixture = jnp.einsum(
        "ghqk,gkhe->gqhe",
        weights.astype(jnp.bfloat16),
        value_heads,
        preferred_element_type=jnp.float32,
    )
    mixture = mixture / jnp.transpose(totals, (0, 2, 1))[..., None]
    return mixture.reshape(group_count, query_len, all_width).astype(jnp.bfloat16)


def three_views(window_span, group_size, axis_pos):
    views = []
    for shift_index in range(3):
        piece = lax.slice_in_dim(
            window_span,
            shift_index * BLOCK,
            shift_index * BLOCK + group_size * BLOCK,
            axis=axis_pos,
        )
        new_shape = (
            window_span.shape[:axis_pos] + (group_size, BLOCK) + window_span.shape[axis_pos + 1 :]
        )
        views.append(piece.reshape(new_shape))
    return jnp.concatenate(views, axis=axis_pos + 1)


def shards(
    tokens, w_qkv, w_out, ln_gain, ln_bias, random_blocks, summary_pos, summary_blocks, pair_lengths
):
    tok_rows = tokens.shape[1]
    head_cols = tokens.shape[2]
    heads_here = head_cols // HEAD
    full_width = w_out.shape[1]
    ctx_count = lax.axis_size("ctx")
    ctx_index = lax.axis_index("ctx")
    block_count = tok_rows // BLOCK
    seq_total = tok_rows * ctx_count
    bounds = jnp.cumsum(pair_lengths[0])
    own_tokens = tokens[0]
    projected = jnp.einsum(
        "nc,kcd->knd",
        lax.all_gather(own_tokens, "heads", axis=1, tiled=True),
        w_qkv,
        preferred_element_type=jnp.float32,
    ).astype(jnp.bfloat16)
    queries = projected[0]
    own_kv = projected[1:3]
    rim_kv = extended(own_kv, (("ctx", 1),), BLOCK)
    query_pos = ctx_index * tok_rows + jnp.arange(tok_rows, dtype=jnp.int32)
    own_seg = segment_ids(query_pos, bounds)
    rim_pos = ctx_index * tok_rows - BLOCK + jnp.arange(tok_rows + 2 * BLOCK, dtype=jnp.int32)
    rim_ok = (rim_pos >= 0) & (rim_pos < seq_total)
    rim_seg = segment_ids(rim_pos, bounds)
    rand_count = random_blocks.shape[2]
    picked = random_blocks[0].reshape(-1)
    pick_count = picked.shape[0]
    capacity = max(2, -(-pick_count // ctx_count))
    owners = picked // block_count
    within = picked % block_count
    slot_order = jnp.arange(pick_count, dtype=jnp.int32)
    earlier = (owners[:, None] == owners[None, :]) & (slot_order[None, :] < slot_order[:, None])
    pick_rank = jnp.sum(earlier.astype(jnp.int32), axis=1)
    pick_slot = owners * capacity + pick_rank
    slot_table = (
        pick_slot[:, None] == jnp.arange(ctx_count * capacity, dtype=jnp.int32)[None, :]
    ).astype(jnp.int32)
    requests = jnp.sum(slot_table * within[:, None], axis=0).reshape(ctx_count, capacity)
    own_blocks = own_kv.reshape(2, block_count, BLOCK, head_cols).transpose(1, 0, 2, 3)
    reply = jnp.take(
        own_blocks, lax.all_to_all(requests, "ctx", split_axis=0, concat_axis=0, tiled=True), axis=0
    )
    fetched = lax.all_to_all(reply, "ctx", split_axis=0, concat_axis=0, tiled=True)
    flat_blocks = fetched.reshape(ctx_count * capacity, 2, BLOCK, head_cols)
    far_kv = jnp.take(flat_blocks, pick_slot, axis=0).reshape(
        block_count, rand_count, 2, BLOCK, head_cols
    )
    far_kv = far_kv.transpose(2, 0, 1, 3, 4).reshape(2, block_count, rand_count * BLOCK, head_cols)
    far_pos = (
        picked.reshape(block_count, rand_count)[:, :, None] * BLOCK
        + jnp.arange(BLOCK, dtype=jnp.int32)
    ).reshape(block_count, rand_count * BLOCK)
    far_seg = segment_ids(far_pos, bounds)
    group_size = min(4, block_count)
    group_steps = block_count // group_size

    def window_step(unused, step_index):
        near_kv = three_views(rim_kv, group_size, 1)
        near_ok = three_views(rim_ok, group_size, 0)
        near_seg = three_views(rim_seg, group_size, 0)
        key_set = jnp.concatenate([near_kv, far_kv], axis=2)
        key_seg = jnp.concatenate([near_seg, far_seg], axis=1)
        key_ok = jnp.concatenate([near_ok, jnp.ones(far_seg.shape, jnp.bool_)], axis=1)
        query_seg = own_seg.reshape(group_size, BLOCK)
        allowed = key_ok[:, None, :] & (key_seg[:, None, :] == query_seg[:, :, None])
        query_group = queries.reshape(group_size, BLOCK, head_cols)
        return (unused, attend(query_group, key_set[0], key_set[1], allowed, heads_here))

    _, window_out = lax.scan(window_step, 0, jnp.arange(group_steps, dtype=jnp.int32))
    attention = window_out.reshape(tok_rows, head_cols)
    summary_rows = summary_pos[0]
    summary_lists = summary_blocks[0]
    summaries = summary_rows.shape[0]
    per_device = summaries // ctx_count
    mine = (
        lax.dynamic_slice_in_dim(summary_rows, ctx_index * per_device, per_device, 0)
        - ctx_index * tok_rows
    )
    summary_query = jnp.take(queries, mine, axis=0)
    all_queries = lax.all_gather(summary_query, "ctx", axis=0, tiled=True)
    summary_seg = segment_ids(summary_rows, bounds)
    key_block = ctx_index * block_count + jnp.arange(block_count, dtype=jnp.int32)
    listed = jnp.any(summary_lists[:, :, None] == key_block[None, None, :], axis=1)
    key_heads = own_kv[0].reshape(tok_rows, heads_here, HEAD)
    value_heads = own_kv[1].reshape(tok_rows, heads_here, HEAD)
    summary_group = min(128, summaries)
    group_total = summaries // summary_group

    def group_scores():
        query_part = all_queries.reshape(summary_group, heads_here, HEAD)
        allowed = jnp.broadcast_to(listed[:, :, None], (summary_group, block_count, BLOCK)).reshape(
            summary_group, tok_rows
        )
        allowed = allowed & (own_seg[None, :] == summary_seg[:, None])
        scores = jnp.einsum(
            "qhe,khe->hqk", query_part, key_heads, preferred_element_type=jnp.float32
        ) * HEAD ** (-0.5)
        return (jnp.where(allowed[None], scores, MASKED), allowed)

    def weigh(scores, allowed, maxima):
        weights = jnp.where(allowed[None], jnp.exp(scores - maxima[:, :, None]), 0.0)
        totals = jnp.sum(weights, axis=-1)
        mixture = jnp.einsum(
            "hqk,khe->qhe",
            weights.astype(jnp.bfloat16),
            value_heads,
            preferred_element_type=jnp.float32,
        )
        return (totals.T, mixture.reshape(summary_group, head_cols))

    def max_step(unused, group_index):
        scores, allowed = group_scores()
        return (unused, jnp.max(scores, axis=-1).T)

    _, maxima_all = lax.scan(max_step, 0, jnp.arange(group_total, dtype=jnp.int32))
    maxima_all = lax.pmax(maxima_all.reshape(summaries, heads_here), "ctx")

    def sum_step(unused, group_index):
        scores, allowed = group_scores()
        maxima = maxima_all.T
        return (unused, weigh(scores, allowed, maxima))

    _, (totals_all, mixture_all) = lax.scan(sum_step, 0, jnp.arange(group_total, dtype=jnp.int32))
    totals_all = totals_all.reshape(summaries, heads_here)
    mixture_all = mixture_all.reshape(summaries, head_cols)
    totals_all, mixture_all = (
        lax.psum(totals_all.astype(jnp.bfloat16), "ctx").astype(jnp.float32),
        lax.psum(mixture_all.astype(jnp.bfloat16), "ctx").astype(jnp.float32),
    )
    own_totals = lax.dynamic_slice_in_dim(totals_all, ctx_index * per_device, per_device, 0)
    own_mixture = lax.dynamic_slice_in_dim(mixture_all, ctx_index * per_device, per_device, 0)
    summary_out = (own_mixture / jnp.repeat(own_totals, HEAD, axis=1)).astype(jnp.bfloat16)
    attention = attention.at[mine].set(summary_out)
    partial_value = jnp.dot(attention, w_out, preferred_element_type=jnp.float32)
    summed = lax.psum_scatter(
        partial_value.astype(jnp.bfloat16), "heads", scatter_dimension=1, tiled=True
    ).astype(jnp.float32)
    hidden = own_tokens.astype(jnp.float32) + summed
    row_sums = lax.psum((jnp.sum(hidden, axis=1), jnp.sum(hidden * hidden, axis=1)), "heads")
    row_mean = row_sums[0] / full_width
    row_var = row_sums[1] / full_width - row_mean * row_mean
    normed = (hidden - row_mean[:, None]) * lax.rsqrt(row_var + 1e-05)[:, None] * ln_gain + ln_bias
    return normed.astype(jnp.bfloat16)[None]


def fast_kernel(
    ctx_count, rand, tok_hbm, wq_hbm, wo_hbm, gain_ref, bias_ref, rb_ref, pair_ref, spos_ref,
    slist_ref, out_ref, wq, wo, tok, own, xin, bias, kv_out, kv_in, q_out, q_in, sq_out,
    sq_in, s_ok, s_res, meta_out, meta_in, meta_s, o_out, o_in, rs_out, rs_in, hidden, st_out,
    st_in, w_sem, tok_sem, far_send, own_recv, fwd_send, x_send, x_recv, meta_send, meta_recv, meta_sem, kv_send, kv_recv,
    q_send, q_recv, sq_send, sq_recv, o_send, o_recv, rs_sem, st_sem,
):
    z = lax.axis_index("ctx")
    half = lax.axis_index("heads")
    core = lax.axis_index("dp")
    other = 1 - half
    rows, cols = tok_hbm.shape
    nblk = rows // BLOCK
    wide = kv_in.shape[3]
    group = wide // HEAD
    blocks = ctx_count * nblk
    seq = blocks * BLOCK
    pairs = pair_ref.shape[1]
    listed = slist_ref.shape[1]
    per = spos_ref.shape[1] // ctx_count
    srows = per * group
    side = z // 2
    place = lax.rem(z, 2)
    sib = z + 1 - 2 * place
    home = core == side
    guest = core != side
    gate = z == 1 + side
    mate = 2 * place + core
    away = 2 * (1 - side)
    f32, bf16, i32 = jnp.float32, jnp.bfloat16, jnp.int32
    mates = [(z, 1 - core), (sib, core), (sib, 1 - core)]

    def remote(src, dst, send, recv, to):
        return pltpu.make_async_remote_copy(
            src_ref=src, dst_ref=dst, send_sem=send, recv_sem=recv,
            device_id=to, device_id_type=pl.DeviceIdType.MESH,
        )

    def arrived(dst, sem):
        pltpu.make_async_copy(dst, dst, sem).wait()

    def at_mate(d):
        return {"ctx": mates[d][0], "dp": mates[d][1]}

    def mate_index(d):
        return 2 * lax.rem(mates[d][0], 2) + mates[d][1]

    def band(c):
        return pl.ds(pl.multiple_of(c * BLOCK, BLOCK), BLOCK)

    def lanes(i, size):
        return pl.ds(pl.multiple_of(i * size, size), size)

    def own_local(c):
        return pltpu.make_async_copy(
            tok_hbm.at[band(c)], own.at[0, band(c)], own_recv.at[0, c]
        )

    def far_copy(c):
        return remote(
            tok_hbm.at[band(c)], own.at[place, band(c)], far_send.at[c], own_recv.at[place, c],
            {"ctx": 2 - side, "dp": 1 - core},
        )

    def fwd_copy(r, c):
        return remote(
            own.at[r, band(c)], own.at[r, band(c)], fwd_send.at[r, c], own_recv.at[r, c],
            {"ctx": sib},
        )

    def x_copy(src, r, c):
        return remote(
            src, xin.at[r, band(c)], x_send.at[r, c], x_recv.at[r, c], {"heads": other}
        )

    def meta_copy(m):
        return remote(
            meta_out, meta_in.at[z], meta_send.at[m], meta_recv.at[z],
            {"ctx": 2 * core + m // 2, "dp": m % 2},
        )

    def kv_copy(m, d, slot, r, c):
        return remote(
            kv_out.at[slot, c], kv_in.at[r * nblk + c], kv_send.at[d, c], kv_recv.at[r, c],
            at_mate(m),
        )

    def q_copy(m, d, slot, r, c):
        return remote(
            q_out.at[slot, c], q_in.at[r * nblk + c], q_send.at[d, c], q_recv.at[r, c],
            at_mate(m),
        )

    def sq_copy(m, d, slot, r):
        return remote(
            sq_out.at[slot], sq_in.at[r], sq_send.at[d], sq_recv.at[r],
            at_mate(m),
        )

    def home_copy(copy, d, *c):
        return copy(d, d, mate_index(d), z, *c)

    def guest_copy(copy, r, *c):
        return copy(0, 3 * r, 2 * (1 - core) + r, away + r, *c)

    def local(out, into, sem):
        pltpu.make_async_copy(out, into, sem).start()

    def owner(i):
        return 2 * (1 - side) + i if i < 2 else 2 * side + i - 2

    def o_copy(i, c):
        r = owner(i)
        return remote(
            o_out.at[r * nblk + c], o_in.at[c, :, lanes(mate, wide)], o_send.at[i, c],
            o_recv.at[mate, c], {"ctx": r, "dp": side},
        )

    def o_local(i, c):
        return pltpu.make_async_copy(
            o_out.at[owner(i) * nblk + c], o_in.at[c, :, lanes(mate, wide)], o_recv.at[mate, c]
        )

    def rs_copy(c):
        return remote(rs_out.at[c], rs_in.at[c], rs_sem.at[0, c], rs_sem.at[1, c], {"heads": other})

    def st_copy(c):
        return remote(st_out.at[c], st_in.at[c], st_sem.at[0, c], st_sem.at[1, c], {"heads": other})

    tok_copy = pltpu.make_async_copy(tok_hbm, tok, tok_sem)
    two = 2 * wide

    def w_copy(k, part):
        if part:
            return pltpu.make_async_copy(
                wq_hbm.at[k, :, lanes(place, two)], wq.at[k, :, pl.ds(0, two)], w_sem.at[k]
            )
        return pltpu.make_async_copy(wq_hbm.at[k], wq.at[k], w_sem.at[k])

    wo_copy = pltpu.make_async_copy(wo_hbm, wo, w_sem.at[3])
    barrier = pltpu.get_barrier_semaphore()
    greeted = [{"heads": other}, {"dp": 1 - core}]
    for d in range(1, ctx_count):
        for other_core in range(2):
            greeted.append({"ctx": lax.rem(z + d, ctx_count), "dp": other_core})
    for to in greeted:
        pl.semaphore_signal(barrier, inc=1, device_id=to, device_id_type=pl.DeviceIdType.MESH)

    @pl.when(home)
    def _():
        for c in range(nblk):
            own_local(c).start()
        for k in (1, 2, 0):
            w_copy(k, False).start()

    @pl.when(guest)
    def _():
        for k in (1, 2, 0):
            w_copy(k, True).start()

    tok_copy.start()
    wo_copy.start()
    meta_out[...] = jnp.zeros_like(meta_out)
    for r in range(rand):
        meta_out[r : r + 1, :nblk] = rb_ref[r]
    meta_out[rand : rand + 1, : ctx_count * per] = spos_ref[...]
    meta_out[rand + 1 : rand + 2, :pairs] = pair_ref[...]
    meta_out[8 : 8 + listed, : ctx_count * per] = slist_ref[0]
    pl.semaphore_wait(barrier, len(greeted))

    for m in range(4):
        itself = home & (mate == m)

        @pl.when(itself)
        def _():
            pltpu.make_async_copy(meta_out, meta_in.at[z], meta_recv.at[z]).start()

        @pl.when(jnp.logical_not(itself))
        def _():
            meta_copy(m).start()

    @pl.when(home)
    def _():
        for c in range(nblk):
            x_copy(tok_hbm.at[band(c)], 0, c).start()

    @pl.when(guest)
    def _():
        for c in range(nblk):
            far_copy(c).start()

    def relay(r, c):
        arrived(own.at[r, band(c)], own_recv.at[r, c])

        @pl.when(gate)
        def _():
            fwd_copy(r, c).start()

        x_copy(own.at[r, band(c)], r, c).start()

    def product(k, r, c, width):
        val = jnp.dot(
            own[r, band(c), :], wq[k, lanes(half, cols), :width], preferred_element_type=f32
        )
        val = val + jnp.dot(
            xin[r, band(c), :], wq[k, lanes(other, cols), :width], preferred_element_type=f32
        )
        return val.astype(bf16)

    def project_home(c):
        arrived(own.at[0, band(c)], own_recv.at[0, c])
        arrived(xin.at[0, band(c)], x_recv.at[0, c])
        for k in (1, 2):
            val = product(k, 0, c, cols)
            for m in range(4):
                kv_out[m, c, k - 1] = val[:, m * wide : (m + 1) * wide]
        home_copy(kv_copy, 0, c).start()

        @pl.when(jnp.logical_not(gate))
        def _():
            for d in (1, 2):
                home_copy(kv_copy, d, c).start()

        local(kv_out.at[mate, c], kv_in.at[z * nblk + c], kv_recv.at[z, c])
        val = product(0, 0, c, cols)
        for m in range(4):
            q_out[m, c] = val[:, m * wide : (m + 1) * wide]
        home_copy(q_copy, 0, c).start()
        local(q_out.at[mate, c], q_in.at[z * nblk + c], q_recv.at[z, c])

    def project_guest(r, c):
        b = (away + r) * nblk + c
        arrived(xin.at[r, band(c)], x_recv.at[r, c])
        for k in (1, 2):
            val = product(k, r, c, two)
            for m in range(2):
                kv_out[2 * m + r, c, k - 1] = val[:, m * wide : (m + 1) * wide]
        guest_copy(kv_copy, r, c).start()
        local(kv_out.at[2 * core + r, c], kv_in.at[b], kv_recv.at[away + r, c])
        val = product(0, r, c, two)
        for m in range(2):
            q_out[2 * m + r, c] = val[:, m * wide : (m + 1) * wide]
        guest_copy(q_copy, r, c).start()
        local(q_out.at[2 * core + r, c], q_in.at[b], q_recv.at[away + r, c])

    def w_wait(part):
        for k in (1, 2, 0):
            w_copy(k, part).wait()

    order = [(1 - side, c) for c in range(nblk)] + [(side, c) for c in range(nblk)]
    ahead = 3

    @pl.when(guest)
    def _():
        for r, c in order[:ahead]:
            relay(r, c)

    for r in range(ctx_count):
        arrived(meta_in.at[r], meta_recv.at[r])
    meta_local = pltpu.make_async_copy(meta_in, meta_s, meta_sem)
    meta_local.start()
    meta_local.wait()

    bounds = []
    total = 0
    for p in range(pairs):
        total = total + meta_s[0, rand + 1, p]
        bounds.append(total)

    def segments(pos):
        seg = jnp.zeros(pos.shape, i32)
        for bound in bounds:
            seg = seg + jnp.where(pos >= bound, 1, 0)
        return seg

    def spos(i):
        return meta_s[0, rand, i]

    row_1 = lax.broadcasted_iota(i32, (BLOCK, 1), 0)
    lane_1 = lax.broadcasted_iota(i32, (1, BLOCK), 1)

    def mask_block(b, carry):
        r, c = b // nblk, lax.rem(b, nblk)
        seg_q = segments(b * BLOCK + row_1)
        for j in range(3 + rand):
            if j < 3:
                pos = (b + j - 1) * BLOCK + lane_1
                seg = jnp.where((pos >= 0) & (pos < seq), segments(pos), -1)
            else:
                seg = segments(meta_s[r, j - 3, c] * BLOCK + lane_1)
            bias[b, :, j * BLOCK : (j + 1) * BLOCK] = jnp.where(seg_q == seg, 0.0, MASKED)
        return carry

    def masks():
        lax.fori_loop(0, blocks, mask_block, 0)
        key_pos = lax.broadcasted_iota(i32, (1, seq), 1)
        row_all = lax.broadcasted_iota(i32, (ctx_count * srows, 1), 0)
        bits = jnp.zeros((ctx_count * srows, 1), i32)
        places = jnp.zeros((ctx_count * srows, 1), i32)
        for u in range(ctx_count * per):
            word = 0
            for j in range(listed):
                word = word | (1 << meta_s[0, 8 + j, u])
            for g in range(group):
                here = row_all == u // per * srows + g * per + u % per
                bits = jnp.where(here, word, bits)
                places = jnp.where(here, spos(u), places)
        hit = lax.shift_right_logical(
            jnp.broadcast_to(bits, s_ok.shape), jnp.broadcast_to(key_pos // BLOCK, s_ok.shape)
        )
        s_ok[...] = jnp.where(segments(places) == segments(key_pos), hit & 1, 0)

    masks()

    @pl.when(home)
    def _():
        w_wait(False)
        for c in range(nblk):
            project_home(c)

    @pl.when(guest)
    def _():
        w_wait(True)
        for i in range(len(order)):
            project_guest(*order[i])
            if i + ahead < len(order):
                relay(*order[i + ahead])

    row8 = lax.broadcasted_iota(i32, (srows, BLOCK), 0)
    col8 = lax.broadcasted_iota(i32, (srows, BLOCK), 1)

    def pick_rows(slot, r):
        wanted = jnp.zeros((srows, BLOCK), i32)
        for i in range(srows):
            wanted = jnp.where(row8 == i, spos(r * per + i % per), wanted)
        found = jnp.zeros((srows, wide), f32)
        for c in range(nblk):
            pick = (wanted == (r * nblk + c) * BLOCK + col8).astype(f32).astype(bf16)
            found = found + jnp.dot(pick, q_out[slot, c], preferred_element_type=f32)
        sq_out[slot] = found

    @pl.when(home)
    def _():
        for m in range(4):
            pick_rows(m, z)
        for d in (1, 2, 0):
            home_copy(sq_copy, d).start()
        local(sq_out.at[mate], sq_in.at[z], sq_recv.at[z])

    @pl.when(guest)
    def _():
        for r in range(2):
            for m in range(2):
                pick_rows(2 * m + r, away + r)
            guest_copy(sq_copy, r).start()
            local(sq_out.at[2 * core + r], sq_in.at[away + r], sq_recv.at[away + r])

    def range_wait(r):
        for c in range(nblk):
            arrived(kv_in.at[r * nblk + c], kv_recv.at[r, c])

    def to_sibling(copy):
        for c in range(nblk):
            for d in (1, 2):
                home_copy(copy, d, c).start()

    range_wait(away + 1 - side)

    @pl.when(home)
    def _():
        @pl.when(gate)
        def _():
            to_sibling(kv_copy)

        to_sibling(q_copy)

    range_wait(z)
    range_wait(away + side)
    range_wait(sib)
    for r in range(ctx_count):
        arrived(sq_in.at[r], sq_recv.at[r])

    factor = HEAD ** (-0.5)
    nt = (((1,), (1,)), ((), ()))

    def softmax(scores, ok):
        scores = jnp.where(ok, scores * factor, MASKED)
        top = jnp.max(scores, axis=1, keepdims=True)
        weights = jnp.exp(scores - top)
        return weights, jnp.sum(weights, axis=1, keepdims=True)

    lane_head = lax.broadcasted_iota(i32, (ctx_count * srows, wide), 1) // HEAD
    row_head = lax.rem(lax.broadcasted_iota(i32, (ctx_count * srows, wide), 0), srows) // per
    sq = sq_in[...].reshape(ctx_count * srows, wide)
    sq = jnp.where(lane_head == row_head, sq, 0.0).astype(bf16)
    all_k = kv_in[:, 0].reshape(seq, wide)
    scores = lax.dot_general(sq, all_k, nt, preferred_element_type=f32)
    weights, totals = softmax(scores, s_ok[...] > 0)
    all_v = kv_in[:, 1].reshape(seq, wide)
    mixed = jnp.dot(weights.astype(bf16), all_v, preferred_element_type=f32) / totals
    s_res[...] = mixed.reshape(ctx_count, srows, wide)

    lane_q = lax.broadcasted_iota(i32, (BLOCK, wide), 1) // HEAD
    row_q = lax.broadcasted_iota(i32, (BLOCK, wide), 0)
    ones = jnp.ones(((3 + rand) * BLOCK, wide), bf16)

    def attend_block(r, c):
        b = r * nblk + c
        q = q_in[b]
        keys, values = [], []
        for shift in (-1, 0, 1):
            at = jnp.clip(b + shift, 0, blocks - 1)
            keys.append(kv_in[at, 0])
            values.append(kv_in[at, 1])
        for j in range(rand):
            at = meta_s[r, j, c]
            keys.append(kv_in[at, 0])
            values.append(kv_in[at, 1])
        keys = jnp.concatenate(keys, axis=0)
        values = jnp.concatenate([jnp.concatenate(values, axis=0), ones], axis=1)
        out = jnp.zeros((BLOCK, wide), f32)
        for g in range(group):
            qg = jnp.where(lane_q == g, q, jnp.zeros_like(q))
            scores = lax.dot_general(qg, keys, nt, preferred_element_type=f32) + bias[b]
            top = jnp.max(scores, axis=1, keepdims=True)
            weights = jnp.exp2((scores - top) * (factor * LOG2E))
            mix = jnp.dot(weights.astype(bf16), values, preferred_element_type=f32)
            out = jnp.where(lane_q == g, mix[:, :wide] / mix[:, wide:], out)
        res = s_res[r]
        for u in range(per):
            row = res[u : u + 1, :]
            for g in range(1, group):
                row = jnp.where(
                    lane_q[:1] == g, res[g * per + u : g * per + u + 1, :], row
                )
            out = jnp.where(row_q == spos(r * per + u) - b * BLOCK, row, out)
        o_out[b] = out.astype(bf16)

    def attend_step(far, c):
        base = 2 * (1 - side) if far else 2 * side
        for i in range(2):
            arrived(q_in.at[(base + i) * nblk + c], q_recv.at[base + i, c])

        def step(i, carry):
            attend_block(base + i, c)
            return carry

        lax.fori_loop(0, 2, step, 0, unroll=2)
        for i in (0, 1) if far else (2, 3):
            if far:
                o_copy(i, c).start()
            else:
                itself = home & (owner(i) == z)

                @pl.when(itself)
                def _():
                    o_local(i, c).start()

                @pl.when(jnp.logical_not(itself))
                def _():
                    o_copy(i, c).start()

    def output(c):
        for m in range(4):
            arrived(o_in.at[c, :, lanes(m, wide)], o_recv.at[m, c])
        att = o_in[c]
        rs_out[c] = jnp.dot(att, wo[:, lanes(other, cols)], preferred_element_type=f32).astype(bf16)
        rs_copy(c).start()
        term = jnp.dot(att, wo[:, lanes(half, cols)], preferred_element_type=f32).astype(bf16)
        hidden[band(c), :] = term.astype(f32)

    lane_s = lax.broadcasted_iota(i32, (BLOCK, BLOCK), 1)

    def finish(c):
        arrived(rs_in.at[c], rs_sem.at[1, c])
        hid = tok[band(c), :].astype(f32) + (hidden[band(c), :] + rs_in[c].astype(f32))
        hidden[band(c), :] = hid
        first = jnp.sum(hid, axis=1, keepdims=True)
        second = jnp.sum(hid * hid, axis=1, keepdims=True)
        both = jnp.where(lane_s == 0, first, jnp.where(lane_s == 1, second, 0.0))
        st_out[c] = jnp.transpose(both)[:8]
        st_copy(c).start()

    full = 2 * cols

    def norm(c):
        arrived(st_in.at[c], st_sem.at[1, c])
        sums = jnp.transpose(st_out[c] + st_in[c])
        mean = sums[:, 0:1] / full
        var = sums[:, 1:2] / full - mean * mean
        hid = hidden[band(c), :]
        res = (hid - mean) * lax.rsqrt(var + 1e-05) * gain_ref[...] + bias_ref[...]
        out_ref[band(c), :] = res.astype(bf16)

    wo_copy.wait()
    tok_copy.wait()

    def at_home(*steps):
        @pl.when(home)
        def _():
            for do, c in steps:
                do(c)

    def at_guest(*steps):
        @pl.when(guest)
        def _():
            for do, c in steps:
                do(c)

    split = nblk // 2
    for c in range(split):
        attend_step(True, c)
    for c in range(split):
        attend_step(False, c)
    for c in range(split, nblk):
        attend_step(True, c)
    at_home(*[(output, c) for c in range(split)])
    for c in range(split, nblk):
        attend_step(False, c)
    at_home(
        *[(output, c) for c in range(split, nblk)], *[(finish, c) for c in range(nblk)],
        *[(norm, c) for c in range(nblk)],
    )
    tail = []
    for c in range(nblk + 2):
        if c < nblk:
            tail.append((output, c))
        if 1 <= c <= nblk:
            tail.append((finish, c - 1))
        if c >= 2:
            tail.append((norm, c - 2))
    at_guest(*tail)

    for m in range(4):
        @pl.when(jnp.logical_not(home & (mate == m)))
        def _():
            meta_copy(m).wait_send()

    @pl.when(home)
    def _():
        for c in range(nblk):
            x_copy(tok_hbm.at[band(c)], 0, c).wait_send()
            for d in range(3):
                home_copy(kv_copy, d, c).wait_send()
                home_copy(q_copy, d, c).wait_send()
        for d in range(3):
            home_copy(sq_copy, d).wait_send()

    @pl.when(guest)
    def _():
        for c in range(nblk):
            far_copy(c).wait_send()
            for r in range(2):
                x_copy(own.at[r, band(c)], r, c).wait_send()
                guest_copy(kv_copy, r, c).wait_send()
                guest_copy(q_copy, r, c).wait_send()
        for r in range(2):
            guest_copy(sq_copy, r).wait_send()

        @pl.when(gate)
        def _():
            for r, c in order:
                fwd_copy(r, c).wait_send()

    for c in range(nblk):
        rs_copy(c).wait_send()
        st_copy(c).wait_send()
        for i in range(4):
            if i < 2:
                o_copy(i, c).wait_send()
            else:
                @pl.when(jnp.logical_not(home & (owner(i) == z)))
                def _():
                    o_copy(i, c).wait_send()


def fast_shards(
    tokens, w_qkv, w_out, ln_gain, ln_bias, random_blocks, summary_pos, summary_blocks, pair_lengths
):
    ctx_count = lax.axis_size("ctx")
    rows, cols = tokens.shape[1:]
    nblk = rows // BLOCK
    wide = cols // ctx_count
    group = wide // HEAD
    blocks = nblk * ctx_count
    summaries = summary_pos.shape[1]
    per = summaries // ctx_count
    srows = per * group
    rand = random_blocks.shape[2]
    vmem = pl.BlockSpec(memory_space=pltpu.VMEM)
    hbm = pl.BlockSpec(memory_space=pl.ANY)
    bf16, f32, i32 = jnp.bfloat16, jnp.float32, jnp.int32
    dma = pltpu.SemaphoreType.DMA
    out = pl.pallas_call(
        functools.partial(fast_kernel, ctx_count, rand),
        out_shape=jax.ShapeDtypeStruct((rows, cols), bf16),
        in_specs=[hbm, hbm, hbm, vmem, vmem, vmem, vmem, vmem, vmem],
        out_specs=vmem,
        scratch_shapes=[
            pltpu.VMEM((3, 2 * cols, cols), bf16),
            pltpu.VMEM(w_out.shape, bf16),
            pltpu.VMEM((rows, cols), bf16),
            pltpu.VMEM((2, rows, cols), bf16),
            pltpu.VMEM((2, rows, cols), bf16),
            pltpu.VMEM((blocks, BLOCK, (3 + rand) * BLOCK), f32),
            pltpu.VMEM((4, nblk, 2, BLOCK, wide), bf16),
            pltpu.VMEM((blocks, 2, BLOCK, wide), bf16),
            pltpu.VMEM((4, nblk, BLOCK, wide), bf16),
            pltpu.VMEM((blocks, BLOCK, wide), bf16),
            pltpu.VMEM((4, srows, wide), f32),
            pltpu.VMEM((ctx_count, srows, wide), f32),
            pltpu.VMEM((ctx_count * srows, blocks * BLOCK), i32),
            pltpu.VMEM((ctx_count, srows, wide), f32),
            pltpu.VMEM((16, 128), i32),
            pltpu.VMEM((ctx_count, 16, 128), i32),
            pltpu.SMEM((ctx_count, 16, 128), i32),
            pltpu.VMEM((blocks, BLOCK, wide), bf16),
            pltpu.VMEM((nblk, BLOCK, cols), bf16),
            pltpu.VMEM((nblk, BLOCK, cols), bf16),
            pltpu.VMEM((nblk, BLOCK, cols), bf16),
            pltpu.VMEM((rows, cols), f32),
            pltpu.VMEM((nblk, 8, BLOCK), f32),
            pltpu.VMEM((nblk, 8, BLOCK), f32),
            dma((4,)),
            dma,
            dma((nblk,)),
            dma((2, nblk)),
            dma((2, nblk)),
            dma((2, nblk)),
            dma((2, nblk)),
            dma((4,)),
            dma((ctx_count,)),
            dma,
            dma((4, nblk)),
            dma((ctx_count, nblk)),
            dma((4, nblk)),
            dma((ctx_count, nblk)),
            dma((4,)),
            dma((ctx_count,)),
            dma((4, nblk)),
            dma((4, nblk)),
            dma((2, nblk)),
            dma((2, nblk)),
        ],
        compiler_params=pltpu.CompilerParams(
            collective_id=0, has_side_effects=True, vmem_limit_bytes=60000 * 1024
        ),
    )(
        tokens[0], w_qkv, w_out, ln_gain[None], ln_bias[None],
        random_blocks.transpose(2, 0, 1), pair_lengths, summary_pos,
        summary_blocks.transpose(0, 2, 1),
    )
    return out[None]


def solution(mesh):
    in_specs = (
        P(("groups", "dp"), "ctx", "heads"),
        P(None, None, "heads"),
        P("heads", None),
        P("heads"),
        P("heads"),
        P(("groups", "dp"), "ctx", None),
        P(("groups", "dp"), None),
        P(("groups", "dp"), None, None),
        P(("groups", "dp"), None),
    )
    out_specs = P(("groups", "dp"), "ctx", "heads")
    ctx_count = mesh.shape["ctx"]

    def body(*args):
        rows, cols = args[0].shape[1:]
        wide = cols // ctx_count
        by_heads = (
            ctx_count == 4
            and mesh.shape["heads"] == 2
            and mesh.shape["dp"] == 2
            and wide > 0
            and wide % 128 == 0
            and wide * ctx_count == cols
            and rows // BLOCK <= 128
            and rows // BLOCK * ctx_count <= 32
            and args[6].shape[1] // ctx_count * (wide // HEAD) % 8 == 0
            and rows // BLOCK >= 2
            and args[5].shape[2] <= 6
            and args[7].shape[2] <= 8
            and max(rows // BLOCK, args[6].shape[1], args[8].shape[1]) <= 128
        )
        return (fast_shards if by_heads else shards)(*args)

    return jax.shard_map(body, mesh=mesh, in_specs=in_specs, out_specs=out_specs, check_vma=False)
```

```python
import functools

import jax
import jax.numpy as jnp
from jax import lax
from jax.experimental import pallas as pl
from jax.experimental.pallas import tpu as pltpu
from jax.sharding import PartitionSpec as P

HEAD = 64
BLOCK = 128


MASKED = -1e30
LOG2E = 1.4426950408889634


def extended(x, sides, width):
    for axis, dim in sides:
        size, length = (lax.axis_size(axis), x.shape[dim])
        up = [(i, (i + 1) % size) for i in range(size - 1)]
        down = [(j, i) for i, j in up]
        last = lax.slice_in_dim(x, length - width, length, axis=dim)
        first = lax.slice_in_dim(x, 0, width, axis=dim)
        before = lax.ppermute(last, axis, up)
        after = lax.ppermute(first, axis, down)
        x = jnp.concatenate([before, x, after], axis=dim)
    return x


def segment_ids(positions, bounds):
    return jnp.sum((positions[..., None] >= bounds).astype(jnp.int32), axis=-1)


def attend(queries, keys, values, allowed, head_count):
    group_count, query_len, all_width = queries.shape
    key_len = keys.shape[1]
    query_heads = queries.reshape(group_count, query_len, head_count, HEAD)
    key_heads = keys.reshape(group_count, key_len, head_count, HEAD)
    value_heads = values.reshape(group_count, key_len, head_count, HEAD)
    scores = jnp.einsum(
        "gqhe,gkhe->ghqk", query_heads, key_heads, preferred_element_type=jnp.float32
    ) * HEAD ** (-0.5)
    scores = jnp.where(allowed[:, None], scores, MASKED)
    maxima = jnp.max(scores, axis=-1, keepdims=True)
    weights = jnp.where(allowed[:, None], jnp.exp(scores - maxima), 0.0)
    totals = jnp.sum(weights, axis=-1)
    mixture = jnp.einsum(
        "ghqk,gkhe->gqhe",
        weights.astype(jnp.bfloat16),
        value_heads,
        preferred_element_type=jnp.float32,
    )
    mixture = mixture / jnp.transpose(totals, (0, 2, 1))[..., None]
    return mixture.reshape(group_count, query_len, all_width).astype(jnp.bfloat16)


def three_views(window_span, group_size, axis_pos):
    views = []
    for shift_index in range(3):
        piece = lax.slice_in_dim(
            window_span,
            shift_index * BLOCK,
            shift_index * BLOCK + group_size * BLOCK,
            axis=axis_pos,
        )
        new_shape = (
            window_span.shape[:axis_pos] + (group_size, BLOCK) + window_span.shape[axis_pos + 1 :]
        )
        views.append(piece.reshape(new_shape))
    return jnp.concatenate(views, axis=axis_pos + 1)


def shards(
    tokens, w_qkv, w_out, ln_gain, ln_bias, random_blocks, summary_pos, summary_blocks, pair_lengths
):
    tok_rows = tokens.shape[1]
    head_cols = tokens.shape[2]
    heads_here = head_cols // HEAD
    full_width = w_out.shape[1]
    ctx_count = lax.axis_size("ctx")
    ctx_index = lax.axis_index("ctx")
    block_count = tok_rows // BLOCK
    seq_total = tok_rows * ctx_count
    bounds = jnp.cumsum(pair_lengths[0])
    own_tokens = tokens[0]
    projected = jnp.einsum(
        "nc,kcd->knd",
        lax.all_gather(own_tokens, "heads", axis=1, tiled=True),
        w_qkv,
        preferred_element_type=jnp.float32,
    ).astype(jnp.bfloat16)
    queries = projected[0]
    own_kv = projected[1:3]
    rim_kv = extended(own_kv, (("ctx", 1),), BLOCK)
    query_pos = ctx_index * tok_rows + jnp.arange(tok_rows, dtype=jnp.int32)
    own_seg = segment_ids(query_pos, bounds)
    rim_pos = ctx_index * tok_rows - BLOCK + jnp.arange(tok_rows + 2 * BLOCK, dtype=jnp.int32)
    rim_ok = (rim_pos >= 0) & (rim_pos < seq_total)
    rim_seg = segment_ids(rim_pos, bounds)
    rand_count = random_blocks.shape[2]
    picked = random_blocks[0].reshape(-1)
    pick_count = picked.shape[0]
    capacity = max(2, -(-pick_count // ctx_count))
    owners = picked // block_count
    within = picked % block_count
    slot_order = jnp.arange(pick_count, dtype=jnp.int32)
    earlier = (owners[:, None] == owners[None, :]) & (slot_order[None, :] < slot_order[:, None])
    pick_rank = jnp.sum(earlier.astype(jnp.int32), axis=1)
    pick_slot = owners * capacity + pick_rank
    slot_table = (
        pick_slot[:, None] == jnp.arange(ctx_count * capacity, dtype=jnp.int32)[None, :]
    ).astype(jnp.int32)
    requests = jnp.sum(slot_table * within[:, None], axis=0).reshape(ctx_count, capacity)
    own_blocks = own_kv.reshape(2, block_count, BLOCK, head_cols).transpose(1, 0, 2, 3)
    reply = jnp.take(
        own_blocks, lax.all_to_all(requests, "ctx", split_axis=0, concat_axis=0, tiled=True), axis=0
    )
    fetched = lax.all_to_all(reply, "ctx", split_axis=0, concat_axis=0, tiled=True)
    flat_blocks = fetched.reshape(ctx_count * capacity, 2, BLOCK, head_cols)
    far_kv = jnp.take(flat_blocks, pick_slot, axis=0).reshape(
        block_count, rand_count, 2, BLOCK, head_cols
    )
    far_kv = far_kv.transpose(2, 0, 1, 3, 4).reshape(2, block_count, rand_count * BLOCK, head_cols)
    far_pos = (
        picked.reshape(block_count, rand_count)[:, :, None] * BLOCK
        + jnp.arange(BLOCK, dtype=jnp.int32)
    ).reshape(block_count, rand_count * BLOCK)
    far_seg = segment_ids(far_pos, bounds)
    group_size = min(4, block_count)
    group_steps = block_count // group_size

    def window_step(unused, step_index):
        near_kv = three_views(rim_kv, group_size, 1)
        near_ok = three_views(rim_ok, group_size, 0)
        near_seg = three_views(rim_seg, group_size, 0)
        key_set = jnp.concatenate([near_kv, far_kv], axis=2)
        key_seg = jnp.concatenate([near_seg, far_seg], axis=1)
        key_ok = jnp.concatenate([near_ok, jnp.ones(far_seg.shape, jnp.bool_)], axis=1)
        query_seg = own_seg.reshape(group_size, BLOCK)
        allowed = key_ok[:, None, :] & (key_seg[:, None, :] == query_seg[:, :, None])
        query_group = queries.reshape(group_size, BLOCK, head_cols)
        return (unused, attend(query_group, key_set[0], key_set[1], allowed, heads_here))

    _, window_out = lax.scan(window_step, 0, jnp.arange(group_steps, dtype=jnp.int32))
    attention = window_out.reshape(tok_rows, head_cols)
    summary_rows = summary_pos[0]
    summary_lists = summary_blocks[0]
    summaries = summary_rows.shape[0]
    per_device = summaries // ctx_count
    mine = (
        lax.dynamic_slice_in_dim(summary_rows, ctx_index * per_device, per_device, 0)
        - ctx_index * tok_rows
    )
    summary_query = jnp.take(queries, mine, axis=0)
    all_queries = lax.all_gather(summary_query, "ctx", axis=0, tiled=True)
    summary_seg = segment_ids(summary_rows, bounds)
    key_block = ctx_index * block_count + jnp.arange(block_count, dtype=jnp.int32)
    listed = jnp.any(summary_lists[:, :, None] == key_block[None, None, :], axis=1)
    key_heads = own_kv[0].reshape(tok_rows, heads_here, HEAD)
    value_heads = own_kv[1].reshape(tok_rows, heads_here, HEAD)
    summary_group = min(128, summaries)
    group_total = summaries // summary_group

    def group_scores():
        query_part = all_queries.reshape(summary_group, heads_here, HEAD)
        allowed = jnp.broadcast_to(listed[:, :, None], (summary_group, block_count, BLOCK)).reshape(
            summary_group, tok_rows
        )
        allowed = allowed & (own_seg[None, :] == summary_seg[:, None])
        scores = jnp.einsum(
            "qhe,khe->hqk", query_part, key_heads, preferred_element_type=jnp.float32
        ) * HEAD ** (-0.5)
        return (jnp.where(allowed[None], scores, MASKED), allowed)

    def weigh(scores, allowed, maxima):
        weights = jnp.where(allowed[None], jnp.exp(scores - maxima[:, :, None]), 0.0)
        totals = jnp.sum(weights, axis=-1)
        mixture = jnp.einsum(
            "hqk,khe->qhe",
            weights.astype(jnp.bfloat16),
            value_heads,
            preferred_element_type=jnp.float32,
        )
        return (totals.T, mixture.reshape(summary_group, head_cols))

    def max_step(unused, group_index):
        scores, allowed = group_scores()
        return (unused, jnp.max(scores, axis=-1).T)

    _, maxima_all = lax.scan(max_step, 0, jnp.arange(group_total, dtype=jnp.int32))
    maxima_all = lax.pmax(maxima_all.reshape(summaries, heads_here), "ctx")

    def sum_step(unused, group_index):
        scores, allowed = group_scores()
        maxima = maxima_all.T
        return (unused, weigh(scores, allowed, maxima))

    _, (totals_all, mixture_all) = lax.scan(sum_step, 0, jnp.arange(group_total, dtype=jnp.int32))
    totals_all = totals_all.reshape(summaries, heads_here)
    mixture_all = mixture_all.reshape(summaries, head_cols)
    totals_all, mixture_all = (
        lax.psum(totals_all.astype(jnp.bfloat16), "ctx").astype(jnp.float32),
        lax.psum(mixture_all.astype(jnp.bfloat16), "ctx").astype(jnp.float32),
    )
    own_totals = lax.dynamic_slice_in_dim(totals_all, ctx_index * per_device, per_device, 0)
    own_mixture = lax.dynamic_slice_in_dim(mixture_all, ctx_index * per_device, per_device, 0)
    summary_out = (own_mixture / jnp.repeat(own_totals, HEAD, axis=1)).astype(jnp.bfloat16)
    attention = attention.at[mine].set(summary_out)
    partial_value = jnp.dot(attention, w_out, preferred_element_type=jnp.float32)
    summed = lax.psum_scatter(
        partial_value.astype(jnp.bfloat16), "heads", scatter_dimension=1, tiled=True
    ).astype(jnp.float32)
    hidden = own_tokens.astype(jnp.float32) + summed
    row_sums = lax.psum((jnp.sum(hidden, axis=1), jnp.sum(hidden * hidden, axis=1)), "heads")
    row_mean = row_sums[0] / full_width
    row_var = row_sums[1] / full_width - row_mean * row_mean
    normed = (hidden - row_mean[:, None]) * lax.rsqrt(row_var + 1e-05)[:, None] * ln_gain + ln_bias
    return normed.astype(jnp.bfloat16)[None]


def fast_kernel(
    ctx_count, rand, tok_hbm, wq_hbm, wo_hbm, gain_ref, bias_ref, rb_ref, pair_ref, spos_ref,
    slist_ref, out_ref, wq, wo, tok, own, xin, bias, kv_out, kv_in, q_out, q_in, sq_out,
    sq_in, s_ok, s_res, meta_out, meta_in, meta_s, o_out, o_in, rs_out, rs_in, hidden, st_out,
    st_in, w_sem, tok_sem, far_send, own_recv, fwd_send, x_send, x_recv, meta_send, meta_recv, meta_sem, kv_send, kv_recv,
    q_send, q_recv, sq_send, sq_recv, o_send, o_recv, rs_sem, st_sem,
    go_sem,
):
    z = lax.axis_index("ctx")
    half = lax.axis_index("heads")
    core = lax.axis_index("dp")
    other = 1 - half
    rows, cols = tok_hbm.shape
    nblk = rows // BLOCK
    wide = kv_in.shape[3]
    group = wide // HEAD
    blocks = ctx_count * nblk
    seq = blocks * BLOCK
    pairs = pair_ref.shape[1]
    listed = slist_ref.shape[1]
    per = spos_ref.shape[1] // ctx_count
    srows = per * group
    side = z // 2
    place = lax.rem(z, 2)
    sib = z + 1 - 2 * place
    home = core == side
    guest = core != side
    gate = z == 1 + side
    mate = 2 * place + core
    away = 2 * (1 - side)
    f32, bf16, i32 = jnp.float32, jnp.bfloat16, jnp.int32
    mates = [(z, 1 - core), (sib, core), (sib, 1 - core)]

    def remote(src, dst, send, recv, to):
        return pltpu.make_async_remote_copy(
            src_ref=src, dst_ref=dst, send_sem=send, recv_sem=recv,
            device_id=to, device_id_type=pl.DeviceIdType.MESH,
        )

    def arrived(dst, sem):
        pltpu.make_async_copy(dst, dst, sem).wait()

    def at_mate(d):
        return {"ctx": mates[d][0], "dp": mates[d][1]}

    def mate_index(d):
        return 2 * lax.rem(mates[d][0], 2) + mates[d][1]

    def band(c):
        return pl.ds(pl.multiple_of(c * BLOCK, BLOCK), BLOCK)

    def lanes(i, size):
        return pl.ds(pl.multiple_of(i * size, size), size)

    def own_local(c):
        return pltpu.make_async_copy(
            tok_hbm.at[band(c)], own.at[0, band(c)], own_recv.at[0, c]
        )

    def far_copy(c):
        return remote(
            tok_hbm.at[band(c)], own.at[place, band(c)], far_send.at[c], own_recv.at[place, c],
            {"ctx": 2 - side, "dp": 1 - core},
        )

    def fwd_copy(r, c):
        return remote(
            own.at[r, band(c)], own.at[r, band(c)], fwd_send.at[r, c], own_recv.at[r, c],
            {"ctx": sib},
        )

    def x_copy(src, r, c):
        return remote(
            src, xin.at[r, band(c)], x_send.at[r, c], x_recv.at[r, c], {"heads": other}
        )

    def meta_copy(m):
        return remote(
            meta_out, meta_in.at[z], meta_send.at[m], meta_recv.at[z],
            {"ctx": 2 * core + m // 2, "dp": m % 2},
        )

    def kv_copy(m, d, slot, r, c):
        return remote(
            kv_out.at[slot, c], kv_in.at[r * nblk + c], kv_send.at[d, c], kv_recv.at[r, c],
            at_mate(m),
        )

    def q_copy(m, d, slot, r, c):
        return remote(
            q_out.at[slot, c], q_in.at[r * nblk + c], q_send.at[d, c], q_recv.at[r, c],
            at_mate(m),
        )

    def sq_copy(m, d, slot, r):
        return remote(
            sq_out.at[slot], sq_in.at[r], sq_send.at[d], sq_recv.at[r],
            at_mate(m),
        )

    def home_copy(copy, d, *c):
        return copy(d, d, mate_index(d), z, *c)

    def guest_copy(copy, r, *c):
        return copy(0, 3 * r, 2 * (1 - core) + r, away + r, *c)

    def local(out, into, sem):
        pltpu.make_async_copy(out, into, sem).start()

    def owner(i):
        return 2 * (1 - side) + i if i < 2 else 2 * side + i - 2

    def o_copy(i, c):
        r = owner(i)
        return remote(
            o_out.at[r * nblk + c], o_in.at[c, :, lanes(mate, wide)], o_send.at[i, c],
            o_recv.at[mate, c], {"ctx": r, "dp": side},
        )

    def o_local(i, c):
        return pltpu.make_async_copy(
            o_out.at[owner(i) * nblk + c], o_in.at[c, :, lanes(mate, wide)], o_recv.at[mate, c]
        )

    def rs_copy(c):
        return remote(rs_out.at[c], rs_in.at[c], rs_sem.at[0, c], rs_sem.at[1, c], {"heads": other})

    def st_copy(c):
        return remote(st_out.at[c], st_in.at[c], st_sem.at[0, c], st_sem.at[1, c], {"heads": other})

    tok_copy = pltpu.make_async_copy(tok_hbm, tok, tok_sem)
    two = 2 * wide

    def w_copy(k, part):
        if part:
            return pltpu.make_async_copy(
                wq_hbm.at[k, :, lanes(place, two)], wq.at[k, :, pl.ds(0, two)], w_sem.at[k]
            )
        return pltpu.make_async_copy(wq_hbm.at[k], wq.at[k], w_sem.at[k])

    wo_copy = pltpu.make_async_copy(wo_hbm, wo, w_sem.at[3])
    barrier = pltpu.get_barrier_semaphore()
    greeted = [{"heads": other}, {"dp": 1 - core}]
    for d in range(1, ctx_count):
        for other_core in range(2):
            greeted.append({"ctx": lax.rem(z + d, ctx_count), "dp": other_core})
    for to in greeted:
        pl.semaphore_signal(barrier, inc=1, device_id=to, device_id_type=pl.DeviceIdType.MESH)

    @pl.when(home)
    def _():
        for c in range(nblk):
            own_local(c).start()
        for k in (1, 2, 0):
            w_copy(k, False).start()

    @pl.when(guest)
    def _():
        for k in (1, 2, 0):
            w_copy(k, True).start()

    tok_copy.start()
    wo_copy.start()
    meta_out[...] = jnp.zeros_like(meta_out)
    for r in range(rand):
        meta_out[r : r + 1, :nblk] = rb_ref[r]
    meta_out[rand : rand + 1, : ctx_count * per] = spos_ref[...]
    meta_out[rand + 1 : rand + 2, :pairs] = pair_ref[...]
    meta_out[8 : 8 + listed, : ctx_count * per] = slist_ref[0]
    pl.semaphore_wait(barrier, len(greeted))

    for m in range(4):
        itself = home & (mate == m)

        @pl.when(itself)
        def _():
            pltpu.make_async_copy(meta_out, meta_in.at[z], meta_recv.at[z]).start()

        @pl.when(jnp.logical_not(itself))
        def _():
            meta_copy(m).start()

    @pl.when(home)
    def _():
        for c in range(nblk):
            x_copy(tok_hbm.at[band(c)], 0, c).start()

    @pl.when(guest)
    def _():
        for c in range(nblk):
            far_copy(c).start()

    def relay(r, c):
        arrived(own.at[r, band(c)], own_recv.at[r, c])

        @pl.when(gate)
        def _():
            fwd_copy(r, c).start()

        x_copy(own.at[r, band(c)], r, c).start()

    def product(k, r, c, width):
        val = jnp.dot(
            own[r, band(c), :], wq[k, lanes(half, cols), :width], preferred_element_type=f32
        )
        val = val + jnp.dot(
            xin[r, band(c), :], wq[k, lanes(other, cols), :width], preferred_element_type=f32
        )
        return val.astype(bf16)

    def project_home(c):
        arrived(own.at[0, band(c)], own_recv.at[0, c])
        arrived(xin.at[0, band(c)], x_recv.at[0, c])
        for k in (1, 2):
            val = product(k, 0, c, cols)
            for m in range(4):
                kv_out[m, c, k - 1] = val[:, m * wide : (m + 1) * wide]
        home_copy(kv_copy, 0, c).start()

        @pl.when(jnp.logical_not(gate))
        def _():
            for d in (1, 2):
                home_copy(kv_copy, d, c).start()

        local(kv_out.at[mate, c], kv_in.at[z * nblk + c], kv_recv.at[z, c])
        val = product(0, 0, c, cols)
        for m in range(4):
            q_out[m, c] = val[:, m * wide : (m + 1) * wide]
        home_copy(q_copy, 0, c).start()
        local(q_out.at[mate, c], q_in.at[z * nblk + c], q_recv.at[z, c])

    def project_guest(r, c):
        b = (away + r) * nblk + c
        arrived(xin.at[r, band(c)], x_recv.at[r, c])
        for k in (1, 2):
            val = product(k, r, c, two)
            for m in range(2):
                kv_out[2 * m + r, c, k - 1] = val[:, m * wide : (m + 1) * wide]
        guest_copy(kv_copy, r, c).start()
        local(kv_out.at[2 * core + r, c], kv_in.at[b], kv_recv.at[away + r, c])
        val = product(0, r, c, two)
        for m in range(2):
            q_out[2 * m + r, c] = val[:, m * wide : (m + 1) * wide]
        guest_copy(q_copy, r, c).start()
        local(q_out.at[2 * core + r, c], q_in.at[b], q_recv.at[away + r, c])

    def w_wait(part):
        for k in (1, 2, 0):
            w_copy(k, part).wait()

    order = [(1 - side, c) for c in range(nblk)] + [(side, c) for c in range(nblk)]
    ahead = 5

    @pl.when(guest)
    def _():
        for r, c in order[:ahead]:
            relay(r, c)

    for r in range(ctx_count):
        arrived(meta_in.at[r], meta_recv.at[r])
    meta_local = pltpu.make_async_copy(meta_in, meta_s, meta_sem)
    meta_local.start()
    meta_local.wait()

    bounds = []
    total = 0
    for p in range(pairs):
        total = total + meta_s[0, rand + 1, p]
        bounds.append(total)

    def segments(pos):
        seg = jnp.zeros(pos.shape, i32)
        for bound in bounds:
            seg = seg + jnp.where(pos >= bound, 1, 0)
        return seg

    def spos(i):
        return meta_s[0, rand, i]

    row_1 = lax.broadcasted_iota(i32, (BLOCK, 1), 0)
    lane_1 = lax.broadcasted_iota(i32, (1, BLOCK), 1)

    def mask_block(b, carry):
        r, c = b // nblk, lax.rem(b, nblk)
        seg_q = segments(b * BLOCK + row_1)
        for j in range(3 + rand):
            if j < 3:
                pos = (b + j - 1) * BLOCK + lane_1
                seg = jnp.where((pos >= 0) & (pos < seq), segments(pos), -1)
            else:
                seg = segments(meta_s[r, j - 3, c] * BLOCK + lane_1)
            bias[b, :, j * BLOCK : (j + 1) * BLOCK] = jnp.where(seg_q == seg, 0.0, MASKED)
        return carry

    def masks():
        lax.fori_loop(0, blocks, mask_block, 0)
        key_pos = lax.broadcasted_iota(i32, (1, seq), 1)
        row_all = lax.broadcasted_iota(i32, (ctx_count * srows, 1), 0)
        bits = jnp.zeros((ctx_count * srows, 1), i32)
        places = jnp.zeros((ctx_count * srows, 1), i32)
        for u in range(ctx_count * per):
            word = 0
            for j in range(listed):
                word = word | (1 << meta_s[0, 8 + j, u])
            for g in range(group):
                here = row_all == u // per * srows + g * per + u % per
                bits = jnp.where(here, word, bits)
                places = jnp.where(here, spos(u), places)
        hit = lax.shift_right_logical(
            jnp.broadcast_to(bits, s_ok.shape), jnp.broadcast_to(key_pos // BLOCK, s_ok.shape)
        )
        s_ok[...] = jnp.where(segments(places) == segments(key_pos), hit & 1, 0)

    masks()

    @pl.when(home)
    def _():
        w_wait(False)
        for c in range(nblk):
            project_home(c)

    @pl.when(guest)
    def _():
        w_wait(True)
        for i in range(len(order)):
            project_guest(*order[i])
            if i + ahead < len(order):
                relay(*order[i + ahead])
            if i + ahead == len(order) - 1:
                @pl.when(gate)
                def _():
                    for r, c in order[:-2]:
                        fwd_copy(r, c).wait_send()
                    pl.semaphore_signal(
                        go_sem, inc=1, device_id={"dp": 1 - core},
                        device_id_type=pl.DeviceIdType.MESH,
                    )

    row8 = lax.broadcasted_iota(i32, (srows, BLOCK), 0)
    col8 = lax.broadcasted_iota(i32, (srows, BLOCK), 1)

    def pick_rows(slot, r):
        wanted = jnp.zeros((srows, BLOCK), i32)
        for i in range(srows):
            wanted = jnp.where(row8 == i, spos(r * per + i % per), wanted)
        found = jnp.zeros((srows, wide), f32)
        for c in range(nblk):
            pick = (wanted == (r * nblk + c) * BLOCK + col8).astype(f32).astype(bf16)
            found = found + jnp.dot(pick, q_out[slot, c], preferred_element_type=f32)
        sq_out[slot] = found

    @pl.when(home)
    def _():
        for m in range(4):
            pick_rows(m, z)
        for d in (1, 2, 0):
            home_copy(sq_copy, d).start()
        local(sq_out.at[mate], sq_in.at[z], sq_recv.at[z])

    @pl.when(guest)
    def _():
        for r in range(2):
            for m in range(2):
                pick_rows(2 * m + r, away + r)
            guest_copy(sq_copy, r).start()
            local(sq_out.at[2 * core + r], sq_in.at[away + r], sq_recv.at[away + r])

    def range_wait(r):
        for c in range(nblk):
            arrived(kv_in.at[r * nblk + c], kv_recv.at[r, c])

    def to_sibling(copy):
        for c in range(nblk):
            for d in (1, 2):
                home_copy(copy, d, c).start()

    @pl.when(home)
    def _():
        @pl.when(gate)
        def _():
            pl.semaphore_wait(go_sem, 1)
            to_sibling(kv_copy)

        to_sibling(q_copy)

    range_wait(away + 1 - side)
    range_wait(z)
    range_wait(away + side)
    range_wait(sib)
    for r in range(ctx_count):
        arrived(sq_in.at[r], sq_recv.at[r])

    factor = HEAD ** (-0.5)
    nt = (((1,), (1,)), ((), ()))

    def softmax(scores, ok):
        scores = jnp.where(ok, scores * factor, MASKED)
        top = jnp.max(scores, axis=1, keepdims=True)
        weights = jnp.exp(scores - top)
        return weights, jnp.sum(weights, axis=1, keepdims=True)

    lane_head = lax.broadcasted_iota(i32, (ctx_count * srows, wide), 1) // HEAD
    row_head = lax.rem(lax.broadcasted_iota(i32, (ctx_count * srows, wide), 0), srows) // per
    sq = sq_in[...].reshape(ctx_count * srows, wide)
    sq = jnp.where(lane_head == row_head, sq, 0.0).astype(bf16)
    all_k = kv_in[:, 0].reshape(seq, wide)
    scores = lax.dot_general(sq, all_k, nt, preferred_element_type=f32)
    weights, totals = softmax(scores, s_ok[...] > 0)
    all_v = kv_in[:, 1].reshape(seq, wide)
    mixed = jnp.dot(weights.astype(bf16), all_v, preferred_element_type=f32) / totals
    s_res[...] = mixed.reshape(ctx_count, srows, wide)

    lane_q = lax.broadcasted_iota(i32, (BLOCK, wide), 1) // HEAD
    row_q = lax.broadcasted_iota(i32, (BLOCK, wide), 0)
    ones = jnp.ones(((3 + rand) * BLOCK, wide), bf16)

    def attend_block(r, c):
        b = r * nblk + c
        q = q_in[b]
        keys, values = [], []
        for shift in (-1, 0, 1):
            at = jnp.clip(b + shift, 0, blocks - 1)
            keys.append(kv_in[at, 0])
            values.append(kv_in[at, 1])
        for j in range(rand):
            at = meta_s[r, j, c]
            keys.append(kv_in[at, 0])
            values.append(kv_in[at, 1])
        keys = jnp.concatenate(keys, axis=0)
        values = jnp.concatenate([jnp.concatenate(values, axis=0), ones], axis=1)
        out = jnp.zeros((BLOCK, wide), f32)
        for g in range(group):
            qg = jnp.where(lane_q == g, q, jnp.zeros_like(q))
            scores = lax.dot_general(qg, keys, nt, preferred_element_type=f32) + bias[b]
            top = jnp.max(scores, axis=1, keepdims=True)
            weights = jnp.exp2((scores - top) * (factor * LOG2E))
            mix = jnp.dot(weights.astype(bf16), values, preferred_element_type=f32)
            out = jnp.where(lane_q == g, mix[:, :wide] / mix[:, wide:], out)
        res = s_res[r]
        for u in range(per):
            row = res[u : u + 1, :]
            for g in range(1, group):
                row = jnp.where(
                    lane_q[:1] == g, res[g * per + u : g * per + u + 1, :], row
                )
            out = jnp.where(row_q == spos(r * per + u) - b * BLOCK, row, out)
        o_out[b] = out.astype(bf16)

    def attend_step(far, c):
        base = 2 * (1 - side) if far else 2 * side
        for i in range(2):
            arrived(q_in.at[(base + i) * nblk + c], q_recv.at[base + i, c])

        def step(i, carry):
            attend_block(base + i, c)
            return carry

        lax.fori_loop(0, 2, step, 0, unroll=2)
        for i in (0, 1) if far else (2, 3):
            if far:
                o_copy(i, c).start()
            else:
                itself = home & (owner(i) == z)

                @pl.when(itself)
                def _():
                    o_local(i, c).start()

                @pl.when(jnp.logical_not(itself))
                def _():
                    o_copy(i, c).start()

    def output(c):
        for m in range(4):
            arrived(o_in.at[c, :, lanes(m, wide)], o_recv.at[m, c])
        att = o_in[c]
        rs_out[c] = jnp.dot(att, wo[:, lanes(other, cols)], preferred_element_type=f32).astype(bf16)
        rs_copy(c).start()
        term = jnp.dot(att, wo[:, lanes(half, cols)], preferred_element_type=f32).astype(bf16)
        hidden[band(c), :] = term.astype(f32)

    lane_s = lax.broadcasted_iota(i32, (BLOCK, BLOCK), 1)

    def finish(c):
        arrived(rs_in.at[c], rs_sem.at[1, c])
        hid = tok[band(c), :].astype(f32) + (hidden[band(c), :] + rs_in[c].astype(f32))
        hidden[band(c), :] = hid
        first = jnp.sum(hid, axis=1, keepdims=True)
        second = jnp.sum(hid * hid, axis=1, keepdims=True)
        both = jnp.where(lane_s == 0, first, jnp.where(lane_s == 1, second, 0.0))
        st_out[c] = jnp.transpose(both)[:8]
        st_copy(c).start()

    full = 2 * cols

    def norm(c):
        arrived(st_in.at[c], st_sem.at[1, c])
        sums = jnp.transpose(st_out[c] + st_in[c])
        mean = sums[:, 0:1] / full
        var = sums[:, 1:2] / full - mean * mean
        hid = hidden[band(c), :]
        res = (hid - mean) * lax.rsqrt(var + 1e-05) * gain_ref[...] + bias_ref[...]
        out_ref[band(c), :] = res.astype(bf16)

    wo_copy.wait()
    tok_copy.wait()

    def only(cond, *steps):
        @pl.when(cond)
        def _():
            for do, c in steps:
                do(c)

    rim = jnp.logical_not(gate)
    done_home, done_guest = 0, 0
    for c in range(nblk):
        attend_step(True, c)
        if 1 <= c < nblk - 1:
            only(home & rim, (output, done_home))
            done_home += 1
        attend_step(False, c)
        if 2 <= c < nblk - 1:
            only(guest & rim, (output, done_guest))
            done_guest += 1

    def rest(first, lead):
        steps = [(output, c) for c in range(first, min(nblk, first + lead))]
        for c in range(nblk):
            steps.append((finish, c))
            if first + lead + c < nblk:
                steps.append((output, first + lead + c))
        return steps + [(norm, c) for c in range(nblk)]

    only(home & rim, *rest(done_home, nblk))
    only(guest & rim, *rest(done_guest, 1))
    only(home & gate, *rest(0, nblk))
    only(guest & gate, *rest(0, 2))

    for m in range(4):
        @pl.when(jnp.logical_not(home & (mate == m)))
        def _():
            meta_copy(m).wait_send()

    @pl.when(home)
    def _():
        for c in range(nblk):
            x_copy(tok_hbm.at[band(c)], 0, c).wait_send()
            for d in range(3):
                home_copy(kv_copy, d, c).wait_send()
                home_copy(q_copy, d, c).wait_send()
        for d in range(3):
            home_copy(sq_copy, d).wait_send()

    @pl.when(guest)
    def _():
        for c in range(nblk):
            far_copy(c).wait_send()
            for r in range(2):
                x_copy(own.at[r, band(c)], r, c).wait_send()
                guest_copy(kv_copy, r, c).wait_send()
                guest_copy(q_copy, r, c).wait_send()
        for r in range(2):
            guest_copy(sq_copy, r).wait_send()

        @pl.when(gate)
        def _():
            for r, c in order[-2:]:
                fwd_copy(r, c).wait_send()

    for c in range(nblk):
        rs_copy(c).wait_send()
        st_copy(c).wait_send()
        for i in range(4):
            if i < 2:
                o_copy(i, c).wait_send()
            else:
                @pl.when(jnp.logical_not(home & (owner(i) == z)))
                def _():
                    o_copy(i, c).wait_send()


def fast_shards(
    tokens, w_qkv, w_out, ln_gain, ln_bias, random_blocks, summary_pos, summary_blocks, pair_lengths
):
    ctx_count = lax.axis_size("ctx")
    rows, cols = tokens.shape[1:]
    nblk = rows // BLOCK
    wide = cols // ctx_count
    group = wide // HEAD
    blocks = nblk * ctx_count
    summaries = summary_pos.shape[1]
    per = summaries // ctx_count
    srows = per * group
    rand = random_blocks.shape[2]
    vmem = pl.BlockSpec(memory_space=pltpu.VMEM)
    hbm = pl.BlockSpec(memory_space=pl.ANY)
    bf16, f32, i32 = jnp.bfloat16, jnp.float32, jnp.int32
    dma = pltpu.SemaphoreType.DMA
    out = pl.pallas_call(
        functools.partial(fast_kernel, ctx_count, rand),
        out_shape=jax.ShapeDtypeStruct((rows, cols), bf16),
        in_specs=[hbm, hbm, hbm, vmem, vmem, vmem, vmem, vmem, vmem],
        out_specs=vmem,
        scratch_shapes=[
            pltpu.VMEM((3, 2 * cols, cols), bf16),
            pltpu.VMEM(w_out.shape, bf16),
            pltpu.VMEM((rows, cols), bf16),
            pltpu.VMEM((2, rows, cols), bf16),
            pltpu.VMEM((2, rows, cols), bf16),
            pltpu.VMEM((blocks, BLOCK, (3 + rand) * BLOCK), f32),
            pltpu.VMEM((4, nblk, 2, BLOCK, wide), bf16),
            pltpu.VMEM((blocks, 2, BLOCK, wide), bf16),
            pltpu.VMEM((4, nblk, BLOCK, wide), bf16),
            pltpu.VMEM((blocks, BLOCK, wide), bf16),
            pltpu.VMEM((4, srows, wide), f32),
            pltpu.VMEM((ctx_count, srows, wide), f32),
            pltpu.VMEM((ctx_count * srows, blocks * BLOCK), i32),
            pltpu.VMEM((ctx_count, srows, wide), f32),
            pltpu.VMEM((16, 128), i32),
            pltpu.VMEM((ctx_count, 16, 128), i32),
            pltpu.SMEM((ctx_count, 16, 128), i32),
            pltpu.VMEM((blocks, BLOCK, wide), bf16),
            pltpu.VMEM((nblk, BLOCK, cols), bf16),
            pltpu.VMEM((nblk, BLOCK, cols), bf16),
            pltpu.VMEM((nblk, BLOCK, cols), bf16),
            pltpu.VMEM((rows, cols), f32),
            pltpu.VMEM((nblk, 8, BLOCK), f32),
            pltpu.VMEM((nblk, 8, BLOCK), f32),
            dma((4,)),
            dma,
            dma((nblk,)),
            dma((2, nblk)),
            dma((2, nblk)),
            dma((2, nblk)),
            dma((2, nblk)),
            dma((4,)),
            dma((ctx_count,)),
            dma,
            dma((4, nblk)),
            dma((ctx_count, nblk)),
            dma((4, nblk)),
            dma((ctx_count, nblk)),
            dma((4,)),
            dma((ctx_count,)),
            dma((4, nblk)),
            dma((4, nblk)),
            dma((2, nblk)),
            dma((2, nblk)),
            pltpu.SemaphoreType.REGULAR,
        ],
        compiler_params=pltpu.CompilerParams(
            collective_id=0, has_side_effects=True, vmem_limit_bytes=60000 * 1024
        ),
    )(
        tokens[0], w_qkv, w_out, ln_gain[None], ln_bias[None],
        random_blocks.transpose(2, 0, 1), pair_lengths, summary_pos,
        summary_blocks.transpose(0, 2, 1),
    )
    return out[None]


def solution(mesh):
    in_specs = (
        P(("groups", "dp"), "ctx", "heads"),
        P(None, None, "heads"),
        P("heads", None),
        P("heads"),
        P("heads"),
        P(("groups", "dp"), "ctx", None),
        P(("groups", "dp"), None),
        P(("groups", "dp"), None, None),
        P(("groups", "dp"), None),
    )
    out_specs = P(("groups", "dp"), "ctx", "heads")
    ctx_count = mesh.shape["ctx"]

    def body(*args):
        rows, cols = args[0].shape[1:]
        wide = cols // ctx_count
        by_heads = (
            ctx_count == 4
            and mesh.shape["heads"] == 2
            and mesh.shape["dp"] == 2
            and wide > 0
            and wide % 128 == 0
            and wide * ctx_count == cols
            and rows // BLOCK <= 128
            and rows // BLOCK * ctx_count <= 32
            and args[6].shape[1] // ctx_count * (wide // HEAD) % 8 == 0
            and rows // BLOCK >= 2
            and args[5].shape[2] <= 6
            and args[7].shape[2] <= 8
            and max(rows // BLOCK, args[6].shape[1], args[8].shape[1]) <= 128
        )
        return (fast_shards if by_heads else shards)(*args)

    return jax.shard_map(body, mesh=mesh, in_specs=in_specs, out_specs=out_specs, check_vma=False)
```

```python
import functools

import jax
import jax.numpy as jnp
from jax import lax
from jax.experimental import pallas as pl
from jax.experimental.pallas import tpu as pltpu
from jax.sharding import PartitionSpec as P

HEAD = 64
BLOCK = 128


MASKED = -1e30
LOG2E = 1.4426950408889634


def extended(x, sides, width):
    for axis, dim in sides:
        size, length = (lax.axis_size(axis), x.shape[dim])
        up = [(i, (i + 1) % size) for i in range(size - 1)]
        down = [(j, i) for i, j in up]
        last = lax.slice_in_dim(x, length - width, length, axis=dim)
        first = lax.slice_in_dim(x, 0, width, axis=dim)
        before = lax.ppermute(last, axis, up)
        after = lax.ppermute(first, axis, down)
        x = jnp.concatenate([before, x, after], axis=dim)
    return x


def segment_ids(positions, bounds):
    return jnp.sum((positions[..., None] >= bounds).astype(jnp.int32), axis=-1)


def attend(queries, keys, values, allowed, head_count):
    group_count, query_len, all_width = queries.shape
    key_len = keys.shape[1]
    query_heads = queries.reshape(group_count, query_len, head_count, HEAD)
    key_heads = keys.reshape(group_count, key_len, head_count, HEAD)
    value_heads = values.reshape(group_count, key_len, head_count, HEAD)
    scores = jnp.einsum(
        "gqhe,gkhe->ghqk", query_heads, key_heads, preferred_element_type=jnp.float32
    ) * HEAD ** (-0.5)
    scores = jnp.where(allowed[:, None], scores, MASKED)
    maxima = jnp.max(scores, axis=-1, keepdims=True)
    weights = jnp.where(allowed[:, None], jnp.exp(scores - maxima), 0.0)
    totals = jnp.sum(weights, axis=-1)
    mixture = jnp.einsum(
        "ghqk,gkhe->gqhe",
        weights.astype(jnp.bfloat16),
        value_heads,
        preferred_element_type=jnp.float32,
    )
    mixture = mixture / jnp.transpose(totals, (0, 2, 1))[..., None]
    return mixture.reshape(group_count, query_len, all_width).astype(jnp.bfloat16)


def three_views(window_span, group_size, axis_pos):
    views = []
    for shift_index in range(3):
        piece = lax.slice_in_dim(
            window_span,
            shift_index * BLOCK,
            shift_index * BLOCK + group_size * BLOCK,
            axis=axis_pos,
        )
        new_shape = (
            window_span.shape[:axis_pos] + (group_size, BLOCK) + window_span.shape[axis_pos + 1 :]
        )
        views.append(piece.reshape(new_shape))
    return jnp.concatenate(views, axis=axis_pos + 1)


def shards(
    tokens, w_qkv, w_out, ln_gain, ln_bias, random_blocks, summary_pos, summary_blocks, pair_lengths
):
    tok_rows = tokens.shape[1]
    head_cols = tokens.shape[2]
    heads_here = head_cols // HEAD
    full_width = w_out.shape[1]
    ctx_count = lax.axis_size("ctx")
    ctx_index = lax.axis_index("ctx")
    block_count = tok_rows // BLOCK
    seq_total = tok_rows * ctx_count
    bounds = jnp.cumsum(pair_lengths[0])
    own_tokens = tokens[0]
    projected = jnp.einsum(
        "nc,kcd->knd",
        lax.all_gather(own_tokens, "heads", axis=1, tiled=True),
        w_qkv,
        preferred_element_type=jnp.float32,
    ).astype(jnp.bfloat16)
    queries = projected[0]
    own_kv = projected[1:3]
    rim_kv = extended(own_kv, (("ctx", 1),), BLOCK)
    query_pos = ctx_index * tok_rows + jnp.arange(tok_rows, dtype=jnp.int32)
    own_seg = segment_ids(query_pos, bounds)
    rim_pos = ctx_index * tok_rows - BLOCK + jnp.arange(tok_rows + 2 * BLOCK, dtype=jnp.int32)
    rim_ok = (rim_pos >= 0) & (rim_pos < seq_total)
    rim_seg = segment_ids(rim_pos, bounds)
    rand_count = random_blocks.shape[2]
    picked = random_blocks[0].reshape(-1)
    pick_count = picked.shape[0]
    capacity = max(2, -(-pick_count // ctx_count))
    owners = picked // block_count
    within = picked % block_count
    slot_order = jnp.arange(pick_count, dtype=jnp.int32)
    earlier = (owners[:, None] == owners[None, :]) & (slot_order[None, :] < slot_order[:, None])
    pick_rank = jnp.sum(earlier.astype(jnp.int32), axis=1)
    pick_slot = owners * capacity + pick_rank
    slot_table = (
        pick_slot[:, None] == jnp.arange(ctx_count * capacity, dtype=jnp.int32)[None, :]
    ).astype(jnp.int32)
    requests = jnp.sum(slot_table * within[:, None], axis=0).reshape(ctx_count, capacity)
    own_blocks = own_kv.reshape(2, block_count, BLOCK, head_cols).transpose(1, 0, 2, 3)
    reply = jnp.take(
        own_blocks, lax.all_to_all(requests, "ctx", split_axis=0, concat_axis=0, tiled=True), axis=0
    )
    fetched = lax.all_to_all(reply, "ctx", split_axis=0, concat_axis=0, tiled=True)
    flat_blocks = fetched.reshape(ctx_count * capacity, 2, BLOCK, head_cols)
    far_kv = jnp.take(flat_blocks, pick_slot, axis=0).reshape(
        block_count, rand_count, 2, BLOCK, head_cols
    )
    far_kv = far_kv.transpose(2, 0, 1, 3, 4).reshape(2, block_count, rand_count * BLOCK, head_cols)
    far_pos = (
        picked.reshape(block_count, rand_count)[:, :, None] * BLOCK
        + jnp.arange(BLOCK, dtype=jnp.int32)
    ).reshape(block_count, rand_count * BLOCK)
    far_seg = segment_ids(far_pos, bounds)
    group_size = min(4, block_count)
    group_steps = block_count // group_size

    def window_step(unused, step_index):
        near_kv = three_views(rim_kv, group_size, 1)
        near_ok = three_views(rim_ok, group_size, 0)
        near_seg = three_views(rim_seg, group_size, 0)
        key_set = jnp.concatenate([near_kv, far_kv], axis=2)
        key_seg = jnp.concatenate([near_seg, far_seg], axis=1)
        key_ok = jnp.concatenate([near_ok, jnp.ones(far_seg.shape, jnp.bool_)], axis=1)
        query_seg = own_seg.reshape(group_size, BLOCK)
        allowed = key_ok[:, None, :] & (key_seg[:, None, :] == query_seg[:, :, None])
        query_group = queries.reshape(group_size, BLOCK, head_cols)
        return (unused, attend(query_group, key_set[0], key_set[1], allowed, heads_here))

    _, window_out = lax.scan(window_step, 0, jnp.arange(group_steps, dtype=jnp.int32))
    attention = window_out.reshape(tok_rows, head_cols)
    summary_rows = summary_pos[0]
    summary_lists = summary_blocks[0]
    summaries = summary_rows.shape[0]
    per_device = summaries // ctx_count
    mine = (
        lax.dynamic_slice_in_dim(summary_rows, ctx_index * per_device, per_device, 0)
        - ctx_index * tok_rows
    )
    summary_query = jnp.take(queries, mine, axis=0)
    all_queries = lax.all_gather(summary_query, "ctx", axis=0, tiled=True)
    summary_seg = segment_ids(summary_rows, bounds)
    key_block = ctx_index * block_count + jnp.arange(block_count, dtype=jnp.int32)
    listed = jnp.any(summary_lists[:, :, None] == key_block[None, None, :], axis=1)
    key_heads = own_kv[0].reshape(tok_rows, heads_here, HEAD)
    value_heads = own_kv[1].reshape(tok_rows, heads_here, HEAD)
    summary_group = min(128, summaries)
    group_total = summaries // summary_group

    def group_scores():
        query_part = all_queries.reshape(summary_group, heads_here, HEAD)
        allowed = jnp.broadcast_to(listed[:, :, None], (summary_group, block_count, BLOCK)).reshape(
            summary_group, tok_rows
        )
        allowed = allowed & (own_seg[None, :] == summary_seg[:, None])
        scores = jnp.einsum(
            "qhe,khe->hqk", query_part, key_heads, preferred_element_type=jnp.float32
        ) * HEAD ** (-0.5)
        return (jnp.where(allowed[None], scores, MASKED), allowed)

    def weigh(scores, allowed, maxima):
        weights = jnp.where(allowed[None], jnp.exp(scores - maxima[:, :, None]), 0.0)
        totals = jnp.sum(weights, axis=-1)
        mixture = jnp.einsum(
            "hqk,khe->qhe",
            weights.astype(jnp.bfloat16),
            value_heads,
            preferred_element_type=jnp.float32,
        )
        return (totals.T, mixture.reshape(summary_group, head_cols))

    def max_step(unused, group_index):
        scores, allowed = group_scores()
        return (unused, jnp.max(scores, axis=-1).T)

    _, maxima_all = lax.scan(max_step, 0, jnp.arange(group_total, dtype=jnp.int32))
    maxima_all = lax.pmax(maxima_all.reshape(summaries, heads_here), "ctx")

    def sum_step(unused, group_index):
        scores, allowed = group_scores()
        maxima = maxima_all.T
        return (unused, weigh(scores, allowed, maxima))

    _, (totals_all, mixture_all) = lax.scan(sum_step, 0, jnp.arange(group_total, dtype=jnp.int32))
    totals_all = totals_all.reshape(summaries, heads_here)
    mixture_all = mixture_all.reshape(summaries, head_cols)
    totals_all, mixture_all = (
        lax.psum(totals_all.astype(jnp.bfloat16), "ctx").astype(jnp.float32),
        lax.psum(mixture_all.astype(jnp.bfloat16), "ctx").astype(jnp.float32),
    )
    own_totals = lax.dynamic_slice_in_dim(totals_all, ctx_index * per_device, per_device, 0)
    own_mixture = lax.dynamic_slice_in_dim(mixture_all, ctx_index * per_device, per_device, 0)
    summary_out = (own_mixture / jnp.repeat(own_totals, HEAD, axis=1)).astype(jnp.bfloat16)
    attention = attention.at[mine].set(summary_out)
    partial_value = jnp.dot(attention, w_out, preferred_element_type=jnp.float32)
    summed = lax.psum_scatter(
        partial_value.astype(jnp.bfloat16), "heads", scatter_dimension=1, tiled=True
    ).astype(jnp.float32)
    hidden = own_tokens.astype(jnp.float32) + summed
    row_sums = lax.psum((jnp.sum(hidden, axis=1), jnp.sum(hidden * hidden, axis=1)), "heads")
    row_mean = row_sums[0] / full_width
    row_var = row_sums[1] / full_width - row_mean * row_mean
    normed = (hidden - row_mean[:, None]) * lax.rsqrt(row_var + 1e-05)[:, None] * ln_gain + ln_bias
    return normed.astype(jnp.bfloat16)[None]


def fast_kernel(
    ctx_count, rand, tok_hbm, wq_hbm, wo_hbm, gain_ref, bias_ref, rb_ref, pair_ref, spos_ref,
    slist_ref, out_ref, wq, wo, tok, own, xin, bias, kv_out, kv_in, q_out, q_in, sq_out,
    sq_in, s_ok, s_res, meta_out, meta_in, meta_s, o_out, o_in, rs_out, rs_in, hidden, st_out,
    st_in, w_sem, tok_sem, far_send, own_recv, fwd_send, x_send, x_recv, meta_send, meta_recv, meta_sem, kv_send, kv_recv,
    q_send, q_recv, sq_send, sq_recv, o_send, o_recv, rs_sem, st_sem,
    go_sem,
):
    z = lax.axis_index("ctx")
    half = lax.axis_index("heads")
    core = lax.axis_index("dp")
    other = 1 - half
    rows, cols = tok_hbm.shape
    nblk = rows // BLOCK
    wide = kv_in.shape[3]
    group = wide // HEAD
    blocks = ctx_count * nblk
    seq = blocks * BLOCK
    pairs = pair_ref.shape[1]
    listed = slist_ref.shape[1]
    per = spos_ref.shape[1] // ctx_count
    srows = per * group
    side = z // 2
    place = lax.rem(z, 2)
    sib = z + 1 - 2 * place
    home = core == side
    guest = core != side
    gate = z == 1 + side
    mate = 2 * place + core
    away = 2 * (1 - side)
    f32, bf16, i32 = jnp.float32, jnp.bfloat16, jnp.int32
    mates = [(z, 1 - core), (sib, core), (sib, 1 - core)]

    def remote(src, dst, send, recv, to):
        return pltpu.make_async_remote_copy(
            src_ref=src, dst_ref=dst, send_sem=send, recv_sem=recv,
            device_id=to, device_id_type=pl.DeviceIdType.MESH,
        )

    def arrived(dst, sem):
        pltpu.make_async_copy(dst, dst, sem).wait()

    def at_mate(d):
        return {"ctx": mates[d][0], "dp": mates[d][1]}

    def mate_index(d):
        return 2 * lax.rem(mates[d][0], 2) + mates[d][1]

    def band(c):
        return pl.ds(pl.multiple_of(c * BLOCK, BLOCK), BLOCK)

    def lanes(i, size):
        return pl.ds(pl.multiple_of(i * size, size), size)

    def own_local(c):
        return pltpu.make_async_copy(
            tok_hbm.at[band(c)], own.at[0, band(c)], own_recv.at[0, c]
        )

    def far_copy(c):
        return remote(
            tok_hbm.at[band(c)], own.at[place, band(c)], far_send.at[c], own_recv.at[place, c],
            {"ctx": 2 - side, "dp": 1 - core},
        )

    def fwd_copy(r, c):
        return remote(
            own.at[r, band(c)], own.at[r, band(c)], fwd_send.at[r, c], own_recv.at[r, c],
            {"ctx": sib},
        )

    def x_copy(src, r, c):
        return remote(
            src, xin.at[r, band(c)], x_send.at[r, c], x_recv.at[r, c], {"heads": other}
        )

    def meta_copy(m):
        return remote(
            meta_out, meta_in.at[z], meta_send.at[m], meta_recv.at[z],
            {"ctx": 2 * core + m // 2, "dp": m % 2},
        )

    def kv_copy(m, d, slot, r, c):
        return remote(
            kv_out.at[slot, c], kv_in.at[r * nblk + c], kv_send.at[d, c], kv_recv.at[r, c],
            at_mate(m),
        )

    def q_copy(m, d, slot, r, c):
        return remote(
            q_out.at[slot, c], q_in.at[r * nblk + c], q_send.at[d, c], q_recv.at[r, c],
            at_mate(m),
        )

    def sq_copy(m, d, slot, r):
        return remote(
            sq_out.at[slot], sq_in.at[r], sq_send.at[d], sq_recv.at[r],
            at_mate(m),
        )

    def home_copy(copy, d, *c):
        return copy(d, d, mate_index(d), z, *c)

    def guest_copy(copy, r, *c):
        return copy(0, 3 * r, 2 * (1 - core) + r, away + r, *c)

    def local(out, into, sem):
        pltpu.make_async_copy(out, into, sem).start()

    def owner(i):
        return 2 * (1 - side) + i if i < 2 else 2 * side + i - 2

    def o_copy(i, c):
        r = owner(i)
        return remote(
            o_out.at[r * nblk + c], o_in.at[c, :, lanes(mate, wide)], o_send.at[i, c],
            o_recv.at[mate, c], {"ctx": r, "dp": side},
        )

    def o_local(i, c):
        return pltpu.make_async_copy(
            o_out.at[owner(i) * nblk + c], o_in.at[c, :, lanes(mate, wide)], o_recv.at[mate, c]
        )

    def rs_copy(c):
        return remote(rs_out.at[c], rs_in.at[c], rs_sem.at[0, c], rs_sem.at[1, c], {"heads": other})

    def st_copy(c):
        return remote(st_out.at[c], st_in.at[c], st_sem.at[0, c], st_sem.at[1, c], {"heads": other})

    tok_copy = pltpu.make_async_copy(tok_hbm, tok, tok_sem)
    two = 2 * wide

    def w_copy(k, part):
        if part:
            return pltpu.make_async_copy(
                wq_hbm.at[k, :, lanes(place, two)], wq.at[k, :, pl.ds(0, two)], w_sem.at[k]
            )
        return pltpu.make_async_copy(wq_hbm.at[k], wq.at[k], w_sem.at[k])

    wo_copy = pltpu.make_async_copy(wo_hbm, wo, w_sem.at[3])
    barrier = pltpu.get_barrier_semaphore()
    greeted = [{"heads": other}, {"dp": 1 - core}]
    for d in range(1, ctx_count):
        for other_core in range(2):
            greeted.append({"ctx": lax.rem(z + d, ctx_count), "dp": other_core})
    for to in greeted:
        pl.semaphore_signal(barrier, inc=1, device_id=to, device_id_type=pl.DeviceIdType.MESH)

    @pl.when(home)
    def _():
        for c in range(nblk):
            own_local(c).start()
        for k in (1, 2, 0):
            w_copy(k, False).start()

    @pl.when(guest)
    def _():
        for k in (1, 2, 0):
            w_copy(k, True).start()

    tok_copy.start()
    wo_copy.start()
    meta_out[...] = jnp.zeros_like(meta_out)
    for r in range(rand):
        meta_out[r : r + 1, :nblk] = rb_ref[r]
    meta_out[rand : rand + 1, : ctx_count * per] = spos_ref[...]
    meta_out[rand + 1 : rand + 2, :pairs] = pair_ref[...]
    meta_out[8 : 8 + listed, : ctx_count * per] = slist_ref[0]
    pl.semaphore_wait(barrier, len(greeted))

    for m in range(4):
        itself = home & (mate == m)

        @pl.when(itself)
        def _():
            pltpu.make_async_copy(meta_out, meta_in.at[z], meta_recv.at[z]).start()

        @pl.when(jnp.logical_not(itself))
        def _():
            meta_copy(m).start()

    @pl.when(home)
    def _():
        for c in range(nblk):
            x_copy(tok_hbm.at[band(c)], 0, c).start()

    @pl.when(guest)
    def _():
        for c in range(nblk):
            far_copy(c).start()

    def relay(r, c):
        arrived(own.at[r, band(c)], own_recv.at[r, c])

        @pl.when(gate)
        def _():
            fwd_copy(r, c).start()

        x_copy(own.at[r, band(c)], r, c).start()

    def product(k, r, c, width):
        val = jnp.dot(
            own[r, band(c), :], wq[k, lanes(half, cols), :width], preferred_element_type=f32
        )
        val = val + jnp.dot(
            xin[r, band(c), :], wq[k, lanes(other, cols), :width], preferred_element_type=f32
        )
        return val.astype(bf16)

    def project_home(c):
        arrived(own.at[0, band(c)], own_recv.at[0, c])
        arrived(xin.at[0, band(c)], x_recv.at[0, c])
        for k in (1, 2):
            val = product(k, 0, c, cols)
            for m in range(4):
                kv_out[m, c, k - 1] = val[:, m * wide : (m + 1) * wide]
        home_copy(kv_copy, 0, c).start()

        @pl.when(jnp.logical_not(gate))
        def _():
            for d in (1, 2):
                home_copy(kv_copy, d, c).start()

        local(kv_out.at[mate, c], kv_in.at[z * nblk + c], kv_recv.at[z, c])
        val = product(0, 0, c, cols)
        for m in range(4):
            q_out[m, c] = val[:, m * wide : (m + 1) * wide]
        home_copy(q_copy, 0, c).start()
        local(q_out.at[mate, c], q_in.at[z * nblk + c], q_recv.at[z, c])

    def project_guest(r, c):
        b = (away + r) * nblk + c
        arrived(xin.at[r, band(c)], x_recv.at[r, c])
        for k in (1, 2):
            val = product(k, r, c, two)
            for m in range(2):
                kv_out[2 * m + r, c, k - 1] = val[:, m * wide : (m + 1) * wide]
        guest_copy(kv_copy, r, c).start()
        local(kv_out.at[2 * core + r, c], kv_in.at[b], kv_recv.at[away + r, c])
        val = product(0, r, c, two)
        for m in range(2):
            q_out[2 * m + r, c] = val[:, m * wide : (m + 1) * wide]
        guest_copy(q_copy, r, c).start()
        local(q_out.at[2 * core + r, c], q_in.at[b], q_recv.at[away + r, c])

    def w_wait(part):
        for k in (1, 2, 0):
            w_copy(k, part).wait()

    order = [(1 - side, c) for c in range(nblk)] + [(side, c) for c in range(nblk)]
    ahead = 5

    @pl.when(guest)
    def _():
        for r, c in order[:ahead]:
            relay(r, c)

    for r in range(ctx_count):
        arrived(meta_in.at[r], meta_recv.at[r])
    meta_local = pltpu.make_async_copy(meta_in, meta_s, meta_sem)
    meta_local.start()
    meta_local.wait()

    bounds = []
    total = 0
    for p in range(pairs):
        total = total + meta_s[0, rand + 1, p]
        bounds.append(total)

    def segments(pos):
        seg = jnp.zeros(pos.shape, i32)
        for bound in bounds:
            seg = seg + jnp.where(pos >= bound, 1, 0)
        return seg

    def spos(i):
        return meta_s[0, rand, i]

    row_1 = lax.broadcasted_iota(i32, (BLOCK, 1), 0)
    lane_1 = lax.broadcasted_iota(i32, (1, BLOCK), 1)

    def mask_block(b, carry):
        r, c = b // nblk, lax.rem(b, nblk)
        seg_q = segments(b * BLOCK + row_1)
        for j in range(3 + rand):
            if j < 3:
                pos = (b + j - 1) * BLOCK + lane_1
                seg = jnp.where((pos >= 0) & (pos < seq), segments(pos), -1)
            else:
                seg = segments(meta_s[r, j - 3, c] * BLOCK + lane_1)
            bias[b, :, j * BLOCK : (j + 1) * BLOCK] = jnp.where(seg_q == seg, 0.0, MASKED)
        return carry

    def masks():
        lax.fori_loop(0, blocks, mask_block, 0)
        key_pos = lax.broadcasted_iota(i32, (1, seq), 1)
        row_all = lax.broadcasted_iota(i32, (ctx_count * srows, 1), 0)
        bits = jnp.zeros((ctx_count * srows, 1), i32)
        places = jnp.zeros((ctx_count * srows, 1), i32)
        for u in range(ctx_count * per):
            word = 0
            for j in range(listed):
                word = word | (1 << meta_s[0, 8 + j, u])
            for g in range(group):
                here = row_all == u // per * srows + g * per + u % per
                bits = jnp.where(here, word, bits)
                places = jnp.where(here, spos(u), places)
        hit = lax.shift_right_logical(
            jnp.broadcast_to(bits, s_ok.shape), jnp.broadcast_to(key_pos // BLOCK, s_ok.shape)
        )
        s_ok[...] = jnp.where(segments(places) == segments(key_pos), hit & 1, 0)

    masks()

    @pl.when(home)
    def _():
        w_wait(False)
        for c in range(nblk):
            project_home(c)

    @pl.when(guest)
    def _():
        w_wait(True)
        for i in range(len(order)):
            project_guest(*order[i])
            if i + ahead < len(order):
                relay(*order[i + ahead])
            if i + ahead == len(order):
                @pl.when(gate)
                def _():
                    for r, c in order[:-1]:
                        fwd_copy(r, c).wait_send()
                    pl.semaphore_signal(
                        go_sem, inc=1, device_id={"dp": 1 - core},
                        device_id_type=pl.DeviceIdType.MESH,
                    )

    row8 = lax.broadcasted_iota(i32, (srows, BLOCK), 0)
    col8 = lax.broadcasted_iota(i32, (srows, BLOCK), 1)

    def pick_rows(slot, r):
        wanted = jnp.zeros((srows, BLOCK), i32)
        for i in range(srows):
            wanted = jnp.where(row8 == i, spos(r * per + i % per), wanted)
        found = jnp.zeros((srows, wide), f32)
        for c in range(nblk):
            pick = (wanted == (r * nblk + c) * BLOCK + col8).astype(f32).astype(bf16)
            found = found + jnp.dot(pick, q_out[slot, c], preferred_element_type=f32)
        sq_out[slot] = found

    @pl.when(home)
    def _():
        for m in range(4):
            pick_rows(m, z)
        for d in (1, 2, 0):
            home_copy(sq_copy, d).start()
        local(sq_out.at[mate], sq_in.at[z], sq_recv.at[z])

    @pl.when(guest)
    def _():
        for r in range(2):
            for m in range(2):
                pick_rows(2 * m + r, away + r)
            guest_copy(sq_copy, r).start()
            local(sq_out.at[2 * core + r], sq_in.at[away + r], sq_recv.at[away + r])

    def range_wait(r):
        for c in range(nblk):
            arrived(kv_in.at[r * nblk + c], kv_recv.at[r, c])

    def to_sibling(copy):
        for c in range(nblk):
            for d in (1, 2):
                home_copy(copy, d, c).start()

    @pl.when(home)
    def _():
        @pl.when(gate)
        def _():
            pl.semaphore_wait(go_sem, 1)
            to_sibling(kv_copy)

        to_sibling(q_copy)

    range_wait(away + 1 - side)
    range_wait(z)
    range_wait(away + side)
    range_wait(sib)
    for r in range(ctx_count):
        arrived(sq_in.at[r], sq_recv.at[r])

    factor = HEAD ** (-0.5)
    nt = (((1,), (1,)), ((), ()))

    def softmax(scores, ok):
        scores = jnp.where(ok, scores * factor, MASKED)
        top = jnp.max(scores, axis=1, keepdims=True)
        weights = jnp.exp(scores - top)
        return weights, jnp.sum(weights, axis=1, keepdims=True)

    lane_head = lax.broadcasted_iota(i32, (ctx_count * srows, wide), 1) // HEAD
    row_head = lax.rem(lax.broadcasted_iota(i32, (ctx_count * srows, wide), 0), srows) // per
    sq = sq_in[...].reshape(ctx_count * srows, wide)
    sq = jnp.where(lane_head == row_head, sq, 0.0).astype(bf16)
    all_k = kv_in[:, 0].reshape(seq, wide)
    scores = lax.dot_general(sq, all_k, nt, preferred_element_type=f32)
    weights, totals = softmax(scores, s_ok[...] > 0)
    all_v = kv_in[:, 1].reshape(seq, wide)
    mixed = jnp.dot(weights.astype(bf16), all_v, preferred_element_type=f32) / totals
    s_res[...] = mixed.reshape(ctx_count, srows, wide)

    lane_q = lax.broadcasted_iota(i32, (BLOCK, wide), 1) // HEAD
    row_q = lax.broadcasted_iota(i32, (BLOCK, wide), 0)
    ones = jnp.ones(((3 + rand) * BLOCK, wide), bf16)

    def attend_block(r, c):
        b = r * nblk + c
        q = q_in[b]
        keys, values = [], []
        for shift in (-1, 0, 1):
            at = jnp.clip(b + shift, 0, blocks - 1)
            keys.append(kv_in[at, 0])
            values.append(kv_in[at, 1])
        for j in range(rand):
            at = meta_s[r, j, c]
            keys.append(kv_in[at, 0])
            values.append(kv_in[at, 1])
        keys = jnp.concatenate(keys, axis=0)
        values = jnp.concatenate([jnp.concatenate(values, axis=0), ones], axis=1)
        out = jnp.zeros((BLOCK, wide), f32)
        for g in range(group):
            qg = jnp.where(lane_q == g, q, jnp.zeros_like(q))
            scores = lax.dot_general(qg, keys, nt, preferred_element_type=f32) + bias[b]
            top = jnp.max(scores, axis=1, keepdims=True)
            weights = jnp.exp2((scores - top) * (factor * LOG2E))
            mix = jnp.dot(weights.astype(bf16), values, preferred_element_type=f32)
            out = jnp.where(lane_q == g, mix[:, :wide] / mix[:, wide:], out)
        res = s_res[r]
        for u in range(per):
            row = res[u : u + 1, :]
            for g in range(1, group):
                row = jnp.where(
                    lane_q[:1] == g, res[g * per + u : g * per + u + 1, :], row
                )
            out = jnp.where(row_q == spos(r * per + u) - b * BLOCK, row, out)
        o_out[b] = out.astype(bf16)

    def attend_step(far, c):
        base = 2 * (1 - side) if far else 2 * side
        for i in range(2):
            arrived(q_in.at[(base + i) * nblk + c], q_recv.at[base + i, c])

        def step(i, carry):
            attend_block(base + i, c)
            return carry

        lax.fori_loop(0, 2, step, 0, unroll=2)
        for i in (0, 1) if far else (2, 3):
            if far:
                o_copy(i, c).start()
            else:
                itself = home & (owner(i) == z)

                @pl.when(itself)
                def _():
                    o_local(i, c).start()

                @pl.when(jnp.logical_not(itself))
                def _():
                    o_copy(i, c).start()

    def output(c):
        for m in range(4):
            arrived(o_in.at[c, :, lanes(m, wide)], o_recv.at[m, c])
        att = o_in[c]
        rs_out[c] = jnp.dot(att, wo[:, lanes(other, cols)], preferred_element_type=f32).astype(bf16)
        rs_copy(c).start()
        term = jnp.dot(att, wo[:, lanes(half, cols)], preferred_element_type=f32).astype(bf16)
        hidden[band(c), :] = term.astype(f32)

    lane_s = lax.broadcasted_iota(i32, (BLOCK, BLOCK), 1)

    def finish(c):
        arrived(rs_in.at[c], rs_sem.at[1, c])
        hid = tok[band(c), :].astype(f32) + (hidden[band(c), :] + rs_in[c].astype(f32))
        hidden[band(c), :] = hid
        first = jnp.sum(hid, axis=1, keepdims=True)
        second = jnp.sum(hid * hid, axis=1, keepdims=True)
        both = jnp.where(lane_s == 0, first, jnp.where(lane_s == 1, second, 0.0))
        st_out[c] = jnp.transpose(both)[:8]
        st_copy(c).start()

    full = 2 * cols

    def norm(c):
        arrived(st_in.at[c], st_sem.at[1, c])
        sums = jnp.transpose(st_out[c] + st_in[c])
        mean = sums[:, 0:1] / full
        var = sums[:, 1:2] / full - mean * mean
        hid = hidden[band(c), :]
        res = (hid - mean) * lax.rsqrt(var + 1e-05) * gain_ref[...] + bias_ref[...]
        out_ref[band(c), :] = res.astype(bf16)

    wo_copy.wait()
    tok_copy.wait()

    def only(cond, *steps):
        @pl.when(cond)
        def _():
            for do, c in steps:
                do(c)

    rim = jnp.logical_not(gate)
    done_home, done_guest = 0, 0
    for c in range(nblk):
        attend_step(True, c)
        if 1 <= c < nblk - 1:
            only(home & rim, (output, done_home))
            done_home += 1
        attend_step(False, c)
        if 2 <= c < nblk - 1:
            only(guest & rim, (output, done_guest))
            done_guest += 1

    def rest(first, lead):
        steps = [(output, c) for c in range(first, min(nblk, first + lead))]
        for c in range(nblk):
            steps.append((finish, c))
            if first + lead + c < nblk:
                steps.append((output, first + lead + c))
        return steps + [(norm, c) for c in range(nblk)]

    only(home & rim, *rest(done_home, nblk))
    only(guest & rim, *rest(done_guest, 1))
    only(home & gate, *rest(0, nblk))
    only(guest & gate, *rest(0, 2))

    for m in range(4):
        @pl.when(jnp.logical_not(home & (mate == m)))
        def _():
            meta_copy(m).wait_send()

    @pl.when(home)
    def _():
        for c in range(nblk):
            x_copy(tok_hbm.at[band(c)], 0, c).wait_send()
            for d in range(3):
                home_copy(kv_copy, d, c).wait_send()
                home_copy(q_copy, d, c).wait_send()
        for d in range(3):
            home_copy(sq_copy, d).wait_send()

    @pl.when(guest)
    def _():
        for c in range(nblk):
            far_copy(c).wait_send()
            for r in range(2):
                x_copy(own.at[r, band(c)], r, c).wait_send()
                guest_copy(kv_copy, r, c).wait_send()
                guest_copy(q_copy, r, c).wait_send()
        for r in range(2):
            guest_copy(sq_copy, r).wait_send()

        @pl.when(gate)
        def _():
            for r, c in order[-1:]:
                fwd_copy(r, c).wait_send()

    for c in range(nblk):
        rs_copy(c).wait_send()
        st_copy(c).wait_send()
        for i in range(4):
            if i < 2:
                o_copy(i, c).wait_send()
            else:
                @pl.when(jnp.logical_not(home & (owner(i) == z)))
                def _():
                    o_copy(i, c).wait_send()


def store_kernel(src_ref, out_hbm, sem):
    copy = pltpu.make_async_copy(src_ref, out_hbm, sem)
    copy.start()
    copy.wait()


def fast_shards(
    tokens, w_qkv, w_out, ln_gain, ln_bias, random_blocks, summary_pos, summary_blocks, pair_lengths
):
    ctx_count = lax.axis_size("ctx")
    rows, cols = tokens.shape[1:]
    nblk = rows // BLOCK
    wide = cols // ctx_count
    group = wide // HEAD
    blocks = nblk * ctx_count
    summaries = summary_pos.shape[1]
    per = summaries // ctx_count
    srows = per * group
    rand = random_blocks.shape[2]
    vmem = pl.BlockSpec(memory_space=pltpu.VMEM)
    hbm = pl.BlockSpec(memory_space=pl.ANY)
    bf16, f32, i32 = jnp.bfloat16, jnp.float32, jnp.int32
    dma = pltpu.SemaphoreType.DMA
    out = pl.pallas_call(
        functools.partial(fast_kernel, ctx_count, rand),
        out_shape=pltpu.VMEM((rows, cols), bf16),
        in_specs=[hbm, hbm, hbm, vmem, vmem, vmem, vmem, vmem, vmem],
        out_specs=vmem,
        scratch_shapes=[
            pltpu.VMEM((3, 2 * cols, cols), bf16),
            pltpu.VMEM(w_out.shape, bf16),
            pltpu.VMEM((rows, cols), bf16),
            pltpu.VMEM((2, rows, cols), bf16),
            pltpu.VMEM((2, rows, cols), bf16),
            pltpu.VMEM((blocks, BLOCK, (3 + rand) * BLOCK), f32),
            pltpu.VMEM((4, nblk, 2, BLOCK, wide), bf16),
            pltpu.VMEM((blocks, 2, BLOCK, wide), bf16),
            pltpu.VMEM((4, nblk, BLOCK, wide), bf16),
            pltpu.VMEM((blocks, BLOCK, wide), bf16),
            pltpu.VMEM((4, srows, wide), f32),
            pltpu.VMEM((ctx_count, srows, wide), f32),
            pltpu.VMEM((ctx_count * srows, blocks * BLOCK), i32),
            pltpu.VMEM((ctx_count, srows, wide), f32),
            pltpu.VMEM((16, 128), i32),
            pltpu.VMEM((ctx_count, 16, 128), i32),
            pltpu.SMEM((ctx_count, 16, 128), i32),
            pltpu.VMEM((blocks, BLOCK, wide), bf16),
            pltpu.VMEM((nblk, BLOCK, cols), bf16),
            pltpu.VMEM((nblk, BLOCK, cols), bf16),
            pltpu.VMEM((nblk, BLOCK, cols), bf16),
            pltpu.VMEM((rows, cols), f32),
            pltpu.VMEM((nblk, 8, BLOCK), f32),
            pltpu.VMEM((nblk, 8, BLOCK), f32),
            dma((4,)),
            dma,
            dma((nblk,)),
            dma((2, nblk)),
            dma((2, nblk)),
            dma((2, nblk)),
            dma((2, nblk)),
            dma((4,)),
            dma((ctx_count,)),
            dma,
            dma((4, nblk)),
            dma((ctx_count, nblk)),
            dma((4, nblk)),
            dma((ctx_count, nblk)),
            dma((4,)),
            dma((ctx_count,)),
            dma((4, nblk)),
            dma((4, nblk)),
            dma((2, nblk)),
            dma((2, nblk)),
            pltpu.SemaphoreType.REGULAR,
        ],
        compiler_params=pltpu.CompilerParams(
            collective_id=0, has_side_effects=True, vmem_limit_bytes=60000 * 1024
        ),
    )(
        tokens[0], w_qkv, w_out, ln_gain[None], ln_bias[None],
        random_blocks.transpose(2, 0, 1), pair_lengths, summary_pos,
        summary_blocks.transpose(0, 2, 1),
    )
    out = pl.pallas_call(
        store_kernel,
        out_shape=jax.ShapeDtypeStruct((rows, cols), bf16),
        in_specs=[vmem],
        out_specs=hbm,
        scratch_shapes=[dma],
    )(pltpu.with_memory_space_constraint(out, pltpu.VMEM))
    return out[None]


def solution(mesh):
    in_specs = (
        P(("groups", "dp"), "ctx", "heads"),
        P(None, None, "heads"),
        P("heads", None),
        P("heads"),
        P("heads"),
        P(("groups", "dp"), "ctx", None),
        P(("groups", "dp"), None),
        P(("groups", "dp"), None, None),
        P(("groups", "dp"), None),
    )
    out_specs = P(("groups", "dp"), "ctx", "heads")
    ctx_count = mesh.shape["ctx"]

    def body(*args):
        rows, cols = args[0].shape[1:]
        wide = cols // ctx_count
        by_heads = (
            ctx_count == 4
            and mesh.shape["heads"] == 2
            and mesh.shape["dp"] == 2
            and wide > 0
            and wide % 128 == 0
            and wide * ctx_count == cols
            and rows // BLOCK <= 128
            and rows // BLOCK * ctx_count <= 32
            and args[6].shape[1] // ctx_count * (wide // HEAD) % 8 == 0
            and rows // BLOCK >= 2
            and args[5].shape[2] <= 6
            and args[7].shape[2] <= 8
            and max(rows // BLOCK, args[6].shape[1], args[8].shape[1]) <= 128
        )
        return (fast_shards if by_heads else shards)(*args)

    return jax.shard_map(body, mesh=mesh, in_specs=in_specs, out_specs=out_specs, check_vma=False)
```

```python
import functools

import jax
import jax.numpy as jnp
from jax import lax
from jax.experimental import pallas as pl
from jax.experimental.pallas import tpu as pltpu
from jax.sharding import PartitionSpec as P

HEAD = 64
BLOCK = 128


MASKED = -1e30
LOG2E = 1.4426950408889634


def extended(x, sides, width):
    for axis, dim in sides:
        size, length = (lax.axis_size(axis), x.shape[dim])
        up = [(i, (i + 1) % size) for i in range(size - 1)]
        down = [(j, i) for i, j in up]
        last = lax.slice_in_dim(x, length - width, length, axis=dim)
        first = lax.slice_in_dim(x, 0, width, axis=dim)
        before = lax.ppermute(last, axis, up)
        after = lax.ppermute(first, axis, down)
        x = jnp.concatenate([before, x, after], axis=dim)
    return x


def segment_ids(positions, bounds):
    return jnp.sum((positions[..., None] >= bounds).astype(jnp.int32), axis=-1)


def attend(queries, keys, values, allowed, head_count):
    group_count, query_len, all_width = queries.shape
    key_len = keys.shape[1]
    query_heads = queries.reshape(group_count, query_len, head_count, HEAD)
    key_heads = keys.reshape(group_count, key_len, head_count, HEAD)
    value_heads = values.reshape(group_count, key_len, head_count, HEAD)
    scores = jnp.einsum(
        "gqhe,gkhe->ghqk", query_heads, key_heads, preferred_element_type=jnp.float32
    ) * HEAD ** (-0.5)
    scores = jnp.where(allowed[:, None], scores, MASKED)
    maxima = jnp.max(scores, axis=-1, keepdims=True)
    weights = jnp.where(allowed[:, None], jnp.exp(scores - maxima), 0.0)
    totals = jnp.sum(weights, axis=-1)
    mixture = jnp.einsum(
        "ghqk,gkhe->gqhe",
        weights.astype(jnp.bfloat16),
        value_heads,
        preferred_element_type=jnp.float32,
    )
    mixture = mixture / jnp.transpose(totals, (0, 2, 1))[..., None]
    return mixture.reshape(group_count, query_len, all_width).astype(jnp.bfloat16)


def three_views(window_span, group_size, axis_pos):
    views = []
    for shift_index in range(3):
        piece = lax.slice_in_dim(
            window_span,
            shift_index * BLOCK,
            shift_index * BLOCK + group_size * BLOCK,
            axis=axis_pos,
        )
        new_shape = (
            window_span.shape[:axis_pos] + (group_size, BLOCK) + window_span.shape[axis_pos + 1 :]
        )
        views.append(piece.reshape(new_shape))
    return jnp.concatenate(views, axis=axis_pos + 1)


def shards(
    tokens, w_qkv, w_out, ln_gain, ln_bias, random_blocks, summary_pos, summary_blocks, pair_lengths
):
    tok_rows = tokens.shape[1]
    head_cols = tokens.shape[2]
    heads_here = head_cols // HEAD
    full_width = w_out.shape[1]
    ctx_count = lax.axis_size("ctx")
    ctx_index = lax.axis_index("ctx")
    block_count = tok_rows // BLOCK
    seq_total = tok_rows * ctx_count
    bounds = jnp.cumsum(pair_lengths[0])
    own_tokens = tokens[0]
    projected = jnp.einsum(
        "nc,kcd->knd",
        lax.all_gather(own_tokens, "heads", axis=1, tiled=True),
        w_qkv,
        preferred_element_type=jnp.float32,
    ).astype(jnp.bfloat16)
    queries = projected[0]
    own_kv = projected[1:3]
    rim_kv = extended(own_kv, (("ctx", 1),), BLOCK)
    query_pos = ctx_index * tok_rows + jnp.arange(tok_rows, dtype=jnp.int32)
    own_seg = segment_ids(query_pos, bounds)
    rim_pos = ctx_index * tok_rows - BLOCK + jnp.arange(tok_rows + 2 * BLOCK, dtype=jnp.int32)
    rim_ok = (rim_pos >= 0) & (rim_pos < seq_total)
    rim_seg = segment_ids(rim_pos, bounds)
    rand_count = random_blocks.shape[2]
    picked = random_blocks[0].reshape(-1)
    pick_count = picked.shape[0]
    capacity = max(2, -(-pick_count // ctx_count))
    owners = picked // block_count
    within = picked % block_count
    slot_order = jnp.arange(pick_count, dtype=jnp.int32)
    earlier = (owners[:, None] == owners[None, :]) & (slot_order[None, :] < slot_order[:, None])
    pick_rank = jnp.sum(earlier.astype(jnp.int32), axis=1)
    pick_slot = owners * capacity + pick_rank
    slot_table = (
        pick_slot[:, None] == jnp.arange(ctx_count * capacity, dtype=jnp.int32)[None, :]
    ).astype(jnp.int32)
    requests = jnp.sum(slot_table * within[:, None], axis=0).reshape(ctx_count, capacity)
    own_blocks = own_kv.reshape(2, block_count, BLOCK, head_cols).transpose(1, 0, 2, 3)
    reply = jnp.take(
        own_blocks, lax.all_to_all(requests, "ctx", split_axis=0, concat_axis=0, tiled=True), axis=0
    )
    fetched = lax.all_to_all(reply, "ctx", split_axis=0, concat_axis=0, tiled=True)
    flat_blocks = fetched.reshape(ctx_count * capacity, 2, BLOCK, head_cols)
    far_kv = jnp.take(flat_blocks, pick_slot, axis=0).reshape(
        block_count, rand_count, 2, BLOCK, head_cols
    )
    far_kv = far_kv.transpose(2, 0, 1, 3, 4).reshape(2, block_count, rand_count * BLOCK, head_cols)
    far_pos = (
        picked.reshape(block_count, rand_count)[:, :, None] * BLOCK
        + jnp.arange(BLOCK, dtype=jnp.int32)
    ).reshape(block_count, rand_count * BLOCK)
    far_seg = segment_ids(far_pos, bounds)
    group_size = min(4, block_count)
    group_steps = block_count // group_size

    def window_step(unused, step_index):
        near_kv = three_views(rim_kv, group_size, 1)
        near_ok = three_views(rim_ok, group_size, 0)
        near_seg = three_views(rim_seg, group_size, 0)
        key_set = jnp.concatenate([near_kv, far_kv], axis=2)
        key_seg = jnp.concatenate([near_seg, far_seg], axis=1)
        key_ok = jnp.concatenate([near_ok, jnp.ones(far_seg.shape, jnp.bool_)], axis=1)
        query_seg = own_seg.reshape(group_size, BLOCK)
        allowed = key_ok[:, None, :] & (key_seg[:, None, :] == query_seg[:, :, None])
        query_group = queries.reshape(group_size, BLOCK, head_cols)
        return (unused, attend(query_group, key_set[0], key_set[1], allowed, heads_here))

    _, window_out = lax.scan(window_step, 0, jnp.arange(group_steps, dtype=jnp.int32))
    attention = window_out.reshape(tok_rows, head_cols)
    summary_rows = summary_pos[0]
    summary_lists = summary_blocks[0]
    summaries = summary_rows.shape[0]
    per_device = summaries // ctx_count
    mine = (
        lax.dynamic_slice_in_dim(summary_rows, ctx_index * per_device, per_device, 0)
        - ctx_index * tok_rows
    )
    summary_query = jnp.take(queries, mine, axis=0)
    all_queries = lax.all_gather(summary_query, "ctx", axis=0, tiled=True)
    summary_seg = segment_ids(summary_rows, bounds)
    key_block = ctx_index * block_count + jnp.arange(block_count, dtype=jnp.int32)
    listed = jnp.any(summary_lists[:, :, None] == key_block[None, None, :], axis=1)
    key_heads = own_kv[0].reshape(tok_rows, heads_here, HEAD)
    value_heads = own_kv[1].reshape(tok_rows, heads_here, HEAD)
    summary_group = min(128, summaries)
    group_total = summaries // summary_group

    def group_scores():
        query_part = all_queries.reshape(summary_group, heads_here, HEAD)
        allowed = jnp.broadcast_to(listed[:, :, None], (summary_group, block_count, BLOCK)).reshape(
            summary_group, tok_rows
        )
        allowed = allowed & (own_seg[None, :] == summary_seg[:, None])
        scores = jnp.einsum(
            "qhe,khe->hqk", query_part, key_heads, preferred_element_type=jnp.float32
        ) * HEAD ** (-0.5)
        return (jnp.where(allowed[None], scores, MASKED), allowed)

    def weigh(scores, allowed, maxima):
        weights = jnp.where(allowed[None], jnp.exp(scores - maxima[:, :, None]), 0.0)
        totals = jnp.sum(weights, axis=-1)
        mixture = jnp.einsum(
            "hqk,khe->qhe",
            weights.astype(jnp.bfloat16),
            value_heads,
            preferred_element_type=jnp.float32,
        )
        return (totals.T, mixture.reshape(summary_group, head_cols))

    def max_step(unused, group_index):
        scores, allowed = group_scores()
        return (unused, jnp.max(scores, axis=-1).T)

    _, maxima_all = lax.scan(max_step, 0, jnp.arange(group_total, dtype=jnp.int32))
    maxima_all = lax.pmax(maxima_all.reshape(summaries, heads_here), "ctx")

    def sum_step(unused, group_index):
        scores, allowed = group_scores()
        maxima = maxima_all.T
        return (unused, weigh(scores, allowed, maxima))

    _, (totals_all, mixture_all) = lax.scan(sum_step, 0, jnp.arange(group_total, dtype=jnp.int32))
    totals_all = totals_all.reshape(summaries, heads_here)
    mixture_all = mixture_all.reshape(summaries, head_cols)
    totals_all, mixture_all = (
        lax.psum(totals_all.astype(jnp.bfloat16), "ctx").astype(jnp.float32),
        lax.psum(mixture_all.astype(jnp.bfloat16), "ctx").astype(jnp.float32),
    )
    own_totals = lax.dynamic_slice_in_dim(totals_all, ctx_index * per_device, per_device, 0)
    own_mixture = lax.dynamic_slice_in_dim(mixture_all, ctx_index * per_device, per_device, 0)
    summary_out = (own_mixture / jnp.repeat(own_totals, HEAD, axis=1)).astype(jnp.bfloat16)
    attention = attention.at[mine].set(summary_out)
    partial_value = jnp.dot(attention, w_out, preferred_element_type=jnp.float32)
    summed = lax.psum_scatter(
        partial_value.astype(jnp.bfloat16), "heads", scatter_dimension=1, tiled=True
    ).astype(jnp.float32)
    hidden = own_tokens.astype(jnp.float32) + summed
    row_sums = lax.psum((jnp.sum(hidden, axis=1), jnp.sum(hidden * hidden, axis=1)), "heads")
    row_mean = row_sums[0] / full_width
    row_var = row_sums[1] / full_width - row_mean * row_mean
    normed = (hidden - row_mean[:, None]) * lax.rsqrt(row_var + 1e-05)[:, None] * ln_gain + ln_bias
    return normed.astype(jnp.bfloat16)[None]


def fast_kernel(
    ctx_count, rand, tok_hbm, wq_hbm, wo_hbm, gain_ref, bias_ref, rb_ref, pair_ref, spos_ref,
    slist_ref, out_ref, wq, wo, tok, own, xin, bias, kv_out, kv_in, q_out, q_in, sq_out,
    sq_in, s_ok, s_res, meta_out, meta_in, meta_s, o_out, o_in, rs_out, rs_in, hidden, st_out,
    st_in, w_sem, tok_sem, far_send, own_recv, fwd_send, x_send, x_recv, meta_send, meta_recv, meta_sem, kv_send, kv_recv,
    q_send, q_recv, sq_send, sq_recv, o_send, o_recv, rs_sem, st_sem,
    go_sem,
):
    z = lax.axis_index("ctx")
    half = lax.axis_index("heads")
    core = lax.axis_index("dp")
    other = 1 - half
    rows, cols = tok_hbm.shape
    nblk = rows // BLOCK
    wide = kv_in.shape[3]
    group = wide // HEAD
    blocks = ctx_count * nblk
    seq = blocks * BLOCK
    pairs = pair_ref.shape[1]
    listed = slist_ref.shape[1]
    per = spos_ref.shape[1] // ctx_count
    srows = per * group
    side = z // 2
    place = lax.rem(z, 2)
    sib = z + 1 - 2 * place
    home = core == side
    guest = core != side
    gate = z == 1 + side
    mate = 2 * place + core
    away = 2 * (1 - side)
    f32, bf16, i32 = jnp.float32, jnp.bfloat16, jnp.int32
    mates = [(z, 1 - core), (sib, core), (sib, 1 - core)]

    def remote(src, dst, send, recv, to):
        return pltpu.make_async_remote_copy(
            src_ref=src, dst_ref=dst, send_sem=send, recv_sem=recv,
            device_id=to, device_id_type=pl.DeviceIdType.MESH,
        )

    def arrived(dst, sem):
        pltpu.make_async_copy(dst, dst, sem).wait()

    def at_mate(d):
        return {"ctx": mates[d][0], "dp": mates[d][1]}

    def mate_index(d):
        return 2 * lax.rem(mates[d][0], 2) + mates[d][1]

    def band(c):
        return pl.ds(pl.multiple_of(c * BLOCK, BLOCK), BLOCK)

    def lanes(i, size):
        return pl.ds(pl.multiple_of(i * size, size), size)

    def own_local(c):
        return pltpu.make_async_copy(
            tok_hbm.at[band(c)], own.at[0, band(c)], own_recv.at[0, c]
        )

    def far_copy(c):
        return remote(
            tok_hbm.at[band(c)], own.at[place, band(c)], far_send.at[c], own_recv.at[place, c],
            {"ctx": 2 - side, "dp": 1 - core},
        )

    def fwd_copy(r, c):
        return remote(
            own.at[r, band(c)], own.at[r, band(c)], fwd_send.at[r, c], own_recv.at[r, c],
            {"ctx": sib},
        )

    def x_copy(src, r, c):
        return remote(
            src, xin.at[r, band(c)], x_send.at[r, c], x_recv.at[r, c], {"heads": other}
        )

    def meta_copy(m):
        return remote(
            meta_out, meta_in.at[z], meta_send.at[m], meta_recv.at[z],
            {"ctx": 2 * core + m // 2, "dp": m % 2},
        )

    def kv_copy(m, d, slot, r, c):
        return remote(
            kv_out.at[slot, c], kv_in.at[r * nblk + c], kv_send.at[d, c], kv_recv.at[r, c],
            at_mate(m),
        )

    def q_copy(m, d, slot, r, c):
        return remote(
            q_out.at[slot, c], q_in.at[r * nblk + c], q_send.at[d, c], q_recv.at[r, c],
            at_mate(m),
        )

    def sq_copy(m, d, slot, r):
        return remote(
            sq_out.at[slot], sq_in.at[r], sq_send.at[d], sq_recv.at[r],
            at_mate(m),
        )

    def home_copy(copy, d, *c):
        return copy(d, d, mate_index(d), z, *c)

    def guest_copy(copy, r, *c):
        return copy(0, 3 * r, 2 * (1 - core) + r, away + r, *c)

    def local(out, into, sem):
        pltpu.make_async_copy(out, into, sem).start()

    def owner(i):
        return away + i if i < 2 else 2 * side + i - 2

    def o_copy(i, r, c):
        return remote(
            o_out.at[r * nblk + c], o_in.at[c, :, lanes(mate, wide)], o_send.at[i, c],
            o_recv.at[mate, c], {"ctx": r, "dp": side},
        )

    def o_local(r, c):
        return pltpu.make_async_copy(
            o_out.at[r * nblk + c], o_in.at[c, :, lanes(mate, wide)], o_recv.at[mate, c]
        )

    def rs_copy(c):
        return remote(rs_out.at[c], rs_in.at[c], rs_sem.at[0, c], rs_sem.at[1, c], {"heads": other})

    def st_copy(c):
        return remote(st_out.at[c], st_in.at[c], st_sem.at[0, c], st_sem.at[1, c], {"heads": other})

    tok_copy = pltpu.make_async_copy(tok_hbm, tok, tok_sem)
    two = 2 * wide

    def w_copy(k, part):
        if part:
            return pltpu.make_async_copy(
                wq_hbm.at[k, :, lanes(place, two)], wq.at[k, :, pl.ds(0, two)], w_sem.at[k]
            )
        return pltpu.make_async_copy(wq_hbm.at[k], wq.at[k], w_sem.at[k])

    wo_copy = pltpu.make_async_copy(wo_hbm, wo, w_sem.at[3])
    barrier = pltpu.get_barrier_semaphore()
    greeted = [{"heads": other}, {"dp": 1 - core}]
    for d in range(1, ctx_count):
        for other_core in range(2):
            greeted.append({"ctx": lax.rem(z + d, ctx_count), "dp": other_core})
    for to in greeted:
        pl.semaphore_signal(barrier, inc=1, device_id=to, device_id_type=pl.DeviceIdType.MESH)

    @pl.when(home)
    def _():
        for c in range(nblk):
            own_local(c).start()
        for k in (1, 2, 0):
            w_copy(k, False).start()

    @pl.when(guest)
    def _():
        for k in (1, 2, 0):
            w_copy(k, True).start()

    tok_copy.start()
    wo_copy.start()
    meta_out[...] = jnp.zeros_like(meta_out)
    for r in range(rand):
        meta_out[r : r + 1, :nblk] = rb_ref[r]
    meta_out[rand : rand + 1, : ctx_count * per] = spos_ref[...]
    meta_out[rand + 1 : rand + 2, :pairs] = pair_ref[...]
    meta_out[8 : 8 + listed, : ctx_count * per] = slist_ref[0]
    pl.semaphore_wait(barrier, len(greeted))

    for m in range(4):
        itself = home & (mate == m)

        @pl.when(itself)
        def _():
            pltpu.make_async_copy(meta_out, meta_in.at[z], meta_recv.at[z]).start()

        @pl.when(jnp.logical_not(itself))
        def _():
            meta_copy(m).start()

    @pl.when(home)
    def _():
        for c in range(nblk):
            x_copy(tok_hbm.at[band(c)], 0, c).start()

    @pl.when(guest)
    def _():
        for c in range(nblk):
            far_copy(c).start()

    def relay(r, c):
        arrived(own.at[r, band(c)], own_recv.at[r, c])

        @pl.when(gate)
        def _():
            fwd_copy(r, c).start()

        x_copy(own.at[r, band(c)], r, c).start()

    def product(k, r, c, width):
        val = jnp.dot(
            own[r, band(c), :], wq[k, lanes(half, cols), :width], preferred_element_type=f32
        )
        val = val + jnp.dot(
            xin[r, band(c), :], wq[k, lanes(other, cols), :width], preferred_element_type=f32
        )
        return val.astype(bf16)

    def project_home(c):
        arrived(own.at[0, band(c)], own_recv.at[0, c])
        arrived(xin.at[0, band(c)], x_recv.at[0, c])
        for k in (1, 2):
            val = product(k, 0, c, cols)
            for m in range(4):
                kv_out[m, c, k - 1] = val[:, m * wide : (m + 1) * wide]
        home_copy(kv_copy, 0, c).start()

        @pl.when(jnp.logical_not(gate))
        def _():
            for d in (1, 2):
                home_copy(kv_copy, d, c).start()

        local(kv_out.at[mate, c], kv_in.at[z * nblk + c], kv_recv.at[z, c])
        val = product(0, 0, c, cols)
        for m in range(4):
            q_out[m, c] = val[:, m * wide : (m + 1) * wide]
        home_copy(q_copy, 0, c).start()
        local(q_out.at[mate, c], q_in.at[z * nblk + c], q_recv.at[z, c])

    def project_guest(r, c):
        b = (away + r) * nblk + c
        arrived(xin.at[r, band(c)], x_recv.at[r, c])
        for k in (1, 2):
            val = product(k, r, c, two)
            for m in range(2):
                kv_out[2 * m + r, c, k - 1] = val[:, m * wide : (m + 1) * wide]
        guest_copy(kv_copy, r, c).start()
        local(kv_out.at[2 * core + r, c], kv_in.at[b], kv_recv.at[away + r, c])
        val = product(0, r, c, two)
        for m in range(2):
            q_out[2 * m + r, c] = val[:, m * wide : (m + 1) * wide]
        guest_copy(q_copy, r, c).start()
        local(q_out.at[2 * core + r, c], q_in.at[b], q_recv.at[away + r, c])

    def w_wait(part):
        for k in (1, 2, 0):
            w_copy(k, part).wait()

    order = [(1 - side, c) for c in range(nblk)] + [(side, c) for c in range(nblk)]
    ahead = 5

    @pl.when(guest)
    def _():
        for r, c in order[:ahead]:
            relay(r, c)

    for r in range(ctx_count):
        arrived(meta_in.at[r], meta_recv.at[r])
    meta_local = pltpu.make_async_copy(meta_in, meta_s, meta_sem)
    meta_local.start()
    meta_local.wait()

    bounds = []
    total = 0
    for p in range(pairs):
        total = total + meta_s[0, rand + 1, p]
        bounds.append(total)

    def segments(pos):
        seg = jnp.zeros(pos.shape, i32)
        for bound in bounds:
            seg = seg + jnp.where(pos >= bound, 1, 0)
        return seg

    def spos(i):
        return meta_s[0, rand, i]

    row_1 = lax.broadcasted_iota(i32, (BLOCK, 1), 0)
    lane_1 = lax.broadcasted_iota(i32, (1, BLOCK), 1)

    def mask_block(b, carry):
        r, c = b // nblk, lax.rem(b, nblk)
        seg_q = segments(b * BLOCK + row_1)
        for j in range(3 + rand):
            if j < 3:
                pos = (b + j - 1) * BLOCK + lane_1
                seg = jnp.where((pos >= 0) & (pos < seq), segments(pos), -1)
            else:
                seg = segments(meta_s[r, j - 3, c] * BLOCK + lane_1)
            bias[b, :, j * BLOCK : (j + 1) * BLOCK] = jnp.where(seg_q == seg, 0.0, MASKED)
        return carry

    def masks():
        lax.fori_loop(0, blocks, mask_block, 0)
        key_pos = lax.broadcasted_iota(i32, (1, seq), 1)
        row_all = lax.broadcasted_iota(i32, (ctx_count * srows, 1), 0)
        bits = jnp.zeros((ctx_count * srows, 1), i32)
        places = jnp.zeros((ctx_count * srows, 1), i32)
        for u in range(ctx_count * per):
            word = 0
            for j in range(listed):
                word = word | (1 << meta_s[0, 8 + j, u])
            for g in range(group):
                here = row_all == u // per * srows + g * per + u % per
                bits = jnp.where(here, word, bits)
                places = jnp.where(here, spos(u), places)
        hit = lax.shift_right_logical(
            jnp.broadcast_to(bits, s_ok.shape), jnp.broadcast_to(key_pos // BLOCK, s_ok.shape)
        )
        s_ok[...] = jnp.where(segments(places) == segments(key_pos), hit & 1, 0)

    masks()

    @pl.when(home)
    def _():
        w_wait(False)
        for c in range(nblk):
            project_home(c)

    @pl.when(guest)
    def _():
        w_wait(True)
        for i in range(len(order)):
            project_guest(*order[i])
            if i + ahead < len(order):
                relay(*order[i + ahead])
            if i + ahead == len(order):
                @pl.when(gate)
                def _():
                    for r, c in order[:-1]:
                        fwd_copy(r, c).wait_send()
                    pl.semaphore_signal(
                        go_sem, inc=1, device_id={"dp": 1 - core},
                        device_id_type=pl.DeviceIdType.MESH,
                    )

    row8 = lax.broadcasted_iota(i32, (srows, BLOCK), 0)
    col8 = lax.broadcasted_iota(i32, (srows, BLOCK), 1)

    def pick_rows(slot, r):
        wanted = jnp.zeros((srows, BLOCK), i32)
        for i in range(srows):
            wanted = jnp.where(row8 == i, spos(r * per + i % per), wanted)
        found = jnp.zeros((srows, wide), f32)
        for c in range(nblk):
            pick = (wanted == (r * nblk + c) * BLOCK + col8).astype(f32).astype(bf16)
            found = found + jnp.dot(pick, q_out[slot, c], preferred_element_type=f32)
        sq_out[slot] = found

    @pl.when(home)
    def _():
        for m in range(4):
            pick_rows(m, z)
        for d in (1, 2, 0):
            home_copy(sq_copy, d).start()
        local(sq_out.at[mate], sq_in.at[z], sq_recv.at[z])

    @pl.when(guest)
    def _():
        for r in range(2):
            for m in range(2):
                pick_rows(2 * m + r, away + r)
            guest_copy(sq_copy, r).start()
            local(sq_out.at[2 * core + r], sq_in.at[away + r], sq_recv.at[away + r])

    def range_wait(r):
        for c in range(nblk):
            arrived(kv_in.at[r * nblk + c], kv_recv.at[r, c])

    def to_sibling(copy):
        for c in range(nblk):
            for d in (1, 2):
                home_copy(copy, d, c).start()

    @pl.when(home)
    def _():
        @pl.when(gate)
        def _():
            pl.semaphore_wait(go_sem, 1)
            to_sibling(kv_copy)

        to_sibling(q_copy)

    range_wait(away + 1 - side)
    range_wait(z)
    range_wait(away + side)
    range_wait(sib)
    for r in range(ctx_count):
        arrived(sq_in.at[r], sq_recv.at[r])

    factor = HEAD ** (-0.5)
    nt = (((1,), (1,)), ((), ()))

    def softmax(scores, ok):
        scores = jnp.where(ok, scores * factor, MASKED)
        top = jnp.max(scores, axis=1, keepdims=True)
        weights = jnp.exp(scores - top)
        return weights, jnp.sum(weights, axis=1, keepdims=True)

    lane_head = lax.broadcasted_iota(i32, (ctx_count * srows, wide), 1) // HEAD
    row_head = lax.rem(lax.broadcasted_iota(i32, (ctx_count * srows, wide), 0), srows) // per
    sq = sq_in[...].reshape(ctx_count * srows, wide)
    sq = jnp.where(lane_head == row_head, sq, 0.0).astype(bf16)
    all_k = kv_in[:, 0].reshape(seq, wide)
    scores = lax.dot_general(sq, all_k, nt, preferred_element_type=f32)
    weights, totals = softmax(scores, s_ok[...] > 0)
    all_v = kv_in[:, 1].reshape(seq, wide)
    mixed = jnp.dot(weights.astype(bf16), all_v, preferred_element_type=f32) / totals
    s_res[...] = mixed.reshape(ctx_count, srows, wide)

    lane_q = lax.broadcasted_iota(i32, (BLOCK, wide), 1) // HEAD
    row_q = lax.broadcasted_iota(i32, (BLOCK, wide), 0)
    ones = jnp.ones(((3 + rand) * BLOCK, wide), bf16)

    def attend_block(r, c):
        b = r * nblk + c
        q = q_in[b]
        keys, values = [], []
        for shift in (-1, 0, 1):
            at = jnp.clip(b + shift, 0, blocks - 1)
            keys.append(kv_in[at, 0])
            values.append(kv_in[at, 1])
        for j in range(rand):
            at = meta_s[r, j, c]
            keys.append(kv_in[at, 0])
            values.append(kv_in[at, 1])
        keys = jnp.concatenate(keys, axis=0)
        values = jnp.concatenate([jnp.concatenate(values, axis=0), ones], axis=1)
        out = jnp.zeros((BLOCK, wide), f32)
        for g in range(group):
            qg = jnp.where(lane_q == g, q, jnp.zeros_like(q))
            scores = lax.dot_general(qg, keys, nt, preferred_element_type=f32) + bias[b]
            top = jnp.max(scores, axis=1, keepdims=True)
            weights = jnp.exp2((scores - top) * (factor * LOG2E))
            mix = jnp.dot(weights.astype(bf16), values, preferred_element_type=f32)
            out = jnp.where(lane_q == g, mix[:, :wide] / mix[:, wide:], out)
        res = s_res[r]
        for u in range(per):
            row = res[u : u + 1, :]
            for g in range(1, group):
                row = jnp.where(
                    lane_q[:1] == g, res[g * per + u : g * per + u + 1, :], row
                )
            out = jnp.where(row_q == spos(r * per + u) - b * BLOCK, row, out)
        o_out[b] = out.astype(bf16)

    def attend_step(far, c):
        base = 2 * (side + far - 2 * side * far)
        for i in range(2):
            arrived(q_in.at[(base + i) * nblk + c], q_recv.at[base + i, c])

        def step(i, carry):
            attend_block(base + i, c)
            return carry

        lax.fori_loop(0, 2, step, 0, unroll=2)
        for i in range(2):
            itself = home & (base + i == z)

            @pl.when(itself)
            def _():
                o_local(base + i, c).start()

            @pl.when(jnp.logical_not(itself))
            def _():
                o_copy(2 - 2 * far + i, base + i, c).start()

    def output(c):
        for m in range(4):
            arrived(o_in.at[c, :, lanes(m, wide)], o_recv.at[m, c])
        att = o_in[c]
        rs_out[c] = jnp.dot(att, wo[:, lanes(other, cols)], preferred_element_type=f32).astype(bf16)
        rs_copy(c).start()
        term = jnp.dot(att, wo[:, lanes(half, cols)], preferred_element_type=f32).astype(bf16)
        hidden[band(c), :] = term.astype(f32)

    lane_s = lax.broadcasted_iota(i32, (BLOCK, BLOCK), 1)

    def finish(c):
        arrived(rs_in.at[c], rs_sem.at[1, c])
        hid = tok[band(c), :].astype(f32) + (hidden[band(c), :] + rs_in[c].astype(f32))
        hidden[band(c), :] = hid
        first = jnp.sum(hid, axis=1, keepdims=True)
        second = jnp.sum(hid * hid, axis=1, keepdims=True)
        both = jnp.where(lane_s == 0, first, jnp.where(lane_s == 1, second, 0.0))
        st_out[c] = jnp.transpose(both)[:8]
        st_copy(c).start()

    full = 2 * cols

    def norm(c):
        arrived(st_in.at[c], st_sem.at[1, c])
        sums = jnp.transpose(st_out[c] + st_in[c])
        mean = sums[:, 0:1] / full
        var = sums[:, 1:2] / full - mean * mean
        hid = hidden[band(c), :]
        res = (hid - mean) * lax.rsqrt(var + 1e-05) * gain_ref[...] + bias_ref[...]
        out_ref[band(c), :] = res.astype(bf16)

    wo_copy.wait()
    tok_copy.wait()

    def only(cond, *steps):
        @pl.when(cond)
        def _():
            for do, c in steps:
                do(c)

    rim = jnp.logical_not(gate)
    rim_order = [(1, 0)]
    gate_order = [(0, 0)]
    for c in range(1, nblk):
        rim_order += [(1, c), (0, c - 1)]
        gate_order += [(0, c), (1, c - 1)]
    rim_order.append((0, nblk - 1))
    gate_order.append((1, nblk - 1))
    inner = place + side - 2 * place * side
    done_home = 0
    for i in range(2 * nblk):
        (f0, c0), (f1, c1) = rim_order[i], gate_order[i]
        attend_step(f0 + inner * (f1 - f0), c0 + inner * (c1 - c0))
        if i >= 3 and i % 2 == 1 and i < 2 * nblk - 1:
            only(home & rim, (output, done_home))
            done_home += 1
        if i == 2 * nblk - 2:
            only(guest & rim, (output, 0))

    def rest(first, lead):
        steps = [(output, c) for c in range(first, min(nblk, first + lead))]
        for c in range(nblk):
            steps.append((finish, c))
            if first + lead + c < nblk:
                steps.append((output, first + lead + c))
        return steps + [(norm, c) for c in range(nblk)]

    only(home & rim, *rest(done_home, nblk))
    only(guest & rim, *rest(1, 1))
    only(home & gate, *rest(0, nblk))
    only(guest & gate, *rest(0, 2))

    for m in range(4):
        @pl.when(jnp.logical_not(home & (mate == m)))
        def _():
            meta_copy(m).wait_send()

    @pl.when(home)
    def _():
        for c in range(nblk):
            x_copy(tok_hbm.at[band(c)], 0, c).wait_send()
            for d in range(3):
                home_copy(kv_copy, d, c).wait_send()
                home_copy(q_copy, d, c).wait_send()
        for d in range(3):
            home_copy(sq_copy, d).wait_send()

    @pl.when(guest)
    def _():
        for c in range(nblk):
            far_copy(c).wait_send()
            for r in range(2):
                x_copy(own.at[r, band(c)], r, c).wait_send()
                guest_copy(kv_copy, r, c).wait_send()
                guest_copy(q_copy, r, c).wait_send()
        for r in range(2):
            guest_copy(sq_copy, r).wait_send()

        @pl.when(gate)
        def _():
            for r, c in order[-1:]:
                fwd_copy(r, c).wait_send()

    for c in range(nblk):
        rs_copy(c).wait_send()
        st_copy(c).wait_send()
        for i in range(4):
            if i < 2:
                o_copy(i, owner(i), c).wait_send()
            else:
                @pl.when(jnp.logical_not(home & (owner(i) == z)))
                def _():
                    o_copy(i, owner(i), c).wait_send()


def store_kernel(src_ref, out_hbm, sem):
    copy = pltpu.make_async_copy(src_ref, out_hbm, sem)
    copy.start()
    copy.wait()


def fast_shards(
    tokens, w_qkv, w_out, ln_gain, ln_bias, random_blocks, summary_pos, summary_blocks, pair_lengths
):
    ctx_count = lax.axis_size("ctx")
    rows, cols = tokens.shape[1:]
    nblk = rows // BLOCK
    wide = cols // ctx_count
    group = wide // HEAD
    blocks = nblk * ctx_count
    summaries = summary_pos.shape[1]
    per = summaries // ctx_count
    srows = per * group
    rand = random_blocks.shape[2]
    vmem = pl.BlockSpec(memory_space=pltpu.VMEM)
    hbm = pl.BlockSpec(memory_space=pl.ANY)
    bf16, f32, i32 = jnp.bfloat16, jnp.float32, jnp.int32
    dma = pltpu.SemaphoreType.DMA
    out = pl.pallas_call(
        functools.partial(fast_kernel, ctx_count, rand),
        out_shape=pltpu.VMEM((rows, cols), bf16),
        in_specs=[hbm, hbm, hbm, vmem, vmem, vmem, vmem, vmem, vmem],
        out_specs=vmem,
        scratch_shapes=[
            pltpu.VMEM((3, 2 * cols, cols), bf16),
            pltpu.VMEM(w_out.shape, bf16),
            pltpu.VMEM((rows, cols), bf16),
            pltpu.VMEM((2, rows, cols), bf16),
            pltpu.VMEM((2, rows, cols), bf16),
            pltpu.VMEM((blocks, BLOCK, (3 + rand) * BLOCK), f32),
            pltpu.VMEM((4, nblk, 2, BLOCK, wide), bf16),
            pltpu.VMEM((blocks, 2, BLOCK, wide), bf16),
            pltpu.VMEM((4, nblk, BLOCK, wide), bf16),
            pltpu.VMEM((blocks, BLOCK, wide), bf16),
            pltpu.VMEM((4, srows, wide), f32),
            pltpu.VMEM((ctx_count, srows, wide), f32),
            pltpu.VMEM((ctx_count * srows, blocks * BLOCK), i32),
            pltpu.VMEM((ctx_count, srows, wide), f32),
            pltpu.VMEM((16, 128), i32),
            pltpu.VMEM((ctx_count, 16, 128), i32),
            pltpu.SMEM((ctx_count, 16, 128), i32),
            pltpu.VMEM((blocks, BLOCK, wide), bf16),
            pltpu.VMEM((nblk, BLOCK, cols), bf16),
            pltpu.VMEM((nblk, BLOCK, cols), bf16),
            pltpu.VMEM((nblk, BLOCK, cols), bf16),
            pltpu.VMEM((rows, cols), f32),
            pltpu.VMEM((nblk, 8, BLOCK), f32),
            pltpu.VMEM((nblk, 8, BLOCK), f32),
            dma((4,)),
            dma,
            dma((nblk,)),
            dma((2, nblk)),
            dma((2, nblk)),
            dma((2, nblk)),
            dma((2, nblk)),
            dma((4,)),
            dma((ctx_count,)),
            dma,
            dma((4, nblk)),
            dma((ctx_count, nblk)),
            dma((4, nblk)),
            dma((ctx_count, nblk)),
            dma((4,)),
            dma((ctx_count,)),
            dma((4, nblk)),
            dma((4, nblk)),
            dma((2, nblk)),
            dma((2, nblk)),
            pltpu.SemaphoreType.REGULAR,
        ],
        compiler_params=pltpu.CompilerParams(
            collective_id=0, has_side_effects=True, vmem_limit_bytes=60000 * 1024
        ),
    )(
        tokens[0], w_qkv, w_out, ln_gain[None], ln_bias[None],
        random_blocks.transpose(2, 0, 1), pair_lengths, summary_pos,
        summary_blocks.transpose(0, 2, 1),
    )
    out = pl.pallas_call(
        store_kernel,
        out_shape=jax.ShapeDtypeStruct((rows, cols), bf16),
        in_specs=[vmem],
        out_specs=hbm,
        scratch_shapes=[dma],
    )(pltpu.with_memory_space_constraint(out, pltpu.VMEM))
    return out[None]


def solution(mesh):
    in_specs = (
        P(("groups", "dp"), "ctx", "heads"),
        P(None, None, "heads"),
        P("heads", None),
        P("heads"),
        P("heads"),
        P(("groups", "dp"), "ctx", None),
        P(("groups", "dp"), None),
        P(("groups", "dp"), None, None),
        P(("groups", "dp"), None),
    )
    out_specs = P(("groups", "dp"), "ctx", "heads")
    ctx_count = mesh.shape["ctx"]

    def body(*args):
        rows, cols = args[0].shape[1:]
        wide = cols // ctx_count
        by_heads = (
            ctx_count == 4
            and mesh.shape["heads"] == 2
            and mesh.shape["dp"] == 2
            and wide > 0
            and wide % 128 == 0
            and wide * ctx_count == cols
            and rows // BLOCK <= 128
            and rows // BLOCK * ctx_count <= 32
            and args[6].shape[1] // ctx_count * (wide // HEAD) % 8 == 0
            and rows // BLOCK >= 2
            and args[5].shape[2] <= 6
            and args[7].shape[2] <= 8
            and max(rows // BLOCK, args[6].shape[1], args[8].shape[1]) <= 128
        )
        return (fast_shards if by_heads else shards)(*args)

    return jax.shard_map(body, mesh=mesh, in_specs=in_specs, out_specs=out_specs, check_vma=False)
```

```python
import functools

import jax
import jax.numpy as jnp
from jax import lax
from jax.experimental import pallas as pl
from jax.experimental.pallas import tpu as pltpu
from jax.sharding import PartitionSpec as P

HEAD = 64
BLOCK = 128


MASKED = -1e30
LOG2E = 1.4426950408889634


def extended(x, sides, width):
    for axis, dim in sides:
        size, length = (lax.axis_size(axis), x.shape[dim])
        up = [(i, (i + 1) % size) for i in range(size - 1)]
        down = [(j, i) for i, j in up]
        last = lax.slice_in_dim(x, length - width, length, axis=dim)
        first = lax.slice_in_dim(x, 0, width, axis=dim)
        before = lax.ppermute(last, axis, up)
        after = lax.ppermute(first, axis, down)
        x = jnp.concatenate([before, x, after], axis=dim)
    return x


def segment_ids(positions, bounds):
    return jnp.sum((positions[..., None] >= bounds).astype(jnp.int32), axis=-1)


def attend(queries, keys, values, allowed, head_count):
    group_count, query_len, all_width = queries.shape
    key_len = keys.shape[1]
    query_heads = queries.reshape(group_count, query_len, head_count, HEAD)
    key_heads = keys.reshape(group_count, key_len, head_count, HEAD)
    value_heads = values.reshape(group_count, key_len, head_count, HEAD)
    scores = jnp.einsum(
        "gqhe,gkhe->ghqk", query_heads, key_heads, preferred_element_type=jnp.float32
    ) * HEAD ** (-0.5)
    scores = jnp.where(allowed[:, None], scores, MASKED)
    maxima = jnp.max(scores, axis=-1, keepdims=True)
    weights = jnp.where(allowed[:, None], jnp.exp(scores - maxima), 0.0)
    totals = jnp.sum(weights, axis=-1)
    mixture = jnp.einsum(
        "ghqk,gkhe->gqhe",
        weights.astype(jnp.bfloat16),
        value_heads,
        preferred_element_type=jnp.float32,
    )
    mixture = mixture / jnp.transpose(totals, (0, 2, 1))[..., None]
    return mixture.reshape(group_count, query_len, all_width).astype(jnp.bfloat16)


def three_views(window_span, group_size, axis_pos):
    views = []
    for shift_index in range(3):
        piece = lax.slice_in_dim(
            window_span,
            shift_index * BLOCK,
            shift_index * BLOCK + group_size * BLOCK,
            axis=axis_pos,
        )
        new_shape = (
            window_span.shape[:axis_pos] + (group_size, BLOCK) + window_span.shape[axis_pos + 1 :]
        )
        views.append(piece.reshape(new_shape))
    return jnp.concatenate(views, axis=axis_pos + 1)


def shards(
    tokens, w_qkv, w_out, ln_gain, ln_bias, random_blocks, summary_pos, summary_blocks, pair_lengths
):
    tok_rows = tokens.shape[1]
    head_cols = tokens.shape[2]
    heads_here = head_cols // HEAD
    full_width = w_out.shape[1]
    ctx_count = lax.axis_size("ctx")
    ctx_index = lax.axis_index("ctx")
    block_count = tok_rows // BLOCK
    seq_total = tok_rows * ctx_count
    bounds = jnp.cumsum(pair_lengths[0])
    own_tokens = tokens[0]
    projected = jnp.einsum(
        "nc,kcd->knd",
        lax.all_gather(own_tokens, "heads", axis=1, tiled=True),
        w_qkv,
        preferred_element_type=jnp.float32,
    ).astype(jnp.bfloat16)
    queries = projected[0]
    own_kv = projected[1:3]
    rim_kv = extended(own_kv, (("ctx", 1),), BLOCK)
    query_pos = ctx_index * tok_rows + jnp.arange(tok_rows, dtype=jnp.int32)
    own_seg = segment_ids(query_pos, bounds)
    rim_pos = ctx_index * tok_rows - BLOCK + jnp.arange(tok_rows + 2 * BLOCK, dtype=jnp.int32)
    rim_ok = (rim_pos >= 0) & (rim_pos < seq_total)
    rim_seg = segment_ids(rim_pos, bounds)
    rand_count = random_blocks.shape[2]
    picked = random_blocks[0].reshape(-1)
    pick_count = picked.shape[0]
    capacity = max(2, -(-pick_count // ctx_count))
    owners = picked // block_count
    within = picked % block_count
    slot_order = jnp.arange(pick_count, dtype=jnp.int32)
    earlier = (owners[:, None] == owners[None, :]) & (slot_order[None, :] < slot_order[:, None])
    pick_rank = jnp.sum(earlier.astype(jnp.int32), axis=1)
    pick_slot = owners * capacity + pick_rank
    slot_table = (
        pick_slot[:, None] == jnp.arange(ctx_count * capacity, dtype=jnp.int32)[None, :]
    ).astype(jnp.int32)
    requests = jnp.sum(slot_table * within[:, None], axis=0).reshape(ctx_count, capacity)
    own_blocks = own_kv.reshape(2, block_count, BLOCK, head_cols).transpose(1, 0, 2, 3)
    reply = jnp.take(
        own_blocks, lax.all_to_all(requests, "ctx", split_axis=0, concat_axis=0, tiled=True), axis=0
    )
    fetched = lax.all_to_all(reply, "ctx", split_axis=0, concat_axis=0, tiled=True)
    flat_blocks = fetched.reshape(ctx_count * capacity, 2, BLOCK, head_cols)
    far_kv = jnp.take(flat_blocks, pick_slot, axis=0).reshape(
        block_count, rand_count, 2, BLOCK, head_cols
    )
    far_kv = far_kv.transpose(2, 0, 1, 3, 4).reshape(2, block_count, rand_count * BLOCK, head_cols)
    far_pos = (
        picked.reshape(block_count, rand_count)[:, :, None] * BLOCK
        + jnp.arange(BLOCK, dtype=jnp.int32)
    ).reshape(block_count, rand_count * BLOCK)
    far_seg = segment_ids(far_pos, bounds)
    group_size = min(4, block_count)
    group_steps = block_count // group_size

    def window_step(unused, step_index):
        near_kv = three_views(rim_kv, group_size, 1)
        near_ok = three_views(rim_ok, group_size, 0)
        near_seg = three_views(rim_seg, group_size, 0)
        key_set = jnp.concatenate([near_kv, far_kv], axis=2)
        key_seg = jnp.concatenate([near_seg, far_seg], axis=1)
        key_ok = jnp.concatenate([near_ok, jnp.ones(far_seg.shape, jnp.bool_)], axis=1)
        query_seg = own_seg.reshape(group_size, BLOCK)
        allowed = key_ok[:, None, :] & (key_seg[:, None, :] == query_seg[:, :, None])
        query_group = queries.reshape(group_size, BLOCK, head_cols)
        return (unused, attend(query_group, key_set[0], key_set[1], allowed, heads_here))

    _, window_out = lax.scan(window_step, 0, jnp.arange(group_steps, dtype=jnp.int32))
    attention = window_out.reshape(tok_rows, head_cols)
    summary_rows = summary_pos[0]
    summary_lists = summary_blocks[0]
    summaries = summary_rows.shape[0]
    per_device = summaries // ctx_count
    mine = (
        lax.dynamic_slice_in_dim(summary_rows, ctx_index * per_device, per_device, 0)
        - ctx_index * tok_rows
    )
    summary_query = jnp.take(queries, mine, axis=0)
    all_queries = lax.all_gather(summary_query, "ctx", axis=0, tiled=True)
    summary_seg = segment_ids(summary_rows, bounds)
    key_block = ctx_index * block_count + jnp.arange(block_count, dtype=jnp.int32)
    listed = jnp.any(summary_lists[:, :, None] == key_block[None, None, :], axis=1)
    key_heads = own_kv[0].reshape(tok_rows, heads_here, HEAD)
    value_heads = own_kv[1].reshape(tok_rows, heads_here, HEAD)
    summary_group = min(128, summaries)
    group_total = summaries // summary_group

    def group_scores():
        query_part = all_queries.reshape(summary_group, heads_here, HEAD)
        allowed = jnp.broadcast_to(listed[:, :, None], (summary_group, block_count, BLOCK)).reshape(
            summary_group, tok_rows
        )
        allowed = allowed & (own_seg[None, :] == summary_seg[:, None])
        scores = jnp.einsum(
            "qhe,khe->hqk", query_part, key_heads, preferred_element_type=jnp.float32
        ) * HEAD ** (-0.5)
        return (jnp.where(allowed[None], scores, MASKED), allowed)

    def weigh(scores, allowed, maxima):
        weights = jnp.where(allowed[None], jnp.exp(scores - maxima[:, :, None]), 0.0)
        totals = jnp.sum(weights, axis=-1)
        mixture = jnp.einsum(
            "hqk,khe->qhe",
            weights.astype(jnp.bfloat16),
            value_heads,
            preferred_element_type=jnp.float32,
        )
        return (totals.T, mixture.reshape(summary_group, head_cols))

    def max_step(unused, group_index):
        scores, allowed = group_scores()
        return (unused, jnp.max(scores, axis=-1).T)

    _, maxima_all = lax.scan(max_step, 0, jnp.arange(group_total, dtype=jnp.int32))
    maxima_all = lax.pmax(maxima_all.reshape(summaries, heads_here), "ctx")

    def sum_step(unused, group_index):
        scores, allowed = group_scores()
        maxima = maxima_all.T
        return (unused, weigh(scores, allowed, maxima))

    _, (totals_all, mixture_all) = lax.scan(sum_step, 0, jnp.arange(group_total, dtype=jnp.int32))
    totals_all = totals_all.reshape(summaries, heads_here)
    mixture_all = mixture_all.reshape(summaries, head_cols)
    totals_all, mixture_all = (
        lax.psum(totals_all.astype(jnp.bfloat16), "ctx").astype(jnp.float32),
        lax.psum(mixture_all.astype(jnp.bfloat16), "ctx").astype(jnp.float32),
    )
    own_totals = lax.dynamic_slice_in_dim(totals_all, ctx_index * per_device, per_device, 0)
    own_mixture = lax.dynamic_slice_in_dim(mixture_all, ctx_index * per_device, per_device, 0)
    summary_out = (own_mixture / jnp.repeat(own_totals, HEAD, axis=1)).astype(jnp.bfloat16)
    attention = attention.at[mine].set(summary_out)
    partial_value = jnp.dot(attention, w_out, preferred_element_type=jnp.float32)
    summed = lax.psum_scatter(
        partial_value.astype(jnp.bfloat16), "heads", scatter_dimension=1, tiled=True
    ).astype(jnp.float32)
    hidden = own_tokens.astype(jnp.float32) + summed
    row_sums = lax.psum((jnp.sum(hidden, axis=1), jnp.sum(hidden * hidden, axis=1)), "heads")
    row_mean = row_sums[0] / full_width
    row_var = row_sums[1] / full_width - row_mean * row_mean
    normed = (hidden - row_mean[:, None]) * lax.rsqrt(row_var + 1e-05)[:, None] * ln_gain + ln_bias
    return normed.astype(jnp.bfloat16)[None]


def fast_kernel(
    ctx_count, rand, tok_hbm, wq_hbm, wo_hbm, gain_ref, bias_ref, rb_ref, pair_ref, spos_ref,
    slist_ref, out_ref, wq, wo, tok, own, xin, bias, kv_out, kv_in, q_out, q_in, sq_out,
    sq_in, s_ok, s_res, meta_out, meta_in, meta_s, o_out, o_in, rs_out, rs_in, hidden, st_out,
    st_in, w_sem, tok_sem, far_send, own_recv, fwd_send, x_send, x_recv, meta_send, meta_recv, meta_sem, kv_send, kv_recv,
    q_send, q_recv, sq_send, sq_recv, o_send, o_recv, rs_sem, st_sem,
    go_sem,
):
    z = lax.axis_index("ctx")
    half = lax.axis_index("heads")
    core = lax.axis_index("dp")
    other = 1 - half
    rows, cols = tok_hbm.shape
    nblk = rows // BLOCK
    wide = kv_in.shape[3]
    group = wide // HEAD
    blocks = ctx_count * nblk
    seq = blocks * BLOCK
    pairs = pair_ref.shape[1]
    listed = slist_ref.shape[1]
    per = spos_ref.shape[1] // ctx_count
    srows = per * group
    side = z // 2
    place = lax.rem(z, 2)
    sib = z + 1 - 2 * place
    home = core == side
    guest = core != side
    gate = z == 1 + side
    mate = 2 * place + core
    away = 2 * (1 - side)
    f32, bf16, i32 = jnp.float32, jnp.bfloat16, jnp.int32
    mates = [(z, 1 - core), (sib, core), (sib, 1 - core)]

    def remote(src, dst, send, recv, to):
        return pltpu.make_async_remote_copy(
            src_ref=src, dst_ref=dst, send_sem=send, recv_sem=recv,
            device_id=to, device_id_type=pl.DeviceIdType.MESH,
        )

    def arrived(dst, sem):
        pltpu.make_async_copy(dst, dst, sem).wait()

    def at_mate(d):
        return {"ctx": mates[d][0], "dp": mates[d][1]}

    def mate_index(d):
        return 2 * lax.rem(mates[d][0], 2) + mates[d][1]

    def band(c):
        return pl.ds(pl.multiple_of(c * BLOCK, BLOCK), BLOCK)

    def lanes(i, size):
        return pl.ds(pl.multiple_of(i * size, size), size)

    def own_local(c):
        return pltpu.make_async_copy(
            tok_hbm.at[band(c)], own.at[0, band(c)], own_recv.at[0, c]
        )

    def far_copy(c):
        return remote(
            tok_hbm.at[band(c)], own.at[place, band(c)], far_send, own_recv.at[place, c],
            {"ctx": 2 - side, "dp": 1 - core},
        )

    def fwd_copy(r, c):
        return remote(
            own.at[r, band(c)], own.at[r, band(c)], fwd_send.at[r, c], own_recv.at[r, c],
            {"ctx": sib},
        )

    def x_copy(src, r, c):
        return remote(
            src, xin.at[r, band(c)], x_send.at[r], x_recv.at[r, c], {"heads": other}
        )

    def meta_copy(m):
        return remote(
            meta_out, meta_in.at[z], meta_send.at[m], meta_recv.at[z],
            {"ctx": 2 * core + m // 2, "dp": m % 2},
        )

    def kv_copy(m, d, slot, r, c):
        return remote(
            kv_out.at[slot, c], kv_in.at[r * nblk + c], kv_send.at[d], kv_recv.at[r],
            at_mate(m),
        )

    def q_copy(m, d, slot, r, c):
        return remote(
            q_out.at[slot, c], q_in.at[r * nblk + c], q_send.at[d], q_recv.at[r, c],
            at_mate(m),
        )

    def sq_copy(m, d, slot, r):
        return remote(
            sq_out.at[slot], sq_in.at[r], sq_send.at[d], sq_recv.at[r],
            at_mate(m),
        )

    def home_copy(copy, d, *c):
        return copy(d, d, mate_index(d), z, *c)

    def guest_copy(copy, r, *c):
        return copy(0, 3 * r, 2 * (1 - core) + r, away + r, *c)

    def local(out, into, sem):
        pltpu.make_async_copy(out, into, sem).start()

    def owner(i):
        return away + i if i < 2 else 2 * side + i - 2

    def o_copy(i, r, c):
        return remote(
            o_out.at[r * nblk + c], o_in.at[c, :, lanes(mate, wide)], o_send.at[i],
            o_recv.at[c], {"ctx": r, "dp": side},
        )

    def o_local(r, c):
        return pltpu.make_async_copy(
            o_out.at[r * nblk + c], o_in.at[c, :, lanes(mate, wide)], o_recv.at[c]
        )

    def rs_copy(c):
        return remote(rs_out.at[c], rs_in.at[c], rs_sem.at[nblk], rs_sem.at[c], {"heads": other})

    def st_copy(c):
        return remote(st_out.at[c], st_in.at[c], st_sem.at[nblk], st_sem.at[c], {"heads": other})

    tok_copy = pltpu.make_async_copy(tok_hbm, tok, tok_sem)
    two = 2 * wide

    def w_copy(k, part):
        if part:
            return pltpu.make_async_copy(
                wq_hbm.at[k, :, lanes(place, two)], wq.at[k, :, pl.ds(0, two)], w_sem.at[k]
            )
        return pltpu.make_async_copy(wq_hbm.at[k], wq.at[k], w_sem.at[k])

    wo_copy = pltpu.make_async_copy(wo_hbm, wo, w_sem.at[3])
    barrier = pltpu.get_barrier_semaphore()
    greeted = [{"heads": other}, {"dp": 1 - core}]
    for d in range(1, ctx_count):
        for other_core in range(2):
            greeted.append({"ctx": lax.rem(z + d, ctx_count), "dp": other_core})
    for to in greeted:
        pl.semaphore_signal(barrier, inc=1, device_id=to, device_id_type=pl.DeviceIdType.MESH)

    @pl.when(home)
    def _():
        for c in range(nblk):
            own_local(c).start()
        for k in (1, 2, 0):
            w_copy(k, False).start()

    @pl.when(guest)
    def _():
        for k in (1, 2, 0):
            w_copy(k, True).start()

    tok_copy.start()
    wo_copy.start()
    meta_out[...] = jnp.zeros_like(meta_out)
    for r in range(rand):
        meta_out[r : r + 1, :nblk] = rb_ref[r]
    meta_out[rand : rand + 1, : ctx_count * per] = spos_ref[...]
    meta_out[rand + 1 : rand + 2, :pairs] = pair_ref[...]
    meta_out[8 : 8 + listed, : ctx_count * per] = slist_ref[0]
    pl.semaphore_wait(barrier, len(greeted))

    for m in range(4):
        itself = home & (mate == m)

        @pl.when(itself)
        def _():
            pltpu.make_async_copy(meta_out, meta_in.at[z], meta_recv.at[z]).start()

        @pl.when(jnp.logical_not(itself))
        def _():
            meta_copy(m).start()

    @pl.when(home)
    def _():
        for c in range(nblk):
            x_copy(tok_hbm.at[band(c)], 0, c).start()

    @pl.when(guest)
    def _():
        for c in range(nblk):
            far_copy(c).start()

    def relay(r, c):
        arrived(own.at[r, band(c)], own_recv.at[r, c])

        @pl.when(gate)
        def _():
            fwd_copy(r, c).start()

        x_copy(own.at[r, band(c)], r, c).start()

    def product(k, r, c, width):
        val = jnp.dot(
            own[r, band(c), :], wq[k, lanes(half, cols), :width], preferred_element_type=f32
        )
        val = val + jnp.dot(
            xin[r, band(c), :], wq[k, lanes(other, cols), :width], preferred_element_type=f32
        )
        return val.astype(bf16)

    def project_home(c):
        arrived(own.at[0, band(c)], own_recv.at[0, c])
        arrived(xin.at[0, band(c)], x_recv.at[0, c])
        for k in (1, 2):
            val = product(k, 0, c, cols)
            for m in range(4):
                kv_out[m, c, k - 1] = val[:, m * wide : (m + 1) * wide]
        home_copy(kv_copy, 0, c).start()

        @pl.when(jnp.logical_not(gate))
        def _():
            for d in (1, 2):
                home_copy(kv_copy, d, c).start()

        local(kv_out.at[mate, c], kv_in.at[z * nblk + c], kv_recv.at[z])
        val = product(0, 0, c, cols)
        for m in range(4):
            q_out[m, c] = val[:, m * wide : (m + 1) * wide]
        home_copy(q_copy, 0, c).start()
        local(q_out.at[mate, c], q_in.at[z * nblk + c], q_recv.at[z, c])

    def project_guest(r, c):
        b = (away + r) * nblk + c
        arrived(xin.at[r, band(c)], x_recv.at[r, c])
        for k in (1, 2):
            val = product(k, r, c, two)
            for m in range(2):
                kv_out[2 * m + r, c, k - 1] = val[:, m * wide : (m + 1) * wide]
        guest_copy(kv_copy, r, c).start()
        local(kv_out.at[2 * core + r, c], kv_in.at[b], kv_recv.at[away + r])
        val = product(0, r, c, two)
        for m in range(2):
            q_out[2 * m + r, c] = val[:, m * wide : (m + 1) * wide]
        guest_copy(q_copy, r, c).start()
        local(q_out.at[2 * core + r, c], q_in.at[b], q_recv.at[away + r, c])

    def w_wait(part):
        for k in (1, 2, 0):
            w_copy(k, part).wait()

    order = [(1 - side, c) for c in range(nblk)] + [(side, c) for c in range(nblk)]
    ahead = 5

    @pl.when(guest)
    def _():
        for r, c in order[:ahead]:
            relay(r, c)

    for r in range(ctx_count):
        arrived(meta_in.at[r], meta_recv.at[r])
    meta_local = pltpu.make_async_copy(meta_in, meta_s, meta_sem)
    meta_local.start()
    meta_local.wait()

    bounds = []
    total = 0
    for p in range(pairs):
        total = total + meta_s[0, rand + 1, p]
        bounds.append(total)

    def segments(pos):
        seg = jnp.zeros(pos.shape, i32)
        for bound in bounds:
            seg = seg + jnp.where(pos >= bound, 1, 0)
        return seg

    def spos(i):
        return meta_s[0, rand, i]

    row_1 = lax.broadcasted_iota(i32, (BLOCK, 1), 0)
    lane_1 = lax.broadcasted_iota(i32, (1, BLOCK), 1)

    def mask_block(b, carry):
        r, c = b // nblk, lax.rem(b, nblk)
        seg_q = segments(b * BLOCK + row_1)
        for j in range(3 + rand):
            if j < 3:
                pos = (b + j - 1) * BLOCK + lane_1
                seg = jnp.where((pos >= 0) & (pos < seq), segments(pos), -1)
            else:
                seg = segments(meta_s[r, j - 3, c] * BLOCK + lane_1)
            bias[b, :, j * BLOCK : (j + 1) * BLOCK] = jnp.where(seg_q == seg, 0.0, MASKED)
        return carry

    def masks():
        lax.fori_loop(0, blocks, mask_block, 0)
        key_pos = lax.broadcasted_iota(i32, (1, seq), 1)
        row_all = lax.broadcasted_iota(i32, (ctx_count * srows, 1), 0)
        bits = jnp.zeros((ctx_count * srows, 1), i32)
        places = jnp.zeros((ctx_count * srows, 1), i32)
        for u in range(ctx_count * per):
            word = 0
            for j in range(listed):
                word = word | (1 << meta_s[0, 8 + j, u])
            for g in range(group):
                here = row_all == u // per * srows + g * per + u % per
                bits = jnp.where(here, word, bits)
                places = jnp.where(here, spos(u), places)
        hit = lax.shift_right_logical(
            jnp.broadcast_to(bits, s_ok.shape), jnp.broadcast_to(key_pos // BLOCK, s_ok.shape)
        )
        s_ok[...] = jnp.where(segments(places) == segments(key_pos), hit & 1, 0)

    masks()

    @pl.when(home)
    def _():
        w_wait(False)
        for c in range(nblk):
            project_home(c)

    @pl.when(guest)
    def _():
        w_wait(True)
        for i in range(len(order)):
            project_guest(*order[i])
            if i + ahead < len(order):
                relay(*order[i + ahead])
            if i + ahead == len(order):
                @pl.when(gate)
                def _():
                    for r, c in order[:-1]:
                        fwd_copy(r, c).wait_send()
                    pl.semaphore_signal(
                        go_sem, inc=1, device_id={"dp": 1 - core},
                        device_id_type=pl.DeviceIdType.MESH,
                    )

    row8 = lax.broadcasted_iota(i32, (srows, BLOCK), 0)
    col8 = lax.broadcasted_iota(i32, (srows, BLOCK), 1)

    def pick_rows(slot, r):
        wanted = jnp.zeros((srows, BLOCK), i32)
        for i in range(srows):
            wanted = jnp.where(row8 == i, spos(r * per + i % per), wanted)
        found = jnp.zeros((srows, wide), f32)
        for c in range(nblk):
            pick = (wanted == (r * nblk + c) * BLOCK + col8).astype(f32).astype(bf16)
            found = found + jnp.dot(pick, q_out[slot, c], preferred_element_type=f32)
        sq_out[slot] = found

    @pl.when(home)
    def _():
        for m in range(4):
            pick_rows(m, z)
        for d in (1, 2, 0):
            home_copy(sq_copy, d).start()
        local(sq_out.at[mate], sq_in.at[z], sq_recv.at[z])

    @pl.when(guest)
    def _():
        for r in range(2):
            for m in range(2):
                pick_rows(2 * m + r, away + r)
            guest_copy(sq_copy, r).start()
            local(sq_out.at[2 * core + r], sq_in.at[away + r], sq_recv.at[away + r])

    def range_wait(r):
        arrived(kv_in.at[pl.ds(r * nblk, nblk)], kv_recv.at[r])

    def to_sibling(copy):
        for c in range(nblk):
            for d in (1, 2):
                home_copy(copy, d, c).start()

    @pl.when(home)
    def _():
        @pl.when(gate)
        def _():
            pl.semaphore_wait(go_sem, 1)
            to_sibling(kv_copy)

        to_sibling(q_copy)

    range_wait(away + 1 - side)
    range_wait(z)
    range_wait(away + side)
    range_wait(sib)
    for r in range(ctx_count):
        arrived(sq_in.at[r], sq_recv.at[r])

    factor = HEAD ** (-0.5)
    nt = (((1,), (1,)), ((), ()))

    def softmax(scores, ok):
        scores = jnp.where(ok, scores * factor, MASKED)
        top = jnp.max(scores, axis=1, keepdims=True)
        weights = jnp.exp(scores - top)
        return weights, jnp.sum(weights, axis=1, keepdims=True)

    lane_head = lax.broadcasted_iota(i32, (ctx_count * srows, wide), 1) // HEAD
    row_head = lax.rem(lax.broadcasted_iota(i32, (ctx_count * srows, wide), 0), srows) // per
    sq = sq_in[...].reshape(ctx_count * srows, wide)
    sq = jnp.where(lane_head == row_head, sq, 0.0).astype(bf16)
    all_k = kv_in[:, 0].reshape(seq, wide)
    scores = lax.dot_general(sq, all_k, nt, preferred_element_type=f32)
    weights, totals = softmax(scores, s_ok[...] > 0)
    all_v = kv_in[:, 1].reshape(seq, wide)
    mixed = jnp.dot(weights.astype(bf16), all_v, preferred_element_type=f32) / totals
    s_res[...] = mixed.reshape(ctx_count, srows, wide)

    lane_q = lax.broadcasted_iota(i32, (BLOCK, wide), 1) // HEAD
    row_q = lax.broadcasted_iota(i32, (BLOCK, wide), 0)
    ones = jnp.ones(((3 + rand) * BLOCK, wide), bf16)

    def attend_block(r, c):
        b = r * nblk + c
        q = q_in[b]
        keys, values = [], []
        for shift in (-1, 0, 1):
            at = jnp.clip(b + shift, 0, blocks - 1)
            keys.append(kv_in[at, 0])
            values.append(kv_in[at, 1])
        for j in range(rand):
            at = meta_s[r, j, c]
            keys.append(kv_in[at, 0])
            values.append(kv_in[at, 1])
        keys = jnp.concatenate(keys, axis=0)
        values = jnp.concatenate([jnp.concatenate(values, axis=0), ones], axis=1)
        out = jnp.zeros((BLOCK, wide), f32)
        for g in range(group):
            qg = jnp.where(lane_q == g, q, jnp.zeros_like(q))
            scores = lax.dot_general(qg, keys, nt, preferred_element_type=f32) + bias[b]
            top = jnp.max(scores, axis=1, keepdims=True)
            weights = jnp.exp2((scores - top) * (factor * LOG2E))
            mix = jnp.dot(weights.astype(bf16), values, preferred_element_type=f32)
            out = jnp.where(lane_q == g, mix[:, :wide] / mix[:, wide:], out)
        res = s_res[r]
        for u in range(per):
            row = res[u : u + 1, :]
            for g in range(1, group):
                row = jnp.where(
                    lane_q[:1] == g, res[g * per + u : g * per + u + 1, :], row
                )
            out = jnp.where(row_q == spos(r * per + u) - b * BLOCK, row, out)
        o_out[b] = out.astype(bf16)

    def attend_step(far, c):
        base = 2 * (side + far - 2 * side * far)
        for i in range(2):
            arrived(q_in.at[(base + i) * nblk + c], q_recv.at[base + i, c])

        def step(i, carry):
            attend_block(base + i, c)
            return carry

        lax.fori_loop(0, 2, step, 0, unroll=2)
        for i in range(2):
            itself = home & (base + i == z)

            @pl.when(itself)
            def _():
                o_local(base + i, c).start()

            @pl.when(jnp.logical_not(itself))
            def _():
                o_copy(2 - 2 * far + i, base + i, c).start()

    def output(c):
        arrived(o_in.at[c], o_recv.at[c])
        att = o_in[c]
        rs_out[c] = jnp.dot(att, wo[:, lanes(other, cols)], preferred_element_type=f32).astype(bf16)
        rs_copy(c).start()
        term = jnp.dot(att, wo[:, lanes(half, cols)], preferred_element_type=f32).astype(bf16)
        hidden[band(c), :] = term.astype(f32)

    lane_s = lax.broadcasted_iota(i32, (BLOCK, BLOCK), 1)

    def finish(c):
        arrived(rs_in.at[c], rs_sem.at[c])
        hid = tok[band(c), :].astype(f32) + (hidden[band(c), :] + rs_in[c].astype(f32))
        hidden[band(c), :] = hid
        first = jnp.sum(hid, axis=1, keepdims=True)
        second = jnp.sum(hid * hid, axis=1, keepdims=True)
        both = jnp.where(lane_s == 0, first, jnp.where(lane_s == 1, second, 0.0))
        st_out[c] = jnp.transpose(both)[:8]
        st_copy(c).start()

    full = 2 * cols

    def norm(c):
        arrived(st_in.at[c], st_sem.at[c])
        sums = jnp.transpose(st_out[c] + st_in[c])
        mean = sums[:, 0:1] / full
        var = sums[:, 1:2] / full - mean * mean
        hid = hidden[band(c), :]
        res = (hid - mean) * lax.rsqrt(var + 1e-05) * gain_ref[...] + bias_ref[...]
        out_ref[band(c), :] = res.astype(bf16)

    wo_copy.wait()
    tok_copy.wait()

    def only(cond, *steps):
        @pl.when(cond)
        def _():
            for do, c in steps:
                do(c)

    rim = jnp.logical_not(gate)
    rim_order = [(1, 0)]
    gate_order = [(0, 0)]
    for c in range(1, nblk):
        rim_order += [(1, c), (0, c - 1)]
        gate_order += [(0, c), (1, c - 1)]
    rim_order.append((0, nblk - 1))
    gate_order.append((1, nblk - 1))
    inner = place + side - 2 * place * side
    done_home = 0
    for i in range(2 * nblk):
        (f0, c0), (f1, c1) = rim_order[i], gate_order[i]
        attend_step(f0 + inner * (f1 - f0), c0 + inner * (c1 - c0))
        if i >= 3 and i % 2 == 1 and i < 2 * nblk - 1:
            only(home & rim, (output, done_home))
            done_home += 1
        if i == 2 * nblk - 2:
            only(guest & rim, (output, 0))

    def rest(first, lead):
        steps = [(output, c) for c in range(first, min(nblk, first + lead))]
        for c in range(nblk):
            steps.append((finish, c))
            if first + lead + c < nblk:
                steps.append((output, first + lead + c))
        return steps + [(norm, c) for c in range(nblk)]

    only(home & rim, *rest(done_home, nblk))
    only(guest & rim, *rest(1, 1))
    only(home & gate, *rest(0, nblk))
    only(guest & gate, *rest(0, 2))

    for m in range(4):
        @pl.when(jnp.logical_not(home & (mate == m)))
        def _():
            meta_copy(m).wait_send()

    @pl.when(home)
    def _():
        arrived(own.at[0], x_send.at[0])
        for d in range(3):
            arrived(kv_out.at[d], kv_send.at[d])
            arrived(q_out.at[d], q_send.at[d])
            home_copy(sq_copy, d).wait_send()

    @pl.when(guest)
    def _():
        arrived(tok, far_send)
        for r in range(2):
            arrived(own.at[r], x_send.at[r])
            arrived(kv_out.at[r], kv_send.at[3 * r])
            arrived(q_out.at[r], q_send.at[3 * r])
            guest_copy(sq_copy, r).wait_send()

        @pl.when(gate)
        def _():
            for r, c in order[-1:]:
                fwd_copy(r, c).wait_send()

    arrived(rs_out, rs_sem.at[nblk])
    arrived(st_out, st_sem.at[nblk])
    for i in range(4):
        if i < 2:
            arrived(o_out.at[pl.ds(0, nblk)], o_send.at[i])
        else:
            @pl.when(jnp.logical_not(home & (owner(i) == z)))
            def _():
                arrived(o_out.at[pl.ds(0, nblk)], o_send.at[i])


def store_kernel(src_ref, out_hbm, sem):
    copy = pltpu.make_async_copy(src_ref, out_hbm, sem)
    copy.start()
    copy.wait()


def fast_shards(
    tokens, w_qkv, w_out, ln_gain, ln_bias, random_blocks, summary_pos, summary_blocks, pair_lengths
):
    ctx_count = lax.axis_size("ctx")
    rows, cols = tokens.shape[1:]
    nblk = rows // BLOCK
    wide = cols // ctx_count
    group = wide // HEAD
    blocks = nblk * ctx_count
    summaries = summary_pos.shape[1]
    per = summaries // ctx_count
    srows = per * group
    rand = random_blocks.shape[2]
    vmem = pl.BlockSpec(memory_space=pltpu.VMEM)
    hbm = pl.BlockSpec(memory_space=pl.ANY)
    bf16, f32, i32 = jnp.bfloat16, jnp.float32, jnp.int32
    dma = pltpu.SemaphoreType.DMA
    out = pl.pallas_call(
        functools.partial(fast_kernel, ctx_count, rand),
        out_shape=pltpu.VMEM((rows, cols), bf16),
        in_specs=[hbm, hbm, hbm, vmem, vmem, vmem, vmem, vmem, vmem],
        out_specs=vmem,
        scratch_shapes=[
            pltpu.VMEM((3, 2 * cols, cols), bf16),
            pltpu.VMEM(w_out.shape, bf16),
            pltpu.VMEM((rows, cols), bf16),
            pltpu.VMEM((2, rows, cols), bf16),
            pltpu.VMEM((2, rows, cols), bf16),
            pltpu.VMEM((blocks, BLOCK, (3 + rand) * BLOCK), f32),
            pltpu.VMEM((4, nblk, 2, BLOCK, wide), bf16),
            pltpu.VMEM((blocks, 2, BLOCK, wide), bf16),
            pltpu.VMEM((4, nblk, BLOCK, wide), bf16),
            pltpu.VMEM((blocks, BLOCK, wide), bf16),
            pltpu.VMEM((4, srows, wide), f32),
            pltpu.VMEM((ctx_count, srows, wide), f32),
            pltpu.VMEM((ctx_count * srows, blocks * BLOCK), i32),
            pltpu.VMEM((ctx_count, srows, wide), f32),
            pltpu.VMEM((16, 128), i32),
            pltpu.VMEM((ctx_count, 16, 128), i32),
            pltpu.SMEM((ctx_count, 16, 128), i32),
            pltpu.VMEM((blocks, BLOCK, wide), bf16),
            pltpu.VMEM((nblk, BLOCK, cols), bf16),
            pltpu.VMEM((nblk, BLOCK, cols), bf16),
            pltpu.VMEM((nblk, BLOCK, cols), bf16),
            pltpu.VMEM((rows, cols), f32),
            pltpu.VMEM((nblk, 8, BLOCK), f32),
            pltpu.VMEM((nblk, 8, BLOCK), f32),
            dma((4,)),
            dma,
            dma,
            dma((2, nblk)),
            dma((2, nblk)),
            dma((2,)),
            dma((2, nblk)),
            dma((4,)),
            dma((ctx_count,)),
            dma,
            dma((4,)),
            dma((ctx_count,)),
            dma((4,)),
            dma((ctx_count, nblk)),
            dma((4,)),
            dma((ctx_count,)),
            dma((4,)),
            dma((nblk,)),
            dma((nblk + 1,)),
            dma((nblk + 1,)),
            pltpu.SemaphoreType.REGULAR,
        ],
        compiler_params=pltpu.CompilerParams(
            collective_id=0, has_side_effects=True, vmem_limit_bytes=60000 * 1024
        ),
    )(
        tokens[0], w_qkv, w_out, ln_gain[None], ln_bias[None],
        random_blocks.transpose(2, 0, 1), pair_lengths, summary_pos,
        summary_blocks.transpose(0, 2, 1),
    )
    out = pl.pallas_call(
        store_kernel,
        out_shape=jax.ShapeDtypeStruct((rows, cols), bf16),
        in_specs=[vmem],
        out_specs=hbm,
        scratch_shapes=[dma],
    )(pltpu.with_memory_space_constraint(out, pltpu.VMEM))
    return out[None]


def solution(mesh):
    in_specs = (
        P(("groups", "dp"), "ctx", "heads"),
        P(None, None, "heads"),
        P("heads", None),
        P("heads"),
        P("heads"),
        P(("groups", "dp"), "ctx", None),
        P(("groups", "dp"), None),
        P(("groups", "dp"), None, None),
        P(("groups", "dp"), None),
    )
    out_specs = P(("groups", "dp"), "ctx", "heads")
    ctx_count = mesh.shape["ctx"]

    def body(*args):
        rows, cols = args[0].shape[1:]
        wide = cols // ctx_count
        by_heads = (
            ctx_count == 4
            and mesh.shape["heads"] == 2
            and mesh.shape["dp"] == 2
            and wide > 0
            and wide % 128 == 0
            and wide * ctx_count == cols
            and rows // BLOCK <= 128
            and rows // BLOCK * ctx_count <= 32
            and args[6].shape[1] // ctx_count * (wide // HEAD) % 8 == 0
            and rows // BLOCK >= 2
            and args[5].shape[2] <= 6
            and args[7].shape[2] <= 8
            and max(rows // BLOCK, args[6].shape[1], args[8].shape[1]) <= 128
        )
        return (fast_shards if by_heads else shards)(*args)

    return jax.shard_map(body, mesh=mesh, in_specs=in_specs, out_specs=out_specs, check_vma=False)
```

```python
import functools

import jax
import jax.numpy as jnp
from jax import lax
from jax.experimental import pallas as pl
from jax.experimental.pallas import tpu as pltpu
from jax.sharding import PartitionSpec as P

HEAD = 64
BLOCK = 128


MASKED = -1e30
LOG2E = 1.4426950408889634


def extended(x, sides, width):
    for axis, dim in sides:
        size, length = (lax.axis_size(axis), x.shape[dim])
        up = [(i, (i + 1) % size) for i in range(size - 1)]
        down = [(j, i) for i, j in up]
        last = lax.slice_in_dim(x, length - width, length, axis=dim)
        first = lax.slice_in_dim(x, 0, width, axis=dim)
        before = lax.ppermute(last, axis, up)
        after = lax.ppermute(first, axis, down)
        x = jnp.concatenate([before, x, after], axis=dim)
    return x


def segment_ids(positions, bounds):
    return jnp.sum((positions[..., None] >= bounds).astype(jnp.int32), axis=-1)


def attend(queries, keys, values, allowed, head_count):
    group_count, query_len, all_width = queries.shape
    key_len = keys.shape[1]
    query_heads = queries.reshape(group_count, query_len, head_count, HEAD)
    key_heads = keys.reshape(group_count, key_len, head_count, HEAD)
    value_heads = values.reshape(group_count, key_len, head_count, HEAD)
    scores = jnp.einsum(
        "gqhe,gkhe->ghqk", query_heads, key_heads, preferred_element_type=jnp.float32
    ) * HEAD ** (-0.5)
    scores = jnp.where(allowed[:, None], scores, MASKED)
    maxima = jnp.max(scores, axis=-1, keepdims=True)
    weights = jnp.where(allowed[:, None], jnp.exp(scores - maxima), 0.0)
    totals = jnp.sum(weights, axis=-1)
    mixture = jnp.einsum(
        "ghqk,gkhe->gqhe",
        weights.astype(jnp.bfloat16),
        value_heads,
        preferred_element_type=jnp.float32,
    )
    mixture = mixture / jnp.transpose(totals, (0, 2, 1))[..., None]
    return mixture.reshape(group_count, query_len, all_width).astype(jnp.bfloat16)


def three_views(window_span, group_size, axis_pos):
    views = []
    for shift_index in range(3):
        piece = lax.slice_in_dim(
            window_span,
            shift_index * BLOCK,
            shift_index * BLOCK + group_size * BLOCK,
            axis=axis_pos,
        )
        new_shape = (
            window_span.shape[:axis_pos] + (group_size, BLOCK) + window_span.shape[axis_pos + 1 :]
        )
        views.append(piece.reshape(new_shape))
    return jnp.concatenate(views, axis=axis_pos + 1)


def shards(
    tokens, w_qkv, w_out, ln_gain, ln_bias, random_blocks, summary_pos, summary_blocks, pair_lengths
):
    tok_rows = tokens.shape[1]
    head_cols = tokens.shape[2]
    heads_here = head_cols // HEAD
    full_width = w_out.shape[1]
    ctx_count = lax.axis_size("ctx")
    ctx_index = lax.axis_index("ctx")
    block_count = tok_rows // BLOCK
    seq_total = tok_rows * ctx_count
    bounds = jnp.cumsum(pair_lengths[0])
    own_tokens = tokens[0]
    projected = jnp.einsum(
        "nc,kcd->knd",
        lax.all_gather(own_tokens, "heads", axis=1, tiled=True),
        w_qkv,
        preferred_element_type=jnp.float32,
    ).astype(jnp.bfloat16)
    queries = projected[0]
    own_kv = projected[1:3]
    rim_kv = extended(own_kv, (("ctx", 1),), BLOCK)
    query_pos = ctx_index * tok_rows + jnp.arange(tok_rows, dtype=jnp.int32)
    own_seg = segment_ids(query_pos, bounds)
    rim_pos = ctx_index * tok_rows - BLOCK + jnp.arange(tok_rows + 2 * BLOCK, dtype=jnp.int32)
    rim_ok = (rim_pos >= 0) & (rim_pos < seq_total)
    rim_seg = segment_ids(rim_pos, bounds)
    rand_count = random_blocks.shape[2]
    picked = random_blocks[0].reshape(-1)
    pick_count = picked.shape[0]
    capacity = max(2, -(-pick_count // ctx_count))
    owners = picked // block_count
    within = picked % block_count
    slot_order = jnp.arange(pick_count, dtype=jnp.int32)
    earlier = (owners[:, None] == owners[None, :]) & (slot_order[None, :] < slot_order[:, None])
    pick_rank = jnp.sum(earlier.astype(jnp.int32), axis=1)
    pick_slot = owners * capacity + pick_rank
    slot_table = (
        pick_slot[:, None] == jnp.arange(ctx_count * capacity, dtype=jnp.int32)[None, :]
    ).astype(jnp.int32)
    requests = jnp.sum(slot_table * within[:, None], axis=0).reshape(ctx_count, capacity)
    own_blocks = own_kv.reshape(2, block_count, BLOCK, head_cols).transpose(1, 0, 2, 3)
    reply = jnp.take(
        own_blocks, lax.all_to_all(requests, "ctx", split_axis=0, concat_axis=0, tiled=True), axis=0
    )
    fetched = lax.all_to_all(reply, "ctx", split_axis=0, concat_axis=0, tiled=True)
    flat_blocks = fetched.reshape(ctx_count * capacity, 2, BLOCK, head_cols)
    far_kv = jnp.take(flat_blocks, pick_slot, axis=0).reshape(
        block_count, rand_count, 2, BLOCK, head_cols
    )
    far_kv = far_kv.transpose(2, 0, 1, 3, 4).reshape(2, block_count, rand_count * BLOCK, head_cols)
    far_pos = (
        picked.reshape(block_count, rand_count)[:, :, None] * BLOCK
        + jnp.arange(BLOCK, dtype=jnp.int32)
    ).reshape(block_count, rand_count * BLOCK)
    far_seg = segment_ids(far_pos, bounds)
    group_size = min(4, block_count)
    group_steps = block_count // group_size

    def window_step(unused, step_index):
        near_kv = three_views(rim_kv, group_size, 1)
        near_ok = three_views(rim_ok, group_size, 0)
        near_seg = three_views(rim_seg, group_size, 0)
        key_set = jnp.concatenate([near_kv, far_kv], axis=2)
        key_seg = jnp.concatenate([near_seg, far_seg], axis=1)
        key_ok = jnp.concatenate([near_ok, jnp.ones(far_seg.shape, jnp.bool_)], axis=1)
        query_seg = own_seg.reshape(group_size, BLOCK)
        allowed = key_ok[:, None, :] & (key_seg[:, None, :] == query_seg[:, :, None])
        query_group = queries.reshape(group_size, BLOCK, head_cols)
        return (unused, attend(query_group, key_set[0], key_set[1], allowed, heads_here))

    _, window_out = lax.scan(window_step, 0, jnp.arange(group_steps, dtype=jnp.int32))
    attention = window_out.reshape(tok_rows, head_cols)
    summary_rows = summary_pos[0]
    summary_lists = summary_blocks[0]
    summaries = summary_rows.shape[0]
    per_device = summaries // ctx_count
    mine = (
        lax.dynamic_slice_in_dim(summary_rows, ctx_index * per_device, per_device, 0)
        - ctx_index * tok_rows
    )
    summary_query = jnp.take(queries, mine, axis=0)
    all_queries = lax.all_gather(summary_query, "ctx", axis=0, tiled=True)
    summary_seg = segment_ids(summary_rows, bounds)
    key_block = ctx_index * block_count + jnp.arange(block_count, dtype=jnp.int32)
    listed = jnp.any(summary_lists[:, :, None] == key_block[None, None, :], axis=1)
    key_heads = own_kv[0].reshape(tok_rows, heads_here, HEAD)
    value_heads = own_kv[1].reshape(tok_rows, heads_here, HEAD)
    summary_group = min(128, summaries)
    group_total = summaries // summary_group

    def group_scores():
        query_part = all_queries.reshape(summary_group, heads_here, HEAD)
        allowed = jnp.broadcast_to(listed[:, :, None], (summary_group, block_count, BLOCK)).reshape(
            summary_group, tok_rows
        )
        allowed = allowed & (own_seg[None, :] == summary_seg[:, None])
        scores = jnp.einsum(
            "qhe,khe->hqk", query_part, key_heads, preferred_element_type=jnp.float32
        ) * HEAD ** (-0.5)
        return (jnp.where(allowed[None], scores, MASKED), allowed)

    def weigh(scores, allowed, maxima):
        weights = jnp.where(allowed[None], jnp.exp(scores - maxima[:, :, None]), 0.0)
        totals = jnp.sum(weights, axis=-1)
        mixture = jnp.einsum(
            "hqk,khe->qhe",
            weights.astype(jnp.bfloat16),
            value_heads,
            preferred_element_type=jnp.float32,
        )
        return (totals.T, mixture.reshape(summary_group, head_cols))

    def max_step(unused, group_index):
        scores, allowed = group_scores()
        return (unused, jnp.max(scores, axis=-1).T)

    _, maxima_all = lax.scan(max_step, 0, jnp.arange(group_total, dtype=jnp.int32))
    maxima_all = lax.pmax(maxima_all.reshape(summaries, heads_here), "ctx")

    def sum_step(unused, group_index):
        scores, allowed = group_scores()
        maxima = maxima_all.T
        return (unused, weigh(scores, allowed, maxima))

    _, (totals_all, mixture_all) = lax.scan(sum_step, 0, jnp.arange(group_total, dtype=jnp.int32))
    totals_all = totals_all.reshape(summaries, heads_here)
    mixture_all = mixture_all.reshape(summaries, head_cols)
    totals_all, mixture_all = (
        lax.psum(totals_all.astype(jnp.bfloat16), "ctx").astype(jnp.float32),
        lax.psum(mixture_all.astype(jnp.bfloat16), "ctx").astype(jnp.float32),
    )
    own_totals = lax.dynamic_slice_in_dim(totals_all, ctx_index * per_device, per_device, 0)
    own_mixture = lax.dynamic_slice_in_dim(mixture_all, ctx_index * per_device, per_device, 0)
    summary_out = (own_mixture / jnp.repeat(own_totals, HEAD, axis=1)).astype(jnp.bfloat16)
    attention = attention.at[mine].set(summary_out)
    partial_value = jnp.dot(attention, w_out, preferred_element_type=jnp.float32)
    summed = lax.psum_scatter(
        partial_value.astype(jnp.bfloat16), "heads", scatter_dimension=1, tiled=True
    ).astype(jnp.float32)
    hidden = own_tokens.astype(jnp.float32) + summed
    row_sums = lax.psum((jnp.sum(hidden, axis=1), jnp.sum(hidden * hidden, axis=1)), "heads")
    row_mean = row_sums[0] / full_width
    row_var = row_sums[1] / full_width - row_mean * row_mean
    normed = (hidden - row_mean[:, None]) * lax.rsqrt(row_var + 1e-05)[:, None] * ln_gain + ln_bias
    return normed.astype(jnp.bfloat16)[None]


def fast_kernel(
    ctx_count, rand, tok_hbm, wq_hbm, wo_hbm, gain_ref, bias_ref, rb_ref, pair_ref, spos_ref,
    slist_ref, out_ref, wq, wo, tok, own, xin, bias, kv_out, kv_in, q_out, q_in, sq_out,
    sq_in, s_ok, s_res, meta_out, meta_in, meta_s, o_out, o_in, rs_out, rs_in, hidden, st_out,
    st_in, w_sem, tok_sem, far_send, own_recv, fwd_send, x_send, x_recv, meta_send, meta_recv, meta_sem, kv_send, kv_recv,
    q_send, q_recv, sq_send, sq_recv, o_send, o_recv, rs_sem, st_sem,
    go_sem,
):
    z = lax.axis_index("ctx")
    half = lax.axis_index("heads")
    core = lax.axis_index("dp")
    other = 1 - half
    rows, cols = tok_hbm.shape
    nblk = rows // BLOCK
    wide = kv_in.shape[3]
    group = wide // HEAD
    blocks = ctx_count * nblk
    seq = blocks * BLOCK
    pairs = pair_ref.shape[1]
    listed = slist_ref.shape[1]
    per = spos_ref.shape[1] // ctx_count
    srows = per * group
    side = z // 2
    place = lax.rem(z, 2)
    sib = z + 1 - 2 * place
    home = core == side
    guest = core != side
    gate = z == 1 + side
    mate = 2 * place + core
    away = 2 * (1 - side)
    f32, bf16, i32 = jnp.float32, jnp.bfloat16, jnp.int32
    mates = [(z, 1 - core), (sib, core), (sib, 1 - core)]

    def remote(src, dst, send, recv, to):
        return pltpu.make_async_remote_copy(
            src_ref=src, dst_ref=dst, send_sem=send, recv_sem=recv,
            device_id=to, device_id_type=pl.DeviceIdType.MESH,
        )

    def arrived(dst, sem):
        pltpu.make_async_copy(dst, dst, sem).wait()

    def at_mate(d):
        return {"ctx": mates[d][0], "dp": mates[d][1]}

    def mate_index(d):
        return 2 * lax.rem(mates[d][0], 2) + mates[d][1]

    def band(c):
        return pl.ds(pl.multiple_of(c * BLOCK, BLOCK), BLOCK)

    def lanes(i, size):
        return pl.ds(pl.multiple_of(i * size, size), size)

    def own_local(c):
        return pltpu.make_async_copy(
            tok_hbm.at[band(c)], own.at[0, band(c)], own_recv.at[0, c]
        )

    def far_copy(c):
        return remote(
            tok_hbm.at[band(c)], own.at[place, band(c)], far_send, own_recv.at[place, c],
            {"ctx": 2 - side, "dp": 1 - core},
        )

    def fwd_copy(r, c):
        return remote(
            own.at[r, band(c)], own.at[r, band(c)], fwd_send.at[r, c], own_recv.at[r, c],
            {"ctx": sib},
        )

    def x_copy(src, r, c):
        return remote(
            src, xin.at[r, band(c)], x_send.at[r], x_recv.at[r, c], {"heads": other}
        )

    def meta_copy(m):
        return remote(
            meta_out, meta_in.at[z], meta_send.at[m], meta_recv.at[z],
            {"ctx": 2 * core + m // 2, "dp": m % 2},
        )

    def kv_copy(m, d, slot, r, c):
        return remote(
            kv_out.at[slot, c], kv_in.at[r * nblk + c], kv_send.at[d], kv_recv.at[r],
            at_mate(m),
        )

    def q_copy(m, d, slot, r, c):
        return remote(
            q_out.at[slot, c], q_in.at[r * nblk + c], q_send.at[d], q_recv.at[r, c],
            at_mate(m),
        )

    def sq_copy(m, d, slot, r):
        return remote(
            sq_out.at[slot], sq_in.at[r], sq_send.at[d], sq_recv.at[r],
            at_mate(m),
        )

    def home_copy(copy, d, *c):
        return copy(d, d, mate_index(d), z, *c)

    def guest_copy(copy, r, *c):
        return copy(0, 3 * r, 2 * (1 - core) + r, away + r, *c)

    def local(out, into, sem):
        pltpu.make_async_copy(out, into, sem).start()

    def owner(i):
        return away + i if i < 2 else 2 * side + i - 2

    def o_copy(i, r, c):
        return remote(
            o_out.at[r * nblk + c], o_in.at[c, :, lanes(mate, wide)], o_send.at[i],
            o_recv.at[c], {"ctx": r, "dp": side},
        )

    def o_local(r, c):
        return pltpu.make_async_copy(
            o_out.at[r * nblk + c], o_in.at[c, :, lanes(mate, wide)], o_recv.at[c]
        )

    def rs_copy(c):
        return remote(rs_out.at[c], rs_in.at[c], rs_sem.at[nblk], rs_sem.at[c], {"heads": other})

    def st_copy(c):
        return remote(st_out.at[c], st_in.at[c], st_sem.at[nblk], st_sem.at[c], {"heads": other})

    tok_copy = pltpu.make_async_copy(tok_hbm, tok, tok_sem)
    two = 2 * wide

    def w_copy(k, part):
        if part:
            return pltpu.make_async_copy(
                wq_hbm.at[k, :, lanes(place, two)], wq.at[k, :, pl.ds(0, two)], w_sem.at[k]
            )
        return pltpu.make_async_copy(wq_hbm.at[k], wq.at[k], w_sem.at[k])

    wo_copy = pltpu.make_async_copy(wo_hbm, wo, w_sem.at[3])
    barrier = pltpu.get_barrier_semaphore()
    greeted = [{"heads": other}, {"dp": 1 - core}]
    for d in range(1, ctx_count):
        for other_core in range(2):
            greeted.append({"ctx": lax.rem(z + d, ctx_count), "dp": other_core})
    for to in greeted:
        pl.semaphore_signal(barrier, inc=1, device_id=to, device_id_type=pl.DeviceIdType.MESH)

    @pl.when(home)
    def _():
        for c in range(nblk):
            own_local(c).start()
        for k in (1, 2, 0):
            w_copy(k, False).start()

    @pl.when(guest)
    def _():
        for k in (1, 2, 0):
            w_copy(k, True).start()

    tok_copy.start()
    wo_copy.start()
    meta_out[...] = jnp.zeros_like(meta_out)
    for r in range(rand):
        meta_out[r : r + 1, :nblk] = rb_ref[r]
    meta_out[rand : rand + 1, : ctx_count * per] = spos_ref[...]
    meta_out[rand + 1 : rand + 2, :pairs] = pair_ref[...]
    meta_out[8 : 8 + listed, : ctx_count * per] = slist_ref[0]
    pl.semaphore_wait(barrier, len(greeted))

    for m in range(4):
        itself = home & (mate == m)

        @pl.when(itself)
        def _():
            pltpu.make_async_copy(meta_out, meta_in.at[z], meta_recv.at[z]).start()

        @pl.when(jnp.logical_not(itself))
        def _():
            meta_copy(m).start()

    @pl.when(home)
    def _():
        for c in range(nblk):
            x_copy(tok_hbm.at[band(c)], 0, c).start()

    @pl.when(guest)
    def _():
        for c in range(nblk):
            far_copy(c).start()

    def relay(r, c):
        arrived(own.at[r, band(c)], own_recv.at[r, c])

        @pl.when(gate)
        def _():
            fwd_copy(r, c).start()

        x_copy(own.at[r, band(c)], r, c).start()

    def product(k, r, c, width):
        val = jnp.dot(
            own[r, band(c), :], wq[k, lanes(half, cols), :width], preferred_element_type=f32
        )
        val = val + jnp.dot(
            xin[r, band(c), :], wq[k, lanes(other, cols), :width], preferred_element_type=f32
        )
        return val.astype(bf16)

    def project_home(c):
        arrived(own.at[0, band(c)], own_recv.at[0, c])
        arrived(xin.at[0, band(c)], x_recv.at[0, c])
        for k in (1, 2):
            val = product(k, 0, c, cols)
            for m in range(4):
                kv_out[m, c, k - 1] = val[:, m * wide : (m + 1) * wide]
        home_copy(kv_copy, 0, c).start()

        @pl.when(jnp.logical_not(gate))
        def _():
            for d in (1, 2):
                home_copy(kv_copy, d, c).start()

        local(kv_out.at[mate, c], kv_in.at[z * nblk + c], kv_recv.at[z])
        val = product(0, 0, c, cols)
        for m in range(4):
            q_out[m, c] = val[:, m * wide : (m + 1) * wide]
        home_copy(q_copy, 0, c).start()
        local(q_out.at[mate, c], q_in.at[z * nblk + c], q_recv.at[z, c])

    def project_guest(r, c):
        b = (away + r) * nblk + c
        arrived(xin.at[r, band(c)], x_recv.at[r, c])
        for k in (1, 2):
            val = product(k, r, c, two)
            for m in range(2):
                kv_out[2 * m + r, c, k - 1] = val[:, m * wide : (m + 1) * wide]
        guest_copy(kv_copy, r, c).start()
        local(kv_out.at[2 * core + r, c], kv_in.at[b], kv_recv.at[away + r])
        val = product(0, r, c, two)
        for m in range(2):
            q_out[2 * m + r, c] = val[:, m * wide : (m + 1) * wide]
        guest_copy(q_copy, r, c).start()
        local(q_out.at[2 * core + r, c], q_in.at[b], q_recv.at[away + r, c])

    def w_wait(part):
        for k in (1, 2, 0):
            w_copy(k, part).wait()

    order = [(1 - side, c) for c in range(nblk)] + [(side, c) for c in range(nblk)]
    ahead = 5

    @pl.when(guest)
    def _():
        for r, c in order[:ahead]:
            relay(r, c)

    for r in range(ctx_count):
        arrived(meta_in.at[r], meta_recv.at[r])
    meta_local = pltpu.make_async_copy(meta_in, meta_s, meta_sem)
    meta_local.start()
    meta_local.wait()

    bounds = []
    total = 0
    for p in range(pairs):
        total = total + meta_s[0, rand + 1, p]
        bounds.append(total)

    def segments(pos):
        seg = jnp.zeros(pos.shape, i32)
        for bound in bounds:
            seg = seg + jnp.where(pos >= bound, 1, 0)
        return seg

    def spos(i):
        return meta_s[0, rand, i]

    row_1 = lax.broadcasted_iota(i32, (BLOCK, 1), 0)
    lane_1 = lax.broadcasted_iota(i32, (1, BLOCK), 1)

    def mask_block(b, carry):
        r, c = b // nblk, lax.rem(b, nblk)
        seg_q = segments(b * BLOCK + row_1)
        for j in range(3 + rand):
            if j < 3:
                pos = (b + j - 1) * BLOCK + lane_1
                seg = jnp.where((pos >= 0) & (pos < seq), segments(pos), -1)
            else:
                seg = segments(meta_s[r, j - 3, c] * BLOCK + lane_1)
            bias[b, :, j * BLOCK : (j + 1) * BLOCK] = jnp.where(seg_q == seg, 0.0, MASKED)
        return carry

    def masks():
        lax.fori_loop(0, blocks, mask_block, 0)
        key_pos = lax.broadcasted_iota(i32, (1, seq), 1)
        row_all = lax.broadcasted_iota(i32, (ctx_count * srows, 1), 0)
        bits = jnp.zeros((ctx_count * srows, 1), i32)
        places = jnp.zeros((ctx_count * srows, 1), i32)
        for u in range(ctx_count * per):
            word = 0
            for j in range(listed):
                word = word | (1 << meta_s[0, 8 + j, u])
            for g in range(group):
                here = row_all == u // per * srows + g * per + u % per
                bits = jnp.where(here, word, bits)
                places = jnp.where(here, spos(u), places)
        hit = lax.shift_right_logical(
            jnp.broadcast_to(bits, s_ok.shape), jnp.broadcast_to(key_pos // BLOCK, s_ok.shape)
        )
        s_ok[...] = jnp.where(segments(places) == segments(key_pos), hit & 1, 0)

    masks()

    @pl.when(home)
    def _():
        w_wait(False)
        for c in range(nblk):
            project_home(c)

    @pl.when(guest)
    def _():
        w_wait(True)
        for i in range(len(order)):
            project_guest(*order[i])
            if i + ahead < len(order):
                relay(*order[i + ahead])
            if i + ahead == len(order):
                @pl.when(gate)
                def _():
                    for r, c in order[:-1]:
                        fwd_copy(r, c).wait_send()
                    pl.semaphore_signal(
                        go_sem, inc=1, device_id={"dp": 1 - core},
                        device_id_type=pl.DeviceIdType.MESH,
                    )

    row8 = lax.broadcasted_iota(i32, (srows, BLOCK), 0)
    col8 = lax.broadcasted_iota(i32, (srows, BLOCK), 1)

    def pick_rows(slot, r):
        wanted = jnp.zeros((srows, BLOCK), i32)
        for i in range(srows):
            wanted = jnp.where(row8 == i, spos(r * per + i % per), wanted)
        found = jnp.zeros((srows, wide), f32)
        for c in range(nblk):
            pick = (wanted == (r * nblk + c) * BLOCK + col8).astype(f32).astype(bf16)
            found = found + jnp.dot(pick, q_out[slot, c], preferred_element_type=f32)
        sq_out[slot] = found

    @pl.when(home)
    def _():
        for m in range(4):
            pick_rows(m, z)
        for d in (1, 2, 0):
            home_copy(sq_copy, d).start()
        local(sq_out.at[mate], sq_in.at[z], sq_recv.at[z])

    @pl.when(guest)
    def _():
        for r in range(2):
            for m in range(2):
                pick_rows(2 * m + r, away + r)
            guest_copy(sq_copy, r).start()
            local(sq_out.at[2 * core + r], sq_in.at[away + r], sq_recv.at[away + r])

    def range_wait(r):
        arrived(kv_in.at[pl.ds(r * nblk, nblk)], kv_recv.at[r])

    def to_sibling(copy):
        for c in range(nblk):
            for d in (1, 2):
                home_copy(copy, d, c).start()

    @pl.when(home)
    def _():
        @pl.when(gate)
        def _():
            pl.semaphore_wait(go_sem, 1)
            to_sibling(kv_copy)

        to_sibling(q_copy)

    range_wait(away + 1 - side)
    range_wait(z)
    range_wait(away + side)
    range_wait(sib)
    for r in range(ctx_count):
        arrived(sq_in.at[r], sq_recv.at[r])

    factor = HEAD ** (-0.5)
    nt = (((1,), (1,)), ((), ()))

    def softmax(scores, ok):
        scores = jnp.where(ok, scores * factor, MASKED)
        top = jnp.max(scores, axis=1, keepdims=True)
        weights = jnp.exp(scores - top)
        return weights, jnp.sum(weights, axis=1, keepdims=True)

    lane_head = lax.broadcasted_iota(i32, (ctx_count * srows, wide), 1) // HEAD
    row_head = lax.rem(lax.broadcasted_iota(i32, (ctx_count * srows, wide), 0), srows) // per
    sq = sq_in[...].reshape(ctx_count * srows, wide)
    sq = jnp.where(lane_head == row_head, sq, 0.0).astype(bf16)
    all_k = kv_in[:, 0].reshape(seq, wide)
    scores = lax.dot_general(sq, all_k, nt, preferred_element_type=f32)
    weights, totals = softmax(scores, s_ok[...] > 0)
    all_v = kv_in[:, 1].reshape(seq, wide)
    mixed = jnp.dot(weights.astype(bf16), all_v, preferred_element_type=f32) / totals
    s_res[...] = mixed.reshape(ctx_count, srows, wide)

    lane_q = lax.broadcasted_iota(i32, (BLOCK, wide), 1) // HEAD
    row_q = lax.broadcasted_iota(i32, (BLOCK, wide), 0)
    ones = jnp.ones(((3 + rand) * BLOCK, wide), bf16)

    def attend_block(r, c):
        b = r * nblk + c
        q = q_in[b]
        keys, values = [], []
        for shift in (-1, 0, 1):
            at = jnp.clip(b + shift, 0, blocks - 1)
            keys.append(kv_in[at, 0])
            values.append(kv_in[at, 1])
        for j in range(rand):
            at = meta_s[r, j, c]
            keys.append(kv_in[at, 0])
            values.append(kv_in[at, 1])
        keys = jnp.concatenate(keys, axis=0)
        values = jnp.concatenate([jnp.concatenate(values, axis=0), ones], axis=1)
        out = jnp.zeros((BLOCK, wide), f32)
        for g in range(group):
            qg = jnp.where(lane_q == g, q, jnp.zeros_like(q))
            scores = lax.dot_general(qg, keys, nt, preferred_element_type=f32) + bias[b]
            top = jnp.max(scores, axis=1, keepdims=True)
            weights = jnp.exp2((scores - top) * (factor * LOG2E))
            mix = jnp.dot(weights.astype(bf16), values, preferred_element_type=f32)
            out = jnp.where(lane_q == g, mix[:, :wide] / mix[:, wide:], out)
        res = s_res[r]
        for u in range(per):
            row = res[u : u + 1, :]
            for g in range(1, group):
                row = jnp.where(
                    lane_q[:1] == g, res[g * per + u : g * per + u + 1, :], row
                )
            out = jnp.where(row_q == spos(r * per + u) - b * BLOCK, row, out)
        o_out[b] = out.astype(bf16)

    def attend_step(far, c):
        base = 2 * (side + far - 2 * side * far)
        for i in range(2):
            arrived(q_in.at[(base + i) * nblk + c], q_recv.at[base + i, c])

        def step(i, carry):
            attend_block(base + i, c)
            return carry

        lax.fori_loop(0, 2, step, 0, unroll=2)
        for i in range(2):
            itself = home & (base + i == z)

            @pl.when(itself)
            def _():
                o_local(base + i, c).start()

            @pl.when(jnp.logical_not(itself))
            def _():
                o_copy(2 - 2 * far + i, base + i, c).start()

    def output(c):
        arrived(o_in.at[c], o_recv.at[c])
        att = o_in[c]
        rs_out[c] = jnp.dot(att, wo[:, lanes(other, cols)], preferred_element_type=f32).astype(bf16)
        rs_copy(c).start()
        term = jnp.dot(att, wo[:, lanes(half, cols)], preferred_element_type=f32).astype(bf16)
        hidden[band(c), :] = term.astype(f32)

    lane_s = lax.broadcasted_iota(i32, (BLOCK, BLOCK), 1)

    def finish(c):
        arrived(rs_in.at[c], rs_sem.at[c])
        hid = tok[band(c), :].astype(f32) + (hidden[band(c), :] + rs_in[c].astype(f32))
        hidden[band(c), :] = hid
        first = jnp.sum(hid, axis=1, keepdims=True)
        second = jnp.sum(hid * hid, axis=1, keepdims=True)
        both = jnp.where(lane_s == 0, first, jnp.where(lane_s == 1, second, 0.0))
        st_out[c] = jnp.transpose(both)[:8]
        st_copy(c).start()

    full = 2 * cols

    def norm(c):
        arrived(st_in.at[c], st_sem.at[c])
        sums = jnp.transpose(st_out[c] + st_in[c])
        mean = sums[:, 0:1] / full
        var = sums[:, 1:2] / full - mean * mean
        hid = hidden[band(c), :]
        res = (hid - mean) * lax.rsqrt(var + 1e-05) * gain_ref[...] + bias_ref[...]
        out_ref[band(c), :] = res.astype(bf16)

    wo_copy.wait()
    tok_copy.wait()

    def only(cond, *steps):
        @pl.when(cond)
        def _():
            for do, c in steps:
                do(c)

    rim = jnp.logical_not(gate)
    rim_order = [(1, 0)]
    gate_order = [(0, 0)]
    for c in range(1, nblk):
        rim_order += [(1, c), (0, c - 1)]
        gate_order += [(0, c), (1, c - 1)]
    rim_order.append((0, nblk - 1))
    gate_order.append((1, nblk - 1))
    inner = place + side - 2 * place * side
    done_home = 0
    for i in range(2 * nblk):
        (f0, c0), (f1, c1) = rim_order[i], gate_order[i]
        attend_step(f0 + inner * (f1 - f0), c0 + inner * (c1 - c0))
        if i >= 3 and i % 2 == 1 and i < 2 * nblk - 1:
            only(home & rim, (output, done_home))
            done_home += 1
        if i == 2 * nblk - 3:
            only(guest & rim, (output, 0))

    def rest(first, lead):
        steps = [(output, c) for c in range(first, min(nblk, first + lead))]
        for c in range(nblk):
            steps.append((finish, c))
            if first + lead + c < nblk:
                steps.append((output, first + lead + c))
        return steps + [(norm, c) for c in range(nblk)]

    only(home & rim, *rest(done_home, nblk))
    only(guest & rim, *rest(1, 1))
    only(home & gate, *rest(0, nblk))
    only(guest & gate, *rest(0, 2))

    for m in range(4):
        @pl.when(jnp.logical_not(home & (mate == m)))
        def _():
            meta_copy(m).wait_send()

    @pl.when(home)
    def _():
        arrived(own.at[0], x_send.at[0])
        for d in range(3):
            arrived(kv_out.at[d], kv_send.at[d])
            arrived(q_out.at[d], q_send.at[d])
            home_copy(sq_copy, d).wait_send()

    @pl.when(guest)
    def _():
        arrived(tok, far_send)
        for r in range(2):
            arrived(own.at[r], x_send.at[r])
            arrived(kv_out.at[r], kv_send.at[3 * r])
            arrived(q_out.at[r], q_send.at[3 * r])
            guest_copy(sq_copy, r).wait_send()

        @pl.when(gate)
        def _():
            for r, c in order[-1:]:
                fwd_copy(r, c).wait_send()

    arrived(rs_out, rs_sem.at[nblk])
    arrived(st_out, st_sem.at[nblk])
    for i in range(4):
        if i < 2:
            arrived(o_out.at[pl.ds(0, nblk)], o_send.at[i])
        else:
            @pl.when(jnp.logical_not(home & (owner(i) == z)))
            def _():
                arrived(o_out.at[pl.ds(0, nblk)], o_send.at[i])


def store_kernel(src_ref, out_hbm, sem):
    copy = pltpu.make_async_copy(src_ref, out_hbm, sem)
    copy.start()
    copy.wait()


def fast_shards(
    tokens, w_qkv, w_out, ln_gain, ln_bias, random_blocks, summary_pos, summary_blocks, pair_lengths
):
    ctx_count = lax.axis_size("ctx")
    rows, cols = tokens.shape[1:]
    nblk = rows // BLOCK
    wide = cols // ctx_count
    group = wide // HEAD
    blocks = nblk * ctx_count
    summaries = summary_pos.shape[1]
    per = summaries // ctx_count
    srows = per * group
    rand = random_blocks.shape[2]
    vmem = pl.BlockSpec(memory_space=pltpu.VMEM)
    hbm = pl.BlockSpec(memory_space=pl.ANY)
    bf16, f32, i32 = jnp.bfloat16, jnp.float32, jnp.int32
    dma = pltpu.SemaphoreType.DMA
    out = pl.pallas_call(
        functools.partial(fast_kernel, ctx_count, rand),
        out_shape=pltpu.VMEM((rows, cols), bf16),
        in_specs=[hbm, hbm, hbm, vmem, vmem, vmem, vmem, vmem, vmem],
        out_specs=vmem,
        scratch_shapes=[
            pltpu.VMEM((3, 2 * cols, cols), bf16),
            pltpu.VMEM(w_out.shape, bf16),
            pltpu.VMEM((rows, cols), bf16),
            pltpu.VMEM((2, rows, cols), bf16),
            pltpu.VMEM((2, rows, cols), bf16),
            pltpu.VMEM((blocks, BLOCK, (3 + rand) * BLOCK), f32),
            pltpu.VMEM((4, nblk, 2, BLOCK, wide), bf16),
            pltpu.VMEM((blocks, 2, BLOCK, wide), bf16),
            pltpu.VMEM((4, nblk, BLOCK, wide), bf16),
            pltpu.VMEM((blocks, BLOCK, wide), bf16),
            pltpu.VMEM((4, srows, wide), f32),
            pltpu.VMEM((ctx_count, srows, wide), f32),
            pltpu.VMEM((ctx_count * srows, blocks * BLOCK), i32),
            pltpu.VMEM((ctx_count, srows, wide), f32),
            pltpu.VMEM((16, 128), i32),
            pltpu.VMEM((ctx_count, 16, 128), i32),
            pltpu.SMEM((ctx_count, 16, 128), i32),
            pltpu.VMEM((blocks, BLOCK, wide), bf16),
            pltpu.VMEM((nblk, BLOCK, cols), bf16),
            pltpu.VMEM((nblk, BLOCK, cols), bf16),
            pltpu.VMEM((nblk, BLOCK, cols), bf16),
            pltpu.VMEM((rows, cols), f32),
            pltpu.VMEM((nblk, 8, BLOCK), f32),
            pltpu.VMEM((nblk, 8, BLOCK), f32),
            dma((4,)),
            dma,
            dma,
            dma((2, nblk)),
            dma((2, nblk)),
            dma((2,)),
            dma((2, nblk)),
            dma((4,)),
            dma((ctx_count,)),
            dma,
            dma((4,)),
            dma((ctx_count,)),
            dma((4,)),
            dma((ctx_count, nblk)),
            dma((4,)),
            dma((ctx_count,)),
            dma((4,)),
            dma((nblk,)),
            dma((nblk + 1,)),
            dma((nblk + 1,)),
            pltpu.SemaphoreType.REGULAR,
        ],
        compiler_params=pltpu.CompilerParams(
            collective_id=0, has_side_effects=True, vmem_limit_bytes=60000 * 1024
        ),
    )(
        tokens[0], w_qkv, w_out, ln_gain[None], ln_bias[None],
        random_blocks.transpose(2, 0, 1), pair_lengths, summary_pos,
        summary_blocks.transpose(0, 2, 1),
    )
    out = pl.pallas_call(
        store_kernel,
        out_shape=jax.ShapeDtypeStruct((rows, cols), bf16),
        in_specs=[vmem],
        out_specs=hbm,
        scratch_shapes=[dma],
    )(pltpu.with_memory_space_constraint(out, pltpu.VMEM))
    return out[None]


def solution(mesh):
    in_specs = (
        P(("groups", "dp"), "ctx", "heads"),
        P(None, None, "heads"),
        P("heads", None),
        P("heads"),
        P("heads"),
        P(("groups", "dp"), "ctx", None),
        P(("groups", "dp"), None),
        P(("groups", "dp"), None, None),
        P(("groups", "dp"), None),
    )
    out_specs = P(("groups", "dp"), "ctx", "heads")
    ctx_count = mesh.shape["ctx"]

    def body(*args):
        rows, cols = args[0].shape[1:]
        wide = cols // ctx_count
        by_heads = (
            ctx_count == 4
            and mesh.shape["heads"] == 2
            and mesh.shape["dp"] == 2
            and wide > 0
            and wide % 128 == 0
            and wide * ctx_count == cols
            and rows // BLOCK <= 128
            and rows // BLOCK * ctx_count <= 32
            and args[6].shape[1] // ctx_count * (wide // HEAD) % 8 == 0
            and rows // BLOCK >= 2
            and args[5].shape[2] <= 6
            and args[7].shape[2] <= 8
            and max(rows // BLOCK, args[6].shape[1], args[8].shape[1]) <= 128
        )
        return (fast_shards if by_heads else shards)(*args)

    return jax.shard_map(body, mesh=mesh, in_specs=in_specs, out_specs=out_specs, check_vma=False)
```
